32 devices in a mesh: gx: 2 (over x), gy: 16 (over z, y, core).
Axes of the slice: x: 2, y: 2, z: 4, core: 2. Of those that a mesh axis runs over, the one named last changes fastest.
Arguments:
- features: bfloat16 [4, 128, 16, 8, 256], P('gx', 'gy'), may hold values from -6 to 6
- fractions: bfloat16 [4, 128, 16, 8, 3], P('gx', 'gy'), may hold values from 0 to 1
- counts: int32 [4, 128, 16], P('gx', 'gy'), may hold values from 2 to 8
- k_index: int32 [1024, 3], replicated, may hold values from -112 to 112, as said below
- w_short: bfloat16 [8, 256, 256], replicated, may hold values from -0.375 to 0.375
- w_charge: bfloat16 [256, 256], replicated, may hold values from -0.375 to 0.375
- w_out: bfloat16 [256, 256], replicated, may hold values from -0.75 to 0.75
Outputs:
- updated: bfloat16 [4, 128, 16, 8, 256], P('gx', 'gy')
The draws below stay inside these ranges and needn't reach their ends.
Inputs may be any that keep to these rules, and one draw needn't show every extreme that they name: No two rows of k_index are equal, and no row is all zeros.
All inputs are finite; a program needn't handle non-finite values.
Results may differ from the reference program's by a relative error of at most 0.007.
Values may be sent and summed in bfloat16 or wider, within the bound.
No kernel may reach another device: no remote copies, remote signals or barrier semaphores. Data moves between devices by JAX's collectives and lax.ppermute only.
A program may use at most 128 MiB of HBM per device.

```python
import math
import jax
import jax.numpy as jnp
from jax import lax

F = 256
NB = 8
SLOTS = 8
K = 1024
NX = 4
NY = 128
NZ = 16
SITES = 65536


def draw_k_index(key, part):
    bound_x = NX * 7 // 8
    bound_y = NY * 7 // 8
    bound_z = NZ * 7 // 8
    span_x = 2 * bound_x + 1
    span_y = 2 * bound_y + 1
    span_z = 2 * bound_z + 1
    box_count = span_x * span_y * span_z
    order_key = jax.random.fold_in(key, 11)
    place_key = jax.random.fold_in(key, 23)
    flat_index = jax.random.permutation(order_key, box_count).astype(jnp.int32)
    comp_x = flat_index // (span_y * span_z) - bound_x
    comp_y = flat_index // span_z % span_y - bound_y
    comp_z = flat_index % span_z - bound_z
    quant_x = jnp.abs(comp_x) * 32 // NX
    quant_y = jnp.abs(comp_y) * 32 // NY
    quant_z = jnp.abs(comp_z) * 32 // NZ
    radius_sq = quant_x * quant_x + quant_y * quant_y + quant_z * quant_z
    inside = (radius_sq >= 361) & (radius_sq <= 841)
    largest = max(NX, NY, NZ)
    long_dim = [NX, NY, NZ].index(largest)
    peak_value = largest * 7 // 8
    components = [comp_x, comp_y, comp_z]
    others_zero = jnp.ones_like(inside)
    for which in range(3):
        if which != long_dim:
            others_zero = others_zero & (components[which] == 0)
    on_peak = others_zero & (jnp.abs(components[long_dim]) == peak_value)
    usable = inside & jnp.logical_not(on_peak)
    positions = jnp.arange(box_count, dtype=jnp.int32)
    rank_score = jnp.where(usable, positions, box_count + positions)
    chosen = jnp.argsort(rank_score)[:K - 2]
    selected = jnp.stack([comp_x[chosen], comp_y[chosen], comp_z[chosen]], axis=1)
    forced = jnp.zeros((2, 3), jnp.int32)
    forced = forced.at[0, long_dim].set(peak_value).at[1, long_dim].set(-peak_value)
    rows_all = jnp.concatenate([forced, selected.astype(jnp.int32)], axis=0)
    placing = jax.random.permutation(place_key, K)
    return rows_all[placing].astype(jnp.int32)


def set_ends(values, key, smallest, high):
    longest = values.shape.index(max(values.shape))
    spots = []
    for shift in (0, 1):
        where = [jax.random.randint(jax.random.fold_in(key, axis), (), 0, length) for axis, length in enumerate(values.shape)]
        where[longest] = (where[longest] + shift) % values.shape[longest]
        spots.append(tuple(where))
    return values.at[spots[0]].set(smallest).at[spots[1]].set(high)


def shard_levels(own_key, dims, split, least, high):
    factor_of = 1.0
    for dim, shards_of in split:
        draws = jax.random.uniform(jax.random.fold_in(jax.random.fold_in(own_key, 6), dim), (shards_of,), jnp.float32, least / len(split), high / len(split))
        factor_of = factor_of * jnp.repeat(jnp.exp(draws), dims[dim] // shards_of).reshape((-1,) + (1,) * (len(dims) - 1 - dim))
    return factor_of


def gaussian(key, extent, width, limit, pieces=(), held_as=jnp.bfloat16):
    values = jax.random.normal(key, extent, jnp.float32) * width
    if len(pieces) > 0:
        values = shard_levels(key, extent, pieces, -0.22, 0.18) * values
    return jnp.clip(values, min=-limit, max=limit).astype(held_as)


def setup_inputs(seed: int = 0) -> dict:
    seeds = jax.random.split(jax.random.key(seed), 8)
    return {
        "features": gaussian(seeds[0], (NX, NY, NZ, SLOTS, F), 1.0, 6.0, ((0, 2), (1, 16))),
        "fractions": jnp.clip(1.0 * jax.random.uniform(seeds[1], (NX, NY, NZ, SLOTS, 3), jnp.float32) ** shard_levels(seeds[1], (NX, NY, NZ, SLOTS, 3), ((0, 2), (1, 16)), -0.2, 0.2), 0.0, 1.0).astype(jnp.bfloat16),
        "counts": set_ends(jax.random.randint(seeds[2], (NX, NY, NZ), 2, SLOTS + 1), jax.random.fold_in(seeds[2], 1), 2, SLOTS).astype(jnp.int32),
        "k_index": draw_k_index(jax.random.fold_in(seeds[7], 71), 0),
        "w_short": gaussian(seeds[4], (NB, F, F), F ** -0.5, 0.375),
        "w_charge": gaussian(seeds[5], (F, F), F ** -0.5, 0.375),
        "w_out": gaussian(seeds[6], (F, F), (F // 4) ** -0.5, 0.75),
    }


TWO_PI = 2.0 * math.pi
CUTOFF = 1.0
SHARPNESS = 600.0
CENTER_LOW = 0.2
CENTER_SPAN = 0.5
SCREEN = 16.0

def stencil():
    return [(step_x, step_y, step_z) for step_x in (-1, 0, 1) for step_y in (-1, 0, 1) for step_z in (-1, 0, 1)]

def neighbours(block_feat, block_frac, rows_y, rows_z, slot_count):
    feat_parts = []
    frac_parts = []
    shift_parts = []
    for step_x, step_y, step_z in stencil():
        feat_parts.append(block_feat[1 + step_x, 1 + step_y:1 + step_y + rows_y, 1 + step_z:1 + step_z + rows_z])
        frac_parts.append(block_frac[1 + step_x, 1 + step_y:1 + step_y + rows_y, 1 + step_z:1 + step_z + rows_z])
        shift_parts.append([float(step_x), float(step_y), float(step_z)])
    cells = rows_y * rows_z
    feat_width = block_feat.shape[-1]
    near_feat = jnp.stack(feat_parts, axis=2).reshape(cells, 27 * slot_count, feat_width)
    near_frac = jnp.stack(frac_parts, axis=2).reshape(cells, 27 * slot_count, 3)
    shifts = jnp.repeat(jnp.array(shift_parts, jnp.float32), slot_count, axis=0)
    return (near_feat, near_frac, shifts)

def radial_weights(own_frac, near_frac, shifts, slot_count, basis):
    cells = near_frac.shape[0]
    own_rows = own_frac.reshape(cells, slot_count, 3)
    displace = near_frac[:, None, :, :] + shifts[None, None, :, :] - own_rows[:, :, None, :]
    dist_sq = lax.optimization_barrier(jnp.sum(displace * displace, axis=-1))
    radius = jnp.sqrt(dist_sq)
    envelope = jnp.square(jnp.maximum(1.0 - dist_sq / (CUTOFF * CUTOFF), 0.0))
    pairs = 27 * slot_count
    self_pair = jnp.arange(pairs)[None, :] == (13 * slot_count + jnp.arange(slot_count))[:, None]
    envelope = jnp.where(self_pair[None, :, :], 0.0, envelope)
    centers = CENTER_LOW + jnp.arange(basis).astype(jnp.float32) * (CENTER_SPAN / (basis - 1))
    weights = jnp.exp(-SHARPNESS * jnp.square(radius[:, :, None, :] - centers[None, None, :, None]))
    weights = weights * envelope[:, :, None, :]
    return weights.astype(jnp.bfloat16).reshape(cells, slot_count * basis, pairs)

def k_weights(k_index, grid):
    scaled = k_index.astype(jnp.float32) / jnp.array(grid, jnp.float32)
    wave = TWO_PI * scaled
    k_sq = lax.optimization_barrier(jnp.sum(wave * wave, axis=1))
    screened = jnp.exp(-k_sq / (4.0 * SCREEN)) / k_sq
    return (scaled, screened / jnp.sum(screened))

def phases(scaled, absolute):
    angles = scaled[:, 0:1] * absolute[None, :, 0] + scaled[:, 1:2] * absolute[None, :, 1]
    angles = TWO_PI * (angles + scaled[:, 2:3] * absolute[None, :, 2])
    return (jnp.cos(angles).astype(jnp.bfloat16), jnp.sin(angles).astype(jnp.bfloat16))

def reference(features, fractions, counts, k_index, w_short, w_charge, w_out):
    occupied = jnp.arange(SLOTS, dtype=jnp.int32)[None, None, None, :] < counts[..., None]
    sources = jnp.where(occupied[..., None], features, jnp.zeros_like(features))
    frac32 = fractions.astype(jnp.float32)
    widths = ((1, 1), (1, 1), (1, 1), (0, 0), (0, 0))
    pad_feat = jnp.pad(sources, widths, mode='wrap')
    pad_frac = jnp.pad(frac32, widths, mode='wrap')
    w_flat = w_short.reshape(NB * F, F)
    planes = jnp.arange(NX, dtype=jnp.int32)

    def plane_short(plane_index):
        block_feat = lax.dynamic_slice_in_dim(pad_feat, plane_index, 3, 0)
        block_frac = lax.dynamic_slice_in_dim(pad_frac, plane_index, 3, 0)
        near_feat, near_frac, shifts = neighbours(block_feat, block_frac, NY, NZ, SLOTS)
        own_frac = lax.dynamic_index_in_dim(frac32, plane_index, 0, keepdims=False)
        weights = radial_weights(own_frac, near_frac, shifts, SLOTS, NB)
        aggregate = jnp.einsum('cij,cjf->cif', weights.astype(jnp.float32), near_feat.astype(jnp.float32), precision=lax.Precision.HIGHEST)
        aggregate = aggregate.astype(jnp.bfloat16).reshape(-1, NB * F)
        return jnp.dot(aggregate, w_flat, preferred_element_type=jnp.float32)
    short = lax.map(plane_short, planes).reshape(NX, NY, NZ, SLOTS, F)
    charges = jnp.dot(features.reshape(-1, F), w_charge, preferred_element_type=jnp.float32)
    charges = jnp.where(occupied.reshape(-1, 1), charges, 0.0).astype(jnp.bfloat16).reshape(NX, NY * NZ * SLOTS, F)
    scaled, kweight = k_weights(k_index, (NX, NY, NZ))
    grid_y = jnp.arange(NY).astype(jnp.float32)[:, None, None]
    grid_z = jnp.arange(NZ).astype(jnp.float32)[None, :, None]

    def plane_positions(plane_index):
        own_frac = lax.dynamic_index_in_dim(frac32, plane_index, 0, keepdims=False)
        along_x = plane_index.astype(jnp.float32) + own_frac[..., 0]
        along_y = grid_y + own_frac[..., 1]
        along_z = grid_z + own_frac[..., 2]
        return jnp.stack([along_x, along_y, along_z], axis=-1).reshape(-1, 3)

    def accumulate(running, plane_index):
        phase_cos, phase_sin = phases(scaled, plane_positions(plane_index))
        plane_charge = lax.dynamic_index_in_dim(charges, plane_index, 0, keepdims=False)
        term = jnp.stack([jnp.dot(phase_cos, plane_charge, preferred_element_type=jnp.float32), jnp.dot(phase_sin, plane_charge, preferred_element_type=jnp.float32)])
        return (running + term, None)
    factor, _unused = lax.scan(accumulate, jnp.zeros((2, K, F), jnp.float32), planes)
    weighted = (factor * kweight[None, :, None] * math.sqrt(K / SITES)).astype(jnp.bfloat16)
    contract = (((0,), (0,)), ((), ()))

    def plane_recip(plane_index):
        phase_cos, phase_sin = phases(scaled, plane_positions(plane_index))
        recip = lax.dot_general(phase_cos, weighted[0], contract, preferred_element_type=jnp.float32)
        recip = recip + lax.dot_general(phase_sin, weighted[1], contract, preferred_element_type=jnp.float32)
        return jnp.dot(recip.astype(jnp.bfloat16), w_out, preferred_element_type=jnp.float32)
    long_range = lax.map(plane_recip, planes).reshape(NX, NY, NZ, SLOTS, F)
    updated = features.astype(jnp.float32) + jax.nn.silu(short) + long_range
    return jnp.where(occupied[..., None], updated, 0.0).astype(jnp.bfloat16)
```

```python
import functools
import math

import jax
import jax.numpy as jnp
from jax import lax
from jax.experimental import pallas as pl
from jax.experimental.pallas import tpu as pltpu
from jax.sharding import PartitionSpec as P

TWO_PI = 2.0 * math.pi
SHARPNESS = 600.0
CENTER_LOW = 0.2
CENTER_SPAN = 0.5
SCREEN = 16.0
FAR = 8.0
BF16 = jnp.bfloat16
F32 = jnp.float32
AXES = ("gx", "gy")
KTILE = 256

COS = (
    0.9999992215641686,
    -19.738982514492687,
    64.92872654701725,
    -85.27239608425373,
    58.794033945704726,
    -21.076773632203547,
)
SIN = (
    6.28318281853067,
    -41.34142139672705,
    81.59618382164335,
    -76.58009998806374,
    41.205392442366964,
    -12.271258434551658,
)
NT = (((1,), (1,)), ((), ()))


def horner(coefs, s):
    value = coefs[-1] * s + coefs[-2]
    for c in coefs[-3::-1]:
        value = value * s + c
    return value


def factor_kernel(grid_all, scale_all, pos, kmat, kall, feat, wc_t, mask, ph, fac, charges, kw):
    step = pl.program_id(0)
    atoms = pos.shape[0]
    basis_k = kall.shape[1]

    @pl.when(step == 0)
    def _():
        for j in range(0, atoms, 256):
            c = lax.dot_general(
                wc_t[...], feat[j : j + 256, :], NT, preferred_element_type=F32
            )
            charges[:, j : j + 256] = (c * mask[0:1, j : j + 256]).astype(BF16)
        k_sq = jnp.zeros((1, basis_k), F32)
        for d in range(3):
            wave = TWO_PI * kall[d : d + 1, :].astype(F32)
            k_sq = k_sq + wave * wave
        screened = jnp.exp(-k_sq / (4.0 * SCREEN)) / k_sq
        total = jnp.sum(screened, axis=1, keepdims=True)
        row = screened / total * scale_all
        for j in range(0, basis_k, KTILE):
            kw[j // KTILE] = jnp.broadcast_to(row[:, j : j + KTILE], (8, KTILE))

    for j in range(0, atoms, 256):
        t = jnp.dot(pos[j : j + 256, :], kmat[...], preferred_element_type=F32)
        r = t - jnp.round(t)
        s = r * r
        ph[0, j : j + 256, :] = horner(COS, s).astype(BF16)
        ph[1, j : j + 256, :] = (horner(SIN, s) * r).astype(BF16)
    weight = kw[step][0:1, :]
    rows = charges.shape[0]
    for p in range(2):
        part = jnp.dot(charges[...], ph[p], preferred_element_type=F32)
        fac[p * rows : (p + 1) * rows, :] = part * weight


def factor_call(pos, kmat, feat, wc_t, mask, grid_all, scale_all):
    atoms, width = feat.shape
    vectors = kmat.shape[1]
    steps = vectors // KTILE
    lanes = pos.shape[1]
    return pl.pallas_call(
        functools.partial(factor_kernel, grid_all, scale_all),
        grid=(steps,),
        in_specs=[
            pl.BlockSpec((atoms, lanes), lambda i: (0, 0)),
            pl.BlockSpec((lanes, KTILE), lambda i: (0, i)),
            pl.BlockSpec((lanes, vectors), lambda i: (0, 0)),
            pl.BlockSpec((atoms, width), lambda i: (0, 0)),
            pl.BlockSpec((width, width), lambda i: (0, 0)),
            pl.BlockSpec((1, atoms), lambda i: (0, 0)),
        ],
        out_specs=[
            pl.BlockSpec((2, atoms, KTILE), lambda i: (0, 0, i)),
            pl.BlockSpec((2 * width, KTILE), lambda i: (i, 0)),
        ],
        out_shape=[
            jax.ShapeDtypeStruct((2, atoms, vectors), BF16),
            jax.ShapeDtypeStruct((steps * 2 * width, KTILE), F32),
        ],
        scratch_shapes=[
            pltpu.VMEM((width, atoms), BF16),
            pltpu.VMEM((steps, 8, KTILE), F32),
        ],
        compiler_params=pltpu.CompilerParams(
            dimension_semantics=("arbitrary",), vmem_limit_bytes=40 << 20
        ),
        cost_estimate=pl.CostEstimate(
            flops=6 * atoms * vectors * width, bytes_accessed=16 << 20, transcendentals=0
        ),
        name="factor",
    )(pos, kmat, kmat, feat, wc_t, mask)


def short_kernel(slots, basis, lo, mid, hi, own, feat, w, out, agg):
    xi = pl.program_id(1)
    rows = feat.shape[2]
    width = feat.shape[3]
    pairs = rows // (2 * slots)
    two = 2 * slots
    window = 4 * slots
    sub = lax.broadcasted_iota(jnp.int32, (8, 128), 0)
    lane = lax.broadcasted_iota(jnp.int32, (8, 128), 1)
    lane_block = lane // window
    cell_in_window = (lane % window) // slots
    z_off = jnp.where(sub == 2, (cell_in_window - 1).astype(F32), 0.0)
    refs = (lo, mid, hi)
    columns = [(dx, dy) for dx in (-1, 0, 1) for dy in (-1, 0, 1) if (dx, dy) != (0, 0)]
    columns.append((0, 0))
    placed = []
    for dx, dy in columns:
        coords = refs[dy + 1][xi + 1 + dx, 0, rows : rows + 16, 0:128].astype(F32)[0:8]
        shift = jnp.where(sub == 0, float(dx), jnp.where(sub == 1, float(dy), 0.0))
        placed.append(coords + shift)
    select = jnp.where(
        lax.broadcasted_iota(jnp.int32, (16, 384), 0)
        == lax.broadcasted_iota(jnp.int32, (16, 384), 1) // 128,
        1.0,
        0.0,
    ).astype(BF16)
    own_all = jnp.dot(own[xi, 0], select, preferred_element_type=F32)
    stretch = math.sqrt(SHARPNESS * math.log2(math.e))
    centers = [stretch * (CENTER_LOW + b * (CENTER_SPAN / (basis - 1))) for b in range(basis)]

    for p in range(pairs):
        packed = []
        for h in range(3):
            merged = None
            for c in range(4 * h, min(4 * h + 4, 9)):
                amount = (window * (c % 4) - two * p) % 128
                moved = pltpu.roll(placed[c], amount, axis=1) if amount else placed[c]
                merged = moved if merged is None else jnp.where(lane_block == c % 4, moved, merged)
            merged = merged + z_off
            if h == 2:
                merged = jnp.where(lane_block == 0, merged, FAR)
            packed.append([jnp.broadcast_to(merged[d : d + 1, :], (8, 128)) for d in range(3)])
        parts = [[None, None] for _ in range(3)]
        for h in range(3):
            for q in range(2):
                r0 = two * p + slots * q
                d2 = None
                for d in range(3):
                    mine = own_all[r0 : r0 + slots, 128 * d : 128 * d + 128]
                    if d == 2 and q == 1:
                        mine = mine + 1.0
                    delta = packed[h][d] - mine
                    d2 = delta * delta if d2 is None else d2 + delta * delta
                env = jnp.maximum(1.0 - d2, 0.0)
                env = env * env
                if h == 2:
                    env = jnp.where(lane == sub + slots * (1 + q), 0.0, env)
                ar = jnp.sqrt(d2) * stretch
                values = []
                for b in range(basis):
                    u = ar - centers[b]
                    values.append(jnp.exp2(u * (centers[b] - ar)) * env)
                parts[h][q] = values
        lhs = []
        for h in range(3):
            lhs.append(
                jnp.concatenate(
                    [
                        jnp.concatenate([parts[h][0][b], parts[h][1][b]], axis=0).astype(BF16)
                        for b in range(basis)
                    ],
                    axis=0,
                )
            )
        near = []
        for dx, dy in columns:
            ref = refs[dy + 1]
            near.append(ref[xi + 1 + dx, 0, two * p : two * p + two, :])
            nxt = two * ((p + 1) % pairs)
            near.append(ref[xi + 1 + dx, 0, nxt : nxt + two, :])
        pad = jnp.zeros((384 - 9 * window, width), BF16)
        total = jnp.dot(
            jnp.concatenate(lhs, axis=1),
            jnp.concatenate(near + [pad], axis=0),
            preferred_element_type=F32,
        ).astype(BF16)
        for b in range(basis):
            agg[xi, two * p : two * p + two, width * b : width * (b + 1)] = total[
                two * b : two * b + two
            ]

    @pl.when(xi == pl.num_programs(1) - 1)
    def _():
        planes = feat.shape[0]
        value = jnp.dot(
            agg[...].reshape(planes * rows, basis * width), w[...], preferred_element_type=F32
        )
        value = jax.nn.silu(value).reshape(planes, rows, width)
        out[:, 0] = feat[:, 0].astype(F32) + value


def short_call(ext, own, feat, w_flat, slots, basis, first, count):
    planes, cols, rows, width = feat.shape
    ext_rows = ext.shape[2]
    lanes = own.shape[3]
    window = lambda off: pl.BlockSpec(
        (planes + 2, 1, ext_rows, width), lambda y, x: (0, y + first + off, 0, 0)
    )
    return pl.pallas_call(
        functools.partial(short_kernel, slots, basis),
        grid=(count, planes),
        in_specs=[
            window(0),
            window(1),
            window(2),
            pl.BlockSpec((planes, 1, rows, lanes), lambda y, x: (0, y + first, 0, 0)),
            pl.BlockSpec((planes, 1, rows, width), lambda y, x: (0, y + first, 0, 0)),
            pl.BlockSpec((basis * width, width), lambda y, x: (0, 0)),
        ],
        out_specs=pl.BlockSpec((planes, 1, rows, width), lambda y, x: (0, y, 0, 0)),
        out_shape=jax.ShapeDtypeStruct((planes, count, rows, width), F32),
        scratch_shapes=[pltpu.VMEM((planes, rows, basis * width), BF16)],
        compiler_params=pltpu.CompilerParams(
            dimension_semantics=("arbitrary", "arbitrary"), vmem_limit_bytes=40 << 20
        ),
        cost_estimate=pl.CostEstimate(
            flops=count * planes * rows * width * 2 * (basis * 384 + basis * width),
            bytes_accessed=8 << 20,
            transcendentals=count * planes * rows * 384 * (basis + 1),
        ),
        name="short",
    )(ext, ext, ext, own, feat, w_flat)


def field_kernel(ph, weighted, w_out, base, mask, out):
    tiles = weighted.shape[0]
    lhs = jnp.concatenate(
        [ph[t % 2, :, KTILE * (t // 2) : KTILE * (t // 2 + 1)] for t in range(tiles)], axis=1
    )
    rhs = jnp.concatenate([weighted[t] for t in range(tiles)], axis=1)
    recip = lax.dot_general(lhs, rhs, NT, preferred_element_type=F32)
    far = jnp.dot(recip.astype(BF16), w_out[...], preferred_element_type=F32)
    value = base[...] + far
    out[...] = jnp.where(mask[...] > 0.0, value, 0.0).astype(BF16)


def field_call(ph, weighted, w_out, base, mask, tile=256):
    _, atoms, vectors = ph.shape
    tiles, width, _ = weighted.shape
    return pl.pallas_call(
        field_kernel,
        grid=(atoms // tile,),
        in_specs=[
            pl.BlockSpec((2, tile, vectors), lambda i: (0, i, 0)),
            pl.BlockSpec((tiles, width, KTILE), lambda i: (0, 0, 0)),
            pl.BlockSpec((width, width), lambda i: (0, 0)),
            pl.BlockSpec((tile, width), lambda i: (i, 0)),
            pl.BlockSpec((tile, 1), lambda i: (i, 0)),
        ],
        out_specs=pl.BlockSpec((tile, width), lambda i: (i, 0)),
        out_shape=jax.ShapeDtypeStruct((atoms, width), BF16),
        compiler_params=pltpu.CompilerParams(
            dimension_semantics=("arbitrary",), vmem_limit_bytes=40 << 20
        ),
        cost_estimate=pl.CostEstimate(
            flops=4 * atoms * vectors * width, bytes_accessed=16 << 20, transcendentals=0
        ),
        name="field",
    )(ph, weighted, w_out, base, mask)


def my_index():
    return lax.axis_index("gx") * lax.axis_size("gy") + lax.axis_index("gy")


def swap(value, bit):
    count = lax.axis_size("gx") * lax.axis_size("gy")
    return lax.ppermute(value, AXES, [(i, i ^ bit) for i in range(count)])


def reduce_halving(value, bits):
    for bit in bits:
        half = value.shape[0] // 2
        mine = (my_index() // bit) % 2
        keep = lax.dynamic_slice_in_dim(value, mine * half, half, 0)
        give = lax.dynamic_slice_in_dim(value, (1 - mine) * half, half, 0).astype(BF16)
        value = keep + swap(give, bit).astype(F32)
    return value


def gather_doubling(value, bits):
    for bit in bits:
        mine = (my_index() // bit) % 2
        other = swap(value, bit)
        value = jnp.where(
            mine == 0, jnp.concatenate([value, other]), jnp.concatenate([other, value])
        )
    return value


def with_halo(cells, axis, dim):
    count = lax.axis_size(axis)
    size = cells.shape[dim]
    if count == 2 and size == 2:
        other = lax.ppermute(cells, axis, [(0, 1), (1, 0)])
        left = lax.slice_in_dim(other, 1, 2, axis=dim)
        right = lax.slice_in_dim(other, 0, 1, axis=dim)
    else:
        head = lax.slice_in_dim(cells, 0, 1, axis=dim)
        tail = lax.slice_in_dim(cells, size - 1, size, axis=dim)
        left = lax.ppermute(tail, axis, [(i, (i + 1) % count) for i in range(count)])
        right = lax.ppermute(head, axis, [((i + 1) % count, i) for i in range(count)])
    return jnp.concatenate([left, cells, right], axis=dim)


def on_device(features, fractions, counts, k_index, w_short, w_charge, w_out):
    planes, cols, depth, slots, width = features.shape
    basis = w_short.shape[0]
    vectors = k_index.shape[0]
    rows = depth * slots
    atoms = planes * cols * rows
    grid_all = (planes * lax.axis_size("gx"), cols * lax.axis_size("gy"), depth)
    assert rows == 128 and slots == 8 and vectors % KTILE == 0 and width % 128 == 0
    for extent in grid_all:
        assert extent & (extent - 1) == 0 and extent <= 256
    scale_all = math.sqrt(vectors / (grid_all[0] * grid_all[1] * grid_all[2] * slots))

    occupied = jnp.arange(slots, dtype=jnp.int32) < counts[..., None]
    feat = features.reshape(planes, cols, rows, width)

    placed = jnp.where(occupied[..., None], fractions, jnp.asarray(FAR, BF16))
    placed = jnp.roll(placed.reshape(planes, cols, rows, 3), slots, axis=2)
    placed = jnp.swapaxes(placed, 2, 3)
    placed = jnp.pad(placed, ((0, 0), (0, 0), (0, 13), (0, width - rows)))
    block = jnp.concatenate([feat[:, :, rows - slots :], feat[:, :, : rows - slots], placed], axis=2)
    ext = with_halo(with_halo(block, "gx", 0), "gy", 1)

    start_x = lax.axis_index("gx") * planes
    start_y = lax.axis_index("gy") * cols
    shape = (planes, cols, depth, slots)
    cells = [
        jnp.broadcast_to((start_x + jnp.arange(planes))[:, None, None, None], shape),
        jnp.broadcast_to((start_y + jnp.arange(cols))[None, :, None, None], shape),
        jnp.broadcast_to(jnp.arange(depth)[None, None, :, None], shape),
    ]
    cells = jnp.stack(cells, axis=-1).astype(BF16)
    pos = jnp.concatenate([fractions, cells, jnp.zeros(shape + (10,), BF16)], axis=-1)
    pos = pos.reshape(planes, cols, rows, 16)
    scaled = k_index.astype(F32) / jnp.array(grid_all, F32)
    kmat = jnp.pad(jnp.concatenate([scaled, scaled], axis=1).T, ((0, 10), (0, 0))).astype(BF16)

    flat = feat.reshape(atoms, width)
    mask = occupied.reshape(1, atoms).astype(F32)
    ph, partial = factor_call(
        pos.reshape(atoms, 16), kmat, flat, w_charge.T, mask, grid_all, scale_all
    )

    count = lax.axis_size("gx") * lax.axis_size("gy")
    bits = [1 << i for i in range(count.bit_length() - 1)]
    reduced = reduce_halving(partial, bits).astype(BF16)
    weighted = gather_doubling(reduced, bits[::-1])
    weighted = weighted.reshape(2 * vectors // KTILE, width, KTILE)

    w_flat = w_short.reshape(basis * width, width)
    step = max(cols // 4, 1)
    bases = [
        short_call(ext, pos, feat, w_flat, slots, basis, first, step)
        for first in range(0, cols, step)
    ]
    base = jnp.concatenate(bases, axis=1).reshape(atoms, width)
    out = field_call(ph, weighted, w_out, base, occupied.reshape(atoms, 1).astype(F32))
    return out.reshape(features.shape)


def solution(mesh):
    return jax.shard_map(
        on_device,
        mesh=mesh,
        in_specs=(
            P("gx", "gy", None, None, None),
            P("gx", "gy", None, None, None),
            P("gx", "gy", None),
            P(),
            P(),
            P(),
            P(),
        ),
        out_specs=P("gx", "gy", None, None, None),
        check_vma=False,
    )
```

```python
import functools
import math

import jax
import jax.numpy as jnp
from jax import lax
from jax.experimental import pallas as pl
from jax.experimental.pallas import tpu as pltpu
from jax.sharding import PartitionSpec as P

TWO_PI = 2.0 * math.pi
SHARPNESS = 600.0
CENTER_LOW = 0.2
CENTER_SPAN = 0.5
SCREEN = 16.0
FAR = 8.0
BF16 = jnp.bfloat16
F32 = jnp.float32
AXES = ("gx", "gy")
KTILE = 256

HALF_COS = (
    1.4142134965644628,
    -6.978850988150233,
    5.739461168545313,
    -1.8835629713129327,
    0.3106981552009573,
)
HALF_SIN = (4.442867902918289, -7.307443416752583, 3.594788034903934, -0.7843739144750123)
NT = (((1,), (1,)), ((), ()))
TN = (((0,), (0,)), ((), ()))
TT = (((0,), (1,)), ((), ()))
OCC_ROW = 3
CELL_ROW = 4
POS_ROWS = 16
VMEM = pltpu.VMEM


def horner(coefs, s):
    value = coefs[-1] * s + coefs[-2]
    for c in coefs[-3::-1]:
        value = value * s + c
    return value


def factor_kernel(grid_all, scale_all, pos, kidx, feat, wc, ph, fac, charges, kmat, kw):
    step = pl.program_id(0)
    planes, cols, _, rows = pos.shape
    atoms = planes * cols * rows
    vectors = kidx.shape[1]

    @pl.when(step == 0)
    def _():
        sub = lax.broadcasted_iota(jnp.int32, (POS_ROWS, KTILE), 0)
        parts = []
        for j in range(0, vectors, KTILE):
            waves = [
                kidx[d : d + 1, j : j + KTILE].astype(F32) * (1.0 / grid_all[d]) for d in range(3)
            ]
            value = jnp.zeros((POS_ROWS, KTILE), F32)
            k_sq = jnp.zeros((1, KTILE), F32)
            for d in range(3):
                hit = (sub == d) | (sub == CELL_ROW + d)
                value = jnp.where(hit, jnp.broadcast_to(waves[d], value.shape), value)
                wave = TWO_PI * waves[d]
                k_sq = k_sq + wave * wave
            kmat[j // KTILE] = value.astype(BF16)
            parts.append(jnp.exp(-k_sq / (4.0 * SCREEN)) / k_sq)
        total = sum(jnp.sum(part, axis=1, keepdims=True) for part in parts)
        for j, part in enumerate(parts):
            kw[j] = jnp.broadcast_to(part / total * scale_all, (8, KTILE))
        for x in range(planes):
            for y in range(cols):
                j = (x * cols + y) * rows
                c = lax.dot_general(wc[...], feat[j : j + rows, :], TT, preferred_element_type=F32)
                occ = pos[x, y, OCC_ROW : OCC_ROW + 1, :].astype(F32)
                charges[:, j : j + rows] = (c * occ).astype(BF16)

    sub = lax.broadcasted_iota(jnp.int32, (POS_ROWS, rows), 0)
    depth = (lax.broadcasted_iota(jnp.int32, (POS_ROWS, rows), 1) // 8).astype(F32)
    x0 = (lax.axis_index("gx") * planes).astype(F32)
    y0 = (lax.axis_index("gy") * cols).astype(F32)
    for x in range(planes):
        for y in range(cols):
            j = (x * cols + y) * rows
            tile = pos[x, y].astype(F32)
            tile = jnp.where(sub == CELL_ROW, x0 + float(x), tile)
            tile = jnp.where(sub == CELL_ROW + 1, y0 + float(y), tile)
            tile = jnp.where(sub == CELL_ROW + 2, depth, tile)
            t = lax.dot_general(tile.astype(BF16), kmat[step], TN, preferred_element_type=F32)
            r = t - jnp.round(t)
            s = r * r
            half_c = horner(HALF_COS, s)
            half_s = horner(HALF_SIN, s) * r
            ph[0, j : j + rows, :] = (1.0 - half_s * half_s).astype(BF16)
            ph[1, j : j + rows, :] = (half_s * half_c).astype(BF16)
    weight = kw[step][0:1, :]
    width = charges.shape[0]
    for p in range(2):
        part = jnp.dot(charges[...], ph[p], preferred_element_type=F32)
        fac[p * width : (p + 1) * width, :] = part * weight


def factor_call(pos, kidx, feat, wc, grid_all, scale_all):
    planes, cols, _, rows = pos.shape
    atoms, width = feat.shape
    vectors = kidx.shape[1]
    steps = vectors // KTILE
    return pl.pallas_call(
        functools.partial(factor_kernel, grid_all, scale_all),
        grid=(steps,),
        in_specs=[
            pl.BlockSpec(pos.shape, lambda i: (0, 0, 0, 0)),
            pl.BlockSpec(kidx.shape, lambda i: (0, 0)),
            pl.BlockSpec((atoms, width), lambda i: (0, 0)),
            pl.BlockSpec((width, width), lambda i: (0, 0)),
        ],
        out_specs=[
            pl.BlockSpec((2, atoms, KTILE), lambda i: (0, 0, i)),
            pl.BlockSpec((2 * width, KTILE), lambda i: (i, 0)),
        ],
        out_shape=[
            jax.ShapeDtypeStruct((2, atoms, vectors), BF16),
            jax.ShapeDtypeStruct((steps * 2 * width, KTILE), F32),
        ],
        scratch_shapes=[
            VMEM((width, atoms), BF16),
            VMEM((steps, POS_ROWS, KTILE), BF16),
            VMEM((steps, 8, KTILE), F32),
        ],
        compiler_params=pltpu.CompilerParams(
            dimension_semantics=("arbitrary",), vmem_limit_bytes=20 << 20
        ),
        cost_estimate=pl.CostEstimate(
            flops=24 * atoms * vectors * width, bytes_accessed=16 << 20, transcendentals=0
        ),
        name="factor",
    )(pos, kidx, feat, wc)


def short_rows(slots, basis, planes, rows, width, near_feat, near_pos, own_pos, own_feat, w, out, agg):
    pairs = rows // (2 * slots)
    two = 2 * slots
    window = 4 * slots
    sub = lax.broadcasted_iota(jnp.int32, (8, 128), 0)
    lane = lax.broadcasted_iota(jnp.int32, (8, 128), 1)
    lane_block = lane // window
    cell_in_window = (lane % window) // slots
    z_off = jnp.where(sub == 2, (cell_in_window - 1).astype(F32), 0.0)
    columns = [(dx, dy) for dx in (-1, 0, 1) for dy in (-1, 0, 1) if (dx, dy) != (0, 0)]
    columns.append((0, 0))
    select = jnp.where(
        lax.broadcasted_iota(jnp.int32, (POS_ROWS, 384), 0)
        == lax.broadcasted_iota(jnp.int32, (POS_ROWS, 384), 1) // 128,
        1.0,
        0.0,
    ).astype(BF16)
    stretch = math.sqrt(SHARPNESS * math.log2(math.e))
    centers = [stretch * (CENTER_LOW + b * (CENTER_SPAN / (basis - 1))) for b in range(basis)]

    for xi in range(planes):
        placed = []
        for dx, dy in columns:
            coords = near_pos(xi + dx, dy).astype(F32)[0:8]
            occ = jnp.broadcast_to(coords[OCC_ROW : OCC_ROW + 1, :], coords.shape)
            shift = jnp.where(sub == 0, float(dx), jnp.where(sub == 1, float(dy), 0.0))
            placed.append(jnp.where(occ > 0.0, coords + shift, FAR))
        own_all = lax.dot_general(own_pos(xi), select, TN, preferred_element_type=F32)
        for p in range(pairs):
            packed = []
            for h in range(3):
                merged = None
                for c in range(4 * h, min(4 * h + 4, 9)):
                    amount = (window * (c % 4) - two * p) % 128
                    moved = pltpu.roll(placed[c], amount, axis=1) if amount else placed[c]
                    merged = (
                        moved if merged is None else jnp.where(lane_block == c % 4, moved, merged)
                    )
                merged = merged + z_off
                if h == 2:
                    merged = jnp.where(lane_block == 0, merged, FAR)
                packed.append([jnp.broadcast_to(merged[d : d + 1, :], (8, 128)) for d in range(3)])
            parts = [[None, None] for _ in range(3)]
            for h in range(3):
                for q in range(2):
                    r0 = (two * p + slots * (1 + q)) % rows
                    d2 = None
                    for d in range(3):
                        mine = own_all[r0 : r0 + slots, 128 * d : 128 * d + 128]
                        if d == 2 and q == 1:
                            mine = mine + 1.0
                        delta = packed[h][d] - mine
                        d2 = delta * delta if d2 is None else d2 + delta * delta
                    env = jnp.maximum(1.0 - d2, 0.0)
                    env = env * env
                    if h == 2:
                        env = jnp.where(lane == sub + slots * (1 + q), 0.0, env)
                    ar = jnp.sqrt(d2) * stretch
                    values = []
                    for b in range(basis):
                        u = ar - centers[b]
                        values.append(jnp.exp2(u * (centers[b] - ar)) * env)
                    parts[h][q] = values
            lhs = []
            for h in range(3):
                lhs.append(
                    jnp.concatenate(
                        [
                            jnp.concatenate([parts[h][0][b], parts[h][1][b]], axis=0).astype(BF16)
                            for b in range(basis)
                        ],
                        axis=0,
                    )
                )
            near = []
            nxt = two * ((p + 1) % pairs)
            for dx, dy in columns:
                near.append(near_feat(xi + dx, dy, two * p, two))
                near.append(near_feat(xi + dx, dy, nxt, two))
            pad = jnp.zeros((384 - 9 * window, width), BF16)
            total = jnp.dot(
                jnp.concatenate(lhs, axis=1),
                jnp.concatenate(near + [pad], axis=0),
                preferred_element_type=F32,
            ).astype(BF16)
            for b in range(basis):
                agg[xi, two * p : two * p + two, width * b : width * (b + 1)] = total[
                    two * b : two * b + two
                ]
    value = jnp.dot(
        agg[...].reshape(planes * rows, basis * width), w[...], preferred_element_type=F32
    )
    value = jax.nn.silu(value).reshape(planes, rows, width)
    for xi in range(planes):
        turned = jnp.concatenate([value[xi, rows - slots :], value[xi, : rows - slots]], axis=0)
        out(xi, own_feat(xi).astype(F32) + turned)


def inner_kernel(slots, basis, first, count, feat, pos, side_feat, side_pos, w, out, agg):
    planes, _, rows, width = feat.shape

    def body(i, carry):
        y = first + i

        def pick(ref, side, x):
            if 0 <= x < planes:
                return ref, x
            return side, (0 if x == planes else 1)

        def near_feat(x, dy, start, size):
            ref, i = pick(feat, side_feat, x)
            return ref[i, y + dy, start : start + size, :]

        def near_pos(x, dy):
            ref, i = pick(pos, side_pos, x)
            return ref[i, y + dy]

        def write(x, value):
            out[i, x] = value

        short_rows(
            slots, basis, planes, rows, width, near_feat, near_pos,
            lambda x: pos[x, y], lambda x: feat[x, y], w, write, agg,
        )
        return carry

    lax.fori_loop(0, count, body, 0)


def edge_kernel(slots, basis, y, halo_dy, feat, pos, side_feat, side_pos, halo, w, out, agg):
    planes, _, rows, width = feat.shape

    def pick(ref, side, x):
        if 0 <= x < planes:
            return ref, x
        return side, (0 if x == planes else 1)

    def near_feat(x, dy, start, size):
        if dy == halo_dy:
            return halo[x + 1, 0, start : start + size, :]
        ref, i = pick(feat, side_feat, x)
        return ref[i, y + dy, start : start + size, :]

    def near_pos(x, dy):
        if dy == halo_dy:
            return halo[x + 1, 0, rows : rows + POS_ROWS, 0:128]
        ref, i = pick(pos, side_pos, x)
        return ref[i, y + dy]

    def write(x, value):
        out[0, x] = value

    short_rows(
        slots, basis, planes, rows, width, near_feat, near_pos,
        lambda x: pos[x, y], lambda x: feat[x, y], w, write, agg,
    )


def short_call(kernel, name, count, basis, *args):
    planes, _, rows, width = args[0].shape
    whole = pl.BlockSpec(memory_space=VMEM)
    return pl.pallas_call(
        kernel,
        in_specs=[whole] * len(args),
        out_specs=whole,
        out_shape=jax.ShapeDtypeStruct((count, planes, rows, width), F32),
        scratch_shapes=[VMEM((planes, rows, basis * width), BF16)],
        compiler_params=pltpu.CompilerParams(vmem_limit_bytes=16 << 20),
        cost_estimate=pl.CostEstimate(
            flops=count * planes * rows * width * 8 * (basis * 384 + basis * width),
            bytes_accessed=4 << 20,
            transcendentals=count * planes * rows * 384 * (basis + 1),
        ),
        name=name,
    )(*args)


def field_kernel(ph, weighted, w_out, base, pos, out):
    tiles, width, _ = weighted.shape
    lhs = jnp.concatenate(
        [ph[t % 2, :, KTILE * (t // 2) : KTILE * (t // 2 + 1)] for t in range(tiles)], axis=1
    )
    rhs = jnp.concatenate([weighted[t] for t in range(tiles)], axis=1)
    recip = lax.dot_general(lhs, rhs, NT, preferred_element_type=F32)
    far = jnp.dot(recip.astype(BF16), w_out[...], preferred_element_type=F32)
    sub = lax.broadcasted_iota(jnp.int32, (POS_ROWS, width), 0)
    select = jnp.where(sub == OCC_ROW, 1.0, 0.0).astype(BF16)
    rows = base.shape[2]
    for y in range(base.shape[0]):
        occ = lax.dot_general(pos[0, y], select, TN, preferred_element_type=F32)
        value = base[y, 0] + far[rows * y : rows * (y + 1)]
        out[rows * y : rows * (y + 1), :] = jnp.where(occ > 0.0, value, 0.0).astype(BF16)


def field_call(ph, weighted, w_out, base, pos, group=2):
    _, atoms, vectors = ph.shape
    tiles, width, _ = weighted.shape
    cols, planes, rows, _ = base.shape
    tile = group * rows
    groups = cols // group
    return pl.pallas_call(
        field_kernel,
        grid=(atoms // tile,),
        in_specs=[
            pl.BlockSpec((2, tile, vectors), lambda i: (0, i, 0)),
            pl.BlockSpec((tiles, width, KTILE), lambda i: (0, 0, 0)),
            pl.BlockSpec((width, width), lambda i: (0, 0)),
            pl.BlockSpec((group, 1, rows, width), lambda i: (i % groups, i // groups, 0, 0)),
            pl.BlockSpec((1, group, POS_ROWS, rows), lambda i: (i // groups, i % groups, 0, 0)),
        ],
        out_specs=pl.BlockSpec((tile, width), lambda i: (i, 0)),
        out_shape=jax.ShapeDtypeStruct((atoms, width), BF16),
        compiler_params=pltpu.CompilerParams(
            dimension_semantics=("arbitrary",), vmem_limit_bytes=16 << 20
        ),
        cost_estimate=pl.CostEstimate(
            flops=4 * atoms * vectors * width, bytes_accessed=16 << 20, transcendentals=0
        ),
        name="field",
    )(ph, weighted, w_out, base, pos)


def my_index():
    return lax.axis_index("gx") * lax.axis_size("gy") + lax.axis_index("gy")


def swap(value, mask):
    count = lax.axis_size("gx") * lax.axis_size("gy")
    return lax.ppermute(value, AXES, [(i, i ^ mask) for i in range(count)])


def tied(*values):
    return lax.optimization_barrier(values)


def no_work():
    return ()


class Exchange:
    def __init__(self):
        size_y = lax.axis_size("gy")
        count = lax.axis_size("gx") * size_y
        bits = [1 << i for i in range(count.bit_length() - 1)]
        low = [b for b in bits if b < size_y]
        self.halved = low[:2]
        self.direct = low[2:4]
        self.whole = low[4:] + [b for b in bits if b >= size_y]
        self.masks = [0]
        for b in self.direct:
            self.masks = self.masks + [m ^ b for m in self.masks]

    def place(self):
        return sum(((my_index() // b) % 2) << k for k, b in enumerate(self.direct))

    def halve(self, value, bit, work=no_work, arrived=()):
        half = value.shape[0] // 2
        mine = (my_index() // bit) % 2
        keep = lax.dynamic_slice_in_dim(value, mine * half, half, 0)
        give = lax.dynamic_slice_in_dim(value, (1 - mine) * half, half, 0).astype(BF16)
        got, arrived = tied(swap(give, bit), arrived)
        return keep + got.astype(F32), arrived

    def spread_sum(self, value, work):
        count = len(self.masks)
        value = value.reshape((count, -1) + value.shape[1:])
        me = self.place()
        keep = lax.dynamic_index_in_dim(value, me, 0, False)
        gives = [
            lax.dynamic_index_in_dim(value, me ^ j, 0, False).astype(BF16) for j in range(1, count)
        ]
        gives, done = run_under(gives, self.masks[1:], work)
        for got in gives:
            keep = keep + got.astype(F32)
        return keep, done

    def whole_sum(self, value, bit, work=no_work):
        (got,), done = run_under([value.astype(BF16)], [bit], work)
        return value + got.astype(F32), done

    def spread(self, value, work):
        count = len(self.masks)
        got, done = run_under([value] * (count - 1), self.masks[1:], work)
        parts = jnp.stack([value] + got)
        me = self.place()
        for k in range(len(self.direct)):
            b = 1 << k
            cut = parts.reshape((count // (2 * b), 2, b) + value.shape)
            parts = jnp.where((me >> k) & 1 == 0, cut, cut[:, ::-1]).reshape(parts.shape)
        return parts.reshape((-1,) + value.shape[1:]), done

    def double(self, value, bit, work=no_work):
        mine = (my_index() // bit) % 2
        (other,), done = run_under([value], [bit], work)
        return (
            jnp.where(
                mine == 0, jnp.concatenate([value, other]), jnp.concatenate([other, value])
            ),
            done,
        )


def run_under(gives, masks, work):
    inputs = work.inputs if work is not no_work else ()
    gives, inputs = tied(list(gives), inputs)
    got = [swap(give, mask) for give, mask in zip(gives, masks)]
    done = work(*inputs) if work is not no_work else ()
    return tied(got, done)


class Work:
    def __init__(self, call, *inputs):
        self.call = call
        self.inputs = inputs

    def __call__(self, *inputs):
        return self.call(*inputs)


def side_planes(cells):
    count = lax.axis_size("gx")
    size = cells.shape[0]
    if count == 2 and size == 2:
        return lax.ppermute(cells, "gx", [(0, 1), (1, 0)])
    after = lax.ppermute(cells[:1], "gx", [((i + 1) % count, i) for i in range(count)])
    before = lax.ppermute(cells[size - 1 :], "gx", [(i, (i + 1) % count) for i in range(count)])
    return jnp.concatenate([after, before], axis=0)


def edge_rows(feat, pos, side_feat, side_pos, y):
    width = feat.shape[3]
    parts = []
    for f, q in ((side_feat[1:2], side_pos[1:2]), (feat, pos), (side_feat[0:1], side_pos[0:1])):
        q = jnp.pad(q[:, y : y + 1], ((0, 0), (0, 0), (0, 0), (0, width - q.shape[3])))
        parts.append(jnp.concatenate([f[:, y : y + 1], q], axis=2))
    return jnp.concatenate(parts, axis=0)


def on_device(features, fractions, counts, k_index, w_short, w_charge, w_out):
    planes, cols, depth, slots, width = features.shape
    basis = w_short.shape[0]
    vectors = k_index.shape[0]
    rows = depth * slots
    atoms = planes * cols * rows
    size_x, size_y = lax.axis_size("gx"), lax.axis_size("gy")
    grid_all = (planes * size_x, cols * size_y, depth)
    assert rows == 128 and slots == 8 and planes == 2 and cols == 8 and width == KTILE
    assert vectors % KTILE == 0
    for extent in grid_all:
        assert extent & (extent - 1) == 0 and extent <= 256
    scale_all = math.sqrt(vectors / (grid_all[0] * grid_all[1] * grid_all[2] * slots))

    feat = features.reshape(planes, cols, rows, width)
    side_feat = side_planes(feat)

    occupied = (jnp.arange(slots, dtype=jnp.int32) < counts[..., None]).astype(BF16)
    frac = jnp.transpose(fractions, (0, 1, 4, 2, 3)).reshape(planes, cols, 3, rows)
    pos = jnp.concatenate(
        [
            frac,
            occupied.reshape(planes, cols, 1, rows),
            jnp.zeros((planes, cols, POS_ROWS - 4, rows), BF16),
        ],
        axis=2,
    )
    side_pos = side_planes(pos)

    ph, partial = factor_call(
        pos, k_index.T, feat.reshape(atoms, width), w_charge, grid_all, scale_all
    )

    w_flat = w_short.reshape(basis * width, width)
    exchange = Exchange()

    def inner(first, count):
        kernel = functools.partial(inner_kernel, slots, basis, first, count)
        return lambda *args: short_call(kernel, "short", count, basis, *args)

    def edges(*args):
        *common, low, high, w = args
        first = short_call(
            functools.partial(edge_kernel, slots, basis, 0, -1), "low", 1, basis, *common, low, w
        )
        last = short_call(
            functools.partial(edge_kernel, slots, basis, cols - 1, 1),
            "high", 1, basis, *common, high, w,
        )
        return first, last

    value, _ = exchange.halve(partial, exchange.halved[0])
    value, (side_feat, side_pos) = exchange.halve(
        value, exchange.halved[1], arrived=(side_feat, side_pos)
    )
    near = (feat, pos, side_feat, side_pos)
    up = [(i, (i + 1) % size_y) for i in range(size_y)]
    down = [((i + 1) % size_y, i) for i in range(size_y)]
    low = lax.ppermute(edge_rows(*near, cols - 1), "gy", up)
    high = lax.ppermute(edge_rows(*near, 0), "gy", down)

    value, rows_a = exchange.spread_sum(value, Work(inner(1, 2), *near, w_flat))
    rows_b = None
    for i, bit in enumerate(exchange.whole):
        if i == 0:
            value, rows_b = exchange.whole_sum(value, bit, Work(inner(3, 2), *near, w_flat))
        else:
            value, _ = exchange.whole_sum(value, bit)
    value = value.astype(BF16)
    value, rows_c = exchange.spread(value, Work(inner(5, 2), *near, w_flat))
    value, (row_first, row_last) = exchange.double(
        value, exchange.halved[1], Work(edges, *near, low, high, w_flat)
    )
    value, _ = exchange.double(value, exchange.halved[0])
    weighted = value.reshape(2 * vectors // KTILE, width, KTILE)
    base = jnp.concatenate([row_first, rows_a, rows_b, rows_c, row_last], axis=0)
    out = field_call(ph, weighted, w_out, base, pos)
    return out.reshape(features.shape)


def solution(mesh):
    return jax.shard_map(
        on_device,
        mesh=mesh,
        in_specs=(
            P("gx", "gy", None, None, None),
            P("gx", "gy", None, None, None),
            P("gx", "gy", None),
            P(),
            P(),
            P(),
            P(),
        ),
        out_specs=P("gx", "gy", None, None, None),
        check_vma=False,
    )
```

```python
import functools
import math

import jax
import jax.numpy as jnp
from jax import lax
from jax.experimental import pallas as pl
from jax.experimental.pallas import tpu as pltpu
from jax.sharding import PartitionSpec as P

TWO_PI = 2.0 * math.pi
SHARPNESS = 600.0
CENTER_LOW = 0.2
CENTER_SPAN = 0.5
SCREEN = 16.0
FAR = 8.0
BF16 = jnp.bfloat16
F32 = jnp.float32
AXES = ("gx", "gy")
KTILE = 256

HALF_COS = (
    1.4142134965644628,
    -6.978850988150233,
    5.739461168545313,
    -1.8835629713129327,
    0.3106981552009573,
)
HALF_SIN = (4.442867902918289, -7.307443416752583, 3.594788034903934, -0.7843739144750123)
NT = (((1,), (1,)), ((), ()))
TN = (((0,), (0,)), ((), ()))
TT = (((0,), (1,)), ((), ()))
OCC_ROW = 3
CELL_ROW = 4
POS_ROWS = 16
VMEM = pltpu.VMEM


def horner(coefs, s):
    value = coefs[-1] * s + coefs[-2]
    for c in coefs[-3::-1]:
        value = value * s + c
    return value


def factor_kernel(grid_all, scale_all, pos, kidx, feat, wc, ph, fac, charges, where_at, kmat, kw):
    step = pl.program_id(0)
    planes, cols, _, rows = pos.shape
    vectors = kidx.shape[1]
    atoms, width = feat.shape

    @pl.when(step == 0)
    def _():
        sub = lax.broadcasted_iota(jnp.int32, (POS_ROWS, KTILE), 0)
        parts = []
        for j in range(0, vectors, KTILE):
            waves = [
                kidx[d : d + 1, j : j + KTILE].astype(F32) * (1.0 / grid_all[d]) for d in range(3)
            ]
            value = jnp.zeros((POS_ROWS, KTILE), F32)
            k_sq = jnp.zeros((1, KTILE), F32)
            for d in range(3):
                hit = (sub == d) | (sub == CELL_ROW + d)
                value = jnp.where(hit, jnp.broadcast_to(waves[d], value.shape), value)
                wave = TWO_PI * waves[d]
                k_sq = k_sq + wave * wave
            kmat[j // KTILE] = value.astype(BF16)
            parts.append(jnp.exp(-k_sq / (4.0 * SCREEN)) / k_sq)
        total = sum(jnp.sum(part, axis=1, keepdims=True) for part in parts)
        for j, part in enumerate(parts):
            kw[j] = jnp.broadcast_to(part / total * scale_all, (8, KTILE))
        sub = lax.broadcasted_iota(jnp.int32, (POS_ROWS, rows), 0)
        depth = (lax.broadcasted_iota(jnp.int32, (POS_ROWS, rows), 1) // 8).astype(F32)
        x0 = (lax.axis_index("gx") * planes).astype(F32)
        y0 = (lax.axis_index("gy") * cols).astype(F32)
        turned = wc[...].T
        for x in range(planes):
            for y in range(cols):
                j = (x * cols + y) * rows
                c = lax.dot_general(turned, feat[j : j + rows, :], NT, preferred_element_type=F32)
                tile = pos[x, y].astype(F32)
                charges[:, j : j + rows] = (c * tile[OCC_ROW : OCC_ROW + 1, :]).astype(BF16)
                tile = jnp.where(sub == CELL_ROW, x0 + float(x), tile)
                tile = jnp.where(sub == CELL_ROW + 1, y0 + float(y), tile)
                tile = jnp.where(sub == CELL_ROW + 2, depth, tile)
                where_at[j : j + rows, :] = tile.T.astype(BF16)

    for j in range(0, atoms, 256):
        t_all = jnp.dot(where_at[j : j + 256, :], kmat[step], preferred_element_type=F32)
        for i in range(0, 256, 16):
            t = t_all[i : i + 16]
            r = t - jnp.round(t)
            s = r * r
            half_c = horner(HALF_COS, s)
            half_s = horner(HALF_SIN, s) * r
            ph[0, j + i : j + i + 16, :] = (1.0 - half_s * half_s).astype(BF16)
            ph[1, j + i : j + i + 16, :] = (half_s * half_c).astype(BF16)
    weight = kw[step][0:1, :]
    for p in range(2):
        part = jnp.dot(charges[...], ph[p], preferred_element_type=F32)
        fac[p * width : (p + 1) * width, :] = part * weight


def factor_call(pos, kidx, feat, wc, grid_all, scale_all):
    atoms, width = feat.shape
    vectors = kidx.shape[1]
    steps = vectors // KTILE
    return pl.pallas_call(
        functools.partial(factor_kernel, grid_all, scale_all),
        grid=(steps,),
        in_specs=[
            pl.BlockSpec(pos.shape, lambda i: (0, 0, 0, 0)),
            pl.BlockSpec(kidx.shape, lambda i: (0, 0)),
            pl.BlockSpec((atoms, width), lambda i: (0, 0)),
            pl.BlockSpec((width, width), lambda i: (0, 0)),
        ],
        out_specs=[
            pl.BlockSpec((2, atoms, KTILE), lambda i: (0, 0, i)),
            pl.BlockSpec((2 * width, KTILE), lambda i: (i, 0)),
        ],
        out_shape=[
            jax.ShapeDtypeStruct((2, atoms, vectors), BF16),
            jax.ShapeDtypeStruct((steps * 2 * width, KTILE), F32),
        ],
        scratch_shapes=[
            VMEM((width, atoms), BF16),
            VMEM((atoms, POS_ROWS), BF16),
            VMEM((steps, POS_ROWS, KTILE), BF16),
            VMEM((steps, 8, KTILE), F32),
        ],
        compiler_params=pltpu.CompilerParams(
            dimension_semantics=("arbitrary",), vmem_limit_bytes=56 << 20
        ),
        cost_estimate=pl.CostEstimate(
            flops=24 * atoms * vectors * width, bytes_accessed=16 << 20, transcendentals=0
        ),
        name="factor",
    )(pos, kidx, feat, wc)


def aggregate_row(slots, basis, near_feat, near_pos, own_pos, write):
    rows = 128
    pairs = rows // (2 * slots)
    two = 2 * slots
    window = 4 * slots
    sub = lax.broadcasted_iota(jnp.int32, (8, 128), 0)
    lane = lax.broadcasted_iota(jnp.int32, (8, 128), 1)
    lane_block = lane // window
    cell_in_window = (lane % window) // slots
    z_off = jnp.where(sub == 2, (cell_in_window - 1).astype(F32), 0.0)
    columns = [(dx, dy) for dx in (-1, 0, 1) for dy in (-1, 0, 1) if (dx, dy) != (0, 0)]
    columns.append((0, 0))
    select = jnp.where(
        lax.broadcasted_iota(jnp.int32, (POS_ROWS, 384), 0)
        == lax.broadcasted_iota(jnp.int32, (POS_ROWS, 384), 1) // 128,
        1.0,
        0.0,
    ).astype(BF16)
    stretch = math.sqrt(SHARPNESS)
    centers = [stretch * (CENTER_LOW + b * (CENTER_SPAN / (basis - 1))) for b in range(basis)]

    placed = []
    for dx, dy in columns:
        coords = near_pos(dx, dy).astype(F32)[0:8]
        occ = jnp.broadcast_to(coords[OCC_ROW : OCC_ROW + 1, :], coords.shape)
        shift = jnp.where(sub == 0, float(dx), jnp.where(sub == 1, float(dy), 0.0))
        placed.append(jnp.where(occ > 0.0, coords + shift, FAR))
    own_all = lax.dot_general(own_pos, select, TN, preferred_element_type=F32)
    for p in range(pairs):
        packed = []
        for h in range(3):
            merged = None
            for c in range(4 * h, min(4 * h + 4, 9)):
                amount = (window * (c % 4) - two * p) % 128
                moved = pltpu.roll(placed[c], amount, axis=1) if amount else placed[c]
                merged = moved if merged is None else jnp.where(lane_block == c % 4, moved, merged)
            merged = merged + z_off
            if h == 2:
                merged = jnp.where(lane_block == 0, merged, FAR)
            packed.append([jnp.broadcast_to(merged[d : d + 1, :], (8, 128)) for d in range(3)])
        parts = [[None, None] for _ in range(3)]
        for h in range(3):
            for q in range(2):
                r0 = (two * p + slots * (1 + q)) % rows
                d2 = None
                for d in range(3):
                    mine = own_all[r0 : r0 + slots, 128 * d : 128 * d + 128]
                    if d == 2 and q == 1:
                        mine = mine + 1.0
                    delta = packed[h][d] - mine
                    d2 = delta * delta if d2 is None else d2 + delta * delta
                env = jnp.maximum(1.0 - d2, 0.0)
                env = env * env
                if h == 2:
                    env = jnp.where(lane == sub + slots * (1 + q), 0.0, env)
                ar = (d2 * stretch) * lax.rsqrt(jnp.maximum(d2, 1e-30))
                values = []
                for b in range(basis):
                    u = ar - centers[b]
                    values.append(jnp.exp(u * (centers[b] - ar)) * env)
                parts[h][q] = values
        lhs = []
        for h in range(3):
            lhs.append(
                jnp.concatenate(
                    [
                        jnp.concatenate([parts[h][0][b], parts[h][1][b]], axis=0).astype(BF16)
                        for b in range(basis)
                    ],
                    axis=0,
                )
            )
        near = []
        nxt = two * ((p + 1) % pairs)
        for dx, dy in columns:
            near.append(near_feat(dx, dy, two * p, two))
            near.append(near_feat(dx, dy, nxt, two))
        near.append(jnp.zeros((384 - 9 * window, near[0].shape[1]), BF16))
        total = jnp.dot(
            jnp.concatenate(lhs, axis=1),
            jnp.concatenate(near, axis=0),
            preferred_element_type=F32,
        ).astype(BF16)
        for b in range(basis):
            write(two * p, two, b, total[two * b : two * b + two])


def turn(value, slots):
    return jnp.concatenate([value[128 - slots :], value[: 128 - slots]], axis=0)


def plane_kernel(slots, basis, plane, first, count, feat, pos, side_feat, side_pos, w, *rest):
    out, agg = rest[-2:]
    planes, _, rows, width = feat.shape

    def pick(ref, side, dx):
        x = plane + dx
        return (ref, x) if 0 <= x < planes else (side, 0)

    def body(i, carry):
        y = first + i

        def near_feat(dx, dy, start, size):
            ref, x = pick(feat, side_feat, dx)
            return ref[x, y + dy, start : start + size, :]

        def near_pos(dx, dy):
            ref, x = pick(pos, side_pos, dx)
            return ref[x, y + dy]

        def write(start, size, b, value):
            agg[i, start : start + size, width * b : width * (b + 1)] = value

        aggregate_row(slots, basis, near_feat, near_pos, pos[plane, y], write)
        return carry

    lax.fori_loop(0, count, body, 0)
    value = jnp.dot(
        agg[...].reshape(count * rows, basis * width), w[...], preferred_element_type=F32
    )
    value = jax.nn.silu(value).reshape(count, rows, width)
    for i in range(count):
        out[first + i, plane] = feat[plane, first + i].astype(F32) + turn(value[i], slots)


def edge_kernel(
    slots, basis, y, halo_dy, feat, pos, before, pos_before, after, pos_after, halo, w, *rest
):
    out, agg = rest[-2:]
    planes, _, rows, width = feat.shape
    for plane in range(planes):

        def near_feat(dx, dy, start, size):
            x = plane + dx
            if dy == halo_dy:
                return halo[x + 1, 0, start : start + size, :]
            if 0 <= x < planes:
                return feat[x, y + dy, start : start + size, :]
            return (before if x < 0 else after)[0, y + dy, start : start + size, :]

        def near_pos(dx, dy):
            x = plane + dx
            if dy == halo_dy:
                return halo[x + 1, 0, rows : rows + POS_ROWS, 0:128]
            if 0 <= x < planes:
                return pos[x, y + dy]
            return (pos_before if x < 0 else pos_after)[0, y + dy]

        def write(start, size, b, value):
            agg[plane, start : start + size, width * b : width * (b + 1)] = value

        aggregate_row(slots, basis, near_feat, near_pos, pos[plane, y], write)
    value = jnp.dot(
        agg[...].reshape(planes * rows, basis * width), w[...], preferred_element_type=F32
    )
    value = jax.nn.silu(value).reshape(planes, rows, width)
    for plane in range(planes):
        out[y, plane] = feat[plane, y].astype(F32) + turn(value[plane], slots)


def short_call(kernel, name, lines, basis, args, base):
    planes, cols, rows, width = args[0].shape
    whole = pl.BlockSpec(memory_space=VMEM)
    aliases = {}
    if base is not None:
        aliases = {len(args): 0}
        args = (*args, base)
    return pl.pallas_call(
        kernel,
        in_specs=[whole] * len(args),
        out_specs=whole,
        out_shape=jax.ShapeDtypeStruct((cols, planes, rows, width), F32),
        scratch_shapes=[VMEM((lines, rows, basis * width), BF16)],
        input_output_aliases=aliases,
        compiler_params=pltpu.CompilerParams(vmem_limit_bytes=16 << 20),
        cost_estimate=pl.CostEstimate(
            flops=lines * rows * width * 8 * (basis * 384 + basis * width),
            bytes_accessed=4 << 20,
            transcendentals=lines * rows * 384 * (basis + 1),
        ),
        name=name,
    )(*args)


def field_kernel(ph, weighted, w_out, base, pos, out, rhs):
    tiles, width, _ = weighted.shape

    @pl.when(pl.program_id(0) == 0)
    def _():
        for t in range(tiles):
            rhs[t * KTILE : (t + 1) * KTILE, :] = weighted[t].T

    lhs = jnp.concatenate(
        [ph[t % 2, :, KTILE * (t // 2) : KTILE * (t // 2 + 1)] for t in range(tiles)], axis=1
    )
    recip = jnp.dot(lhs, rhs[...], preferred_element_type=F32)
    far = jnp.dot(recip.astype(BF16), w_out[...], preferred_element_type=F32)
    sub = lax.broadcasted_iota(jnp.int32, (POS_ROWS, width), 0)
    select = jnp.where(sub == OCC_ROW, 1.0, 0.0).astype(BF16)
    rows = base.shape[2]
    for y in range(base.shape[0]):
        occ = lax.dot_general(pos[0, y], select, TN, preferred_element_type=F32)
        value = base[y, 0] + far[rows * y : rows * (y + 1)]
        out[rows * y : rows * (y + 1), :] = jnp.where(occ > 0.0, value, 0.0).astype(BF16)


def field_call(ph, weighted, w_out, base, pos, group=2):
    _, atoms, vectors = ph.shape
    tiles, width, _ = weighted.shape
    cols, planes, rows, _ = base.shape
    tile = group * rows
    groups = cols // group
    return pl.pallas_call(
        field_kernel,
        grid=(atoms // tile,),
        in_specs=[
            pl.BlockSpec((2, tile, vectors), lambda i: (0, i, 0)),
            pl.BlockSpec((tiles, width, KTILE), lambda i: (0, 0, 0)),
            pl.BlockSpec((width, width), lambda i: (0, 0)),
            pl.BlockSpec((group, 1, rows, width), lambda i: (i % groups, i // groups, 0, 0)),
            pl.BlockSpec((1, group, POS_ROWS, rows), lambda i: (i // groups, i % groups, 0, 0)),
        ],
        out_specs=pl.BlockSpec((tile, width), lambda i: (i, 0)),
        out_shape=jax.ShapeDtypeStruct((atoms, width), BF16),
        scratch_shapes=[VMEM((tiles * KTILE, width), BF16)],
        compiler_params=pltpu.CompilerParams(
            dimension_semantics=("arbitrary",), vmem_limit_bytes=54 << 20
        ),
        cost_estimate=pl.CostEstimate(
            flops=4 * atoms * vectors * width, bytes_accessed=16 << 20, transcendentals=0
        ),
        name="field",
    )(ph, weighted, w_out, base, pos)


def my_index():
    return lax.axis_index("gx") * lax.axis_size("gy") + lax.axis_index("gy")


def swap(value, mask):
    count = lax.axis_size("gx") * lax.axis_size("gy")
    return lax.ppermute(value, AXES, [(i, i ^ mask) for i in range(count)])


def tied(*values):
    return lax.optimization_barrier(values)


def no_work():
    return ()


class Exchange:
    def __init__(self):
        size_y = lax.axis_size("gy")
        count = lax.axis_size("gx") * size_y
        bits = [1 << i for i in range(count.bit_length() - 1)]
        low = [b for b in bits if b < size_y]
        self.halved = low[:2]
        self.direct = low[2:4]
        self.whole = low[4:] + [b for b in bits if b >= size_y]
        self.masks = [0]
        for b in self.direct:
            self.masks = self.masks + [m ^ b for m in self.masks]

    def place(self):
        return sum(((my_index() // b) % 2) << k for k, b in enumerate(self.direct))

    def halve(self, value, bit, work=no_work):
        half = value.shape[0] // 2
        mine = (my_index() // bit) % 2
        keep = lax.dynamic_slice_in_dim(value, mine * half, half, 0)
        give = lax.dynamic_slice_in_dim(value, (1 - mine) * half, half, 0).astype(BF16)
        (got,), done = run_under([give], [bit], work)
        return keep + got.astype(F32), done

    def spread_sum(self, value, work):
        count = len(self.masks)
        value = value.reshape((count, -1) + value.shape[1:])
        me = self.place()
        keep = lax.dynamic_index_in_dim(value, me, 0, False)
        gives = [
            lax.dynamic_index_in_dim(value, me ^ j, 0, False).astype(BF16) for j in range(1, count)
        ]
        gives, done = run_under(gives, self.masks[1:], work)
        for got in gives:
            keep = keep + got.astype(F32)
        return keep, done

    def whole_sum(self, value, bit, work=no_work):
        (got,), done = run_under([value.astype(BF16)], [bit], work)
        return value + got.astype(F32), done

    def spread(self, value, work):
        count = len(self.masks)
        got, done = run_under([value] * (count - 1), self.masks[1:], work)
        parts = jnp.stack([value] + got)
        me = self.place()
        for k in range(len(self.direct)):
            b = 1 << k
            cut = parts.reshape((count // (2 * b), 2, b) + value.shape)
            parts = jnp.where((me >> k) & 1 == 0, cut, cut[:, ::-1]).reshape(parts.shape)
        return parts.reshape((-1,) + value.shape[1:]), done

    def double(self, value, bit, work=no_work):
        mine = (my_index() // bit) % 2
        (other,), done = run_under([value], [bit], work)
        return (
            jnp.where(
                mine == 0, jnp.concatenate([value, other]), jnp.concatenate([other, value])
            ),
            done,
        )


def run_under(gives, masks, work):
    inputs = work.inputs if work is not no_work else ()
    gives, inputs = tied(list(gives), inputs)
    got = [swap(give, mask) for give, mask in zip(gives, masks)]
    done = work(*inputs) if work is not no_work else ()
    return tied(got, done)


class Work:
    def __init__(self, call, *inputs):
        self.call = call
        self.inputs = inputs

    def __call__(self, *inputs):
        return self.call(*inputs)


def from_before(cells, axis, dim):
    count = lax.axis_size(axis)
    size = cells.shape[dim]
    tail = lax.slice_in_dim(cells, size - 1, size, axis=dim)
    return lax.ppermute(tail, axis, [(i, (i + 1) % count) for i in range(count)])


def from_after(cells, axis, dim):
    count = lax.axis_size(axis)
    head = lax.slice_in_dim(cells, 0, 1, axis=dim)
    return lax.ppermute(head, axis, [((i + 1) % count, i) for i in range(count)])


def edge_rows(feat_planes, pos_planes, y):
    parts = []
    for f, q in zip(feat_planes, pos_planes):
        q = jnp.pad(q[:, y : y + 1], ((0, 0), (0, 0), (0, 0), (0, f.shape[3] - q.shape[3])))
        parts.append(jnp.concatenate([f[:, y : y + 1], q], axis=2))
    return jnp.concatenate(parts, axis=0)


def on_device(features, fractions, counts, k_index, w_short, w_charge, w_out):
    planes, cols, depth, slots, width = features.shape
    basis = w_short.shape[0]
    vectors = k_index.shape[0]
    rows = depth * slots
    atoms = planes * cols * rows
    size_x, size_y = lax.axis_size("gx"), lax.axis_size("gy")
    grid_all = (planes * size_x, cols * size_y, depth)
    assert rows == 128 and slots == 8 and planes == 2 and cols == 8 and width == KTILE
    assert vectors % KTILE == 0
    for extent in grid_all:
        assert extent & (extent - 1) == 0 and extent <= 256
    scale_all = math.sqrt(vectors / (grid_all[0] * grid_all[1] * grid_all[2] * slots))

    feat = features.reshape(planes, cols, rows, width)
    before = from_before(feat, "gx", 0)

    occupied = (jnp.arange(slots, dtype=jnp.int32) < counts[..., None]).astype(BF16)
    frac = jnp.transpose(fractions, (0, 1, 4, 2, 3)).reshape(planes, cols, 3, rows)
    pos = jnp.concatenate(
        [
            frac,
            occupied.reshape(planes, cols, 1, rows),
            jnp.zeros((planes, cols, POS_ROWS - 4, rows), BF16),
        ],
        axis=2,
    )
    pos_before = from_before(pos, "gx", 0)
    pos_after = from_after(pos, "gx", 0)

    ph, partial = factor_call(
        pos, k_index.T, feat.reshape(atoms, width), w_charge, grid_all, scale_all
    )
    ph, partial, before, pos_before, pos_after = tied(ph, partial, before, pos_before, pos_after)
    after = from_after(feat, "gx", 0)

    w_flat = w_short.reshape(basis * width, width)
    exchange = Exchange()

    def plane_work(plane, first, count, base, *sides):
        kernel = functools.partial(plane_kernel, slots, basis, plane, first, count)
        call = lambda *args: short_call(
            kernel, "plane", count, basis, args[:5], args[5] if len(args) > 5 else None
        )
        inputs = (feat, pos, *sides, w_flat) + (() if base is None else (base,))
        return Work(call, *inputs)

    def edges(*args):
        feat, pos, before, pos_before, after, pos_after, low, high, w, base = args
        common = (feat, pos, before, pos_before, after, pos_after)
        for name, y, dy, halo in (("low", 0, -1, low), ("high", cols - 1, 1, high)):
            kernel = functools.partial(edge_kernel, slots, basis, y, dy)
            base = short_call(kernel, name, planes, basis, (*common, halo, w), base)
        return base

    value, _ = exchange.halve(partial, exchange.halved[0])
    value, base = exchange.halve(
        value, exchange.halved[1], plane_work(0, 1, 3, None, before, pos_before)
    )
    value, base = exchange.spread_sum(value, plane_work(0, 4, 3, base, before, pos_before))
    value, base, after = tied(value, base, after)
    feat_planes = (before, feat, after)
    pos_planes = (pos_before, pos, pos_after)
    low = from_before(edge_rows(feat_planes, pos_planes, cols - 1), "gy", 1)
    high = from_after(edge_rows(feat_planes, pos_planes, 0), "gy", 1)
    for i, bit in enumerate(exchange.whole):
        if i == 0:
            value, base = exchange.whole_sum(
                value, bit, plane_work(1, 1, 3, base, after, pos_after)
            )
        else:
            value, _ = exchange.whole_sum(value, bit)
    value = value.astype(BF16)
    value, base = exchange.spread(value, plane_work(1, 4, 3, base, after, pos_after))
    value, base = exchange.double(
        value,
        exchange.halved[1],
        Work(edges, feat, pos, before, pos_before, after, pos_after, low, high, w_flat, base),
    )
    value, _ = exchange.double(value, exchange.halved[0])
    weighted = value.reshape(2 * vectors // KTILE, width, KTILE)
    out = field_call(ph, weighted, w_out, base, pos)
    return out.reshape(features.shape)


def solution(mesh):
    return jax.shard_map(
        on_device,
        mesh=mesh,
        in_specs=(
            P("gx", "gy", None, None, None),
            P("gx", "gy", None, None, None),
            P("gx", "gy", None),
            P(),
            P(),
            P(),
            P(),
        ),
        out_specs=P("gx", "gy", None, None, None),
        check_vma=False,
    )
```

```python
import functools
import math

import jax
import jax.numpy as jnp
from jax import lax
from jax.experimental import pallas as pl
from jax.experimental.pallas import tpu as pltpu
from jax.sharding import PartitionSpec as P

TWO_PI = 2.0 * math.pi
SHARPNESS = 600.0
CENTER_LOW = 0.2
CENTER_SPAN = 0.5
SCREEN = 16.0
FAR = 8.0
BF16 = jnp.bfloat16
F32 = jnp.float32
AXES = ("gx", "gy")
KTILE = 256

HALF_COS = (
    1.4142134965644628,
    -6.978850988150233,
    5.739461168545313,
    -1.8835629713129327,
    0.3106981552009573,
)
HALF_SIN = (4.442867902918289, -7.307443416752583, 3.594788034903934, -0.7843739144750123)
NT = (((1,), (1,)), ((), ()))
TN = (((0,), (0,)), ((), ()))
TT = (((0,), (1,)), ((), ()))
OCC_ROW = 3
CELL_ROW = 4
POS_ROWS = 16
VMEM = pltpu.VMEM


def horner(coefs, s):
    value = coefs[-1] * s + coefs[-2]
    for c in coefs[-3::-1]:
        value = value * s + c
    return value


def factor_kernel(grid_all, scale_all, pos, kidx, feat, wc, ph_out, fac, ph, charges, where_at, sems):
    planes, cols, _, rows = pos.shape
    copies = []
    steps = ph.shape[0]
    atoms, width = feat.shape

    sub = lax.broadcasted_iota(jnp.int32, (POS_ROWS, KTILE), 0)
    kmat, screened = [], []
    for step in range(steps):
        value = jnp.zeros((POS_ROWS, KTILE), F32)
        k_sq = jnp.zeros((1, KTILE), F32)
        for d in range(3):
            k = kidx[d : d + 1, step * KTILE : (step + 1) * KTILE].astype(F32) * (1.0 / grid_all[d])
            hit = (sub == d) | (sub == CELL_ROW + d)
            value = jnp.where(hit, jnp.broadcast_to(k, value.shape), value)
            k_sq = k_sq + (TWO_PI * k) * (TWO_PI * k)
        kmat.append(value.astype(BF16))
        screened.append(jnp.exp(-k_sq / (4.0 * SCREEN)) / k_sq)
    total = sum(jnp.sum(part, axis=1, keepdims=True) for part in screened)

    sub = lax.broadcasted_iota(jnp.int32, (POS_ROWS, rows), 0)
    depth = (lax.broadcasted_iota(jnp.int32, (POS_ROWS, rows), 1) // 8).astype(F32)
    x0 = (lax.axis_index("gx") * planes).astype(F32)
    y0 = (lax.axis_index("gy") * cols).astype(F32)
    for x in range(planes):
        for y in range(cols):
            j = (x * cols + y) * rows
            tile = pos[x, y].astype(F32)
            tile = jnp.where(sub == CELL_ROW, x0 + float(x), tile)
            tile = jnp.where(sub == CELL_ROW + 1, y0 + float(y), tile)
            tile = jnp.where(sub == CELL_ROW + 2, depth, tile)
            where_at[j : j + rows, :] = tile.T.astype(BF16)
    turned = wc[...].T

    size = 2 * rows
    for step in range(steps + 1):
        sums = [None, None]
        for j in range(0, atoms, size):
            if step < steps:
                t_all = jnp.dot(
                    where_at[j : j + size, :], kmat[step], preferred_element_type=F32
                )
                for i in range(0, size, 16):
                    t = t_all[i : i + 16]
                    r = t - jnp.round(t)
                    s = r * r
                    half_c = horner(HALF_COS, s)
                    half_s = horner(HALF_SIN, s) * r
                    ph[step, 0, j + i : j + i + 16, :] = (1.0 - half_s * half_s).astype(BF16)
                    ph[step, 1, j + i : j + i + 16, :] = (half_s * half_c).astype(BF16)
            if step == 0:
                c = lax.dot_general(turned, feat[j : j + size, :], NT, preferred_element_type=F32)
                line = j // rows
                occ = [
                    pos[n // cols, n % cols, OCC_ROW : OCC_ROW + 1, :].astype(F32)
                    for n in range(line, line + 2)
                ]
                charges[:, j : j + size] = (c * jnp.concatenate(occ, axis=1)).astype(BF16)
            if step > 0:
                for p in range(2):
                    part = jnp.dot(
                        charges[:, j : j + size],
                        ph[step - 1, p, j : j + size, :],
                        preferred_element_type=F32,
                    )
                    sums[p] = part if sums[p] is None else sums[p] + part
        if step < steps:
            copy = pltpu.make_async_copy(ph.at[step], ph_out.at[step], sems.at[step])
            copy.start()
            copies.append(copy)
        if step > 0:
            weight = screened[step - 1] / total * scale_all
            for p in range(2):
                row = (2 * (step - 1) + p) * width
                fac[row : row + width, :] = sums[p] * weight
    for copy in copies:
        copy.wait()


def factor_call(pos, kidx, feat, wc, grid_all, scale_all):
    atoms, width = feat.shape
    vectors = kidx.shape[1]
    steps = vectors // KTILE
    whole = pl.BlockSpec(memory_space=VMEM)
    return pl.pallas_call(
        functools.partial(factor_kernel, grid_all, scale_all),
        in_specs=[whole] * 4,
        out_specs=[pl.BlockSpec(memory_space=pltpu.HBM), whole],
        out_shape=[
            pltpu.HBM((steps, 2, atoms, KTILE), BF16),
            jax.ShapeDtypeStruct((steps * 2 * width, KTILE), F32),
        ],
        scratch_shapes=[
            VMEM((steps, 2, atoms, KTILE), BF16),
            VMEM((width, atoms), BF16),
            VMEM((atoms, POS_ROWS), BF16),
            pltpu.SemaphoreType.DMA((steps,)),
        ],
        compiler_params=pltpu.CompilerParams(vmem_limit_bytes=24 << 20),
        cost_estimate=pl.CostEstimate(
            flops=24 * atoms * vectors * width, bytes_accessed=4 << 20, transcendentals=0
        ),
        name="factor",
    )(pos, kidx, feat, wc)


def aggregate_row(slots, basis, near_feat, near_pos, own_pos, write):
    rows = 128
    pairs = rows // (2 * slots)
    two = 2 * slots
    window = 4 * slots
    sub = lax.broadcasted_iota(jnp.int32, (8, 128), 0)
    lane = lax.broadcasted_iota(jnp.int32, (8, 128), 1)
    lane_block = lane // window
    cell_in_window = (lane % window) // slots
    z_off = jnp.where(sub == 2, (cell_in_window - 1).astype(F32), 0.0)
    columns = [(dx, dy) for dx in (-1, 0, 1) for dy in (-1, 0, 1) if (dx, dy) != (0, 0)]
    columns.append((0, 0))
    select = jnp.where(
        lax.broadcasted_iota(jnp.int32, (POS_ROWS, 384), 0)
        == lax.broadcasted_iota(jnp.int32, (POS_ROWS, 384), 1) // 128,
        1.0,
        0.0,
    ).astype(BF16)
    stretch = math.sqrt(SHARPNESS)
    centers = [stretch * (CENTER_LOW + b * (CENTER_SPAN / (basis - 1))) for b in range(basis)]

    placed = []
    for dx, dy in columns:
        coords = near_pos(dx, dy).astype(F32)[0:8]
        occ = jnp.broadcast_to(coords[OCC_ROW : OCC_ROW + 1, :], coords.shape)
        shift = jnp.where(sub == 0, float(dx), jnp.where(sub == 1, float(dy), 0.0))
        placed.append(jnp.where(occ > 0.0, coords + shift, FAR))
    own_all = lax.dot_general(own_pos, select, TN, preferred_element_type=F32)
    for p in range(pairs):
        packed = []
        for h in range(3):
            merged = None
            for c in range(4 * h, min(4 * h + 4, 9)):
                amount = (window * (c % 4) - two * p) % 128
                moved = pltpu.roll(placed[c], amount, axis=1) if amount else placed[c]
                merged = moved if merged is None else jnp.where(lane_block == c % 4, moved, merged)
            merged = merged + z_off
            if h == 2:
                merged = jnp.where(lane_block == 0, merged, FAR)
            packed.append([jnp.broadcast_to(merged[d : d + 1, :], (8, 128)) for d in range(3)])
        parts = [[None, None] for _ in range(3)]
        for h in range(3):
            for q in range(2):
                r0 = (two * p + slots * (1 + q)) % rows
                d2 = None
                for d in range(3):
                    mine = own_all[r0 : r0 + slots, 128 * d : 128 * d + 128]
                    if d == 2 and q == 1:
                        mine = mine + 1.0
                    delta = packed[h][d] - mine
                    d2 = delta * delta if d2 is None else d2 + delta * delta
                env = jnp.maximum(1.0 - d2, 0.0)
                env = env * env
                if h == 2:
                    env = jnp.where(lane == sub + slots * (1 + q), 0.0, env)
                ar = (d2 * stretch) * lax.rsqrt(jnp.maximum(d2, 1e-30))
                values = []
                for b in range(basis):
                    u = ar - centers[b]
                    values.append(jnp.exp(u * (centers[b] - ar)) * env)
                parts[h][q] = values
        lhs = []
        for h in range(3):
            lhs.append(
                jnp.concatenate(
                    [
                        jnp.concatenate([parts[h][0][b], parts[h][1][b]], axis=0).astype(BF16)
                        for b in range(basis)
                    ],
                    axis=0,
                )
            )
        near = []
        nxt = two * ((p + 1) % pairs)
        for dx, dy in columns:
            near.append(near_feat(dx, dy, two * p, two))
            near.append(near_feat(dx, dy, nxt, two))
        near.append(jnp.zeros((384 - 9 * window, near[0].shape[1]), BF16))
        total = jnp.dot(
            jnp.concatenate(lhs, axis=1),
            jnp.concatenate(near, axis=0),
            preferred_element_type=F32,
        ).astype(BF16)
        for b in range(basis):
            write(two * p, two, b, total[two * b : two * b + two])


def turn(value, slots):
    return jnp.concatenate([value[128 - slots :], value[: 128 - slots]], axis=0)


def plane_kernel(slots, basis, plane, first, count, feat, pos, side_feat, side_pos, w, *rest):
    out, agg = rest[-2:]
    planes, _, rows, width = feat.shape

    def pick(ref, side, dx):
        x = plane + dx
        return (ref, x) if 0 <= x < planes else (side, 0)

    def body(i, carry):
        y = first + i

        def near_feat(dx, dy, start, size):
            ref, x = pick(feat, side_feat, dx)
            return ref[x, y + dy, start : start + size, :]

        def near_pos(dx, dy):
            ref, x = pick(pos, side_pos, dx)
            return ref[x, y + dy]

        def write(start, size, b, value):
            agg[i, start : start + size, width * b : width * (b + 1)] = value

        aggregate_row(slots, basis, near_feat, near_pos, pos[plane, y], write)
        return carry

    lax.fori_loop(0, count, body, 0)
    value = jnp.dot(
        agg[...].reshape(count * rows, basis * width), w[...], preferred_element_type=F32
    )
    value = jax.nn.silu(value).reshape(count, rows, width)
    for i in range(count):
        out[first + i, plane] = feat[plane, first + i].astype(F32) + turn(value[i], slots)


def edge_kernel(
    slots, basis, y, halo_dy, feat, pos, before, pos_before, after, pos_after, halo, w, *rest
):
    out, agg = rest[-2:]
    planes, _, rows, width = feat.shape
    for plane in range(planes):

        def near_feat(dx, dy, start, size):
            x = plane + dx
            if dy == halo_dy:
                return halo[x + 1, 0, start : start + size, :]
            if 0 <= x < planes:
                return feat[x, y + dy, start : start + size, :]
            return (before if x < 0 else after)[0, y + dy, start : start + size, :]

        def near_pos(dx, dy):
            x = plane + dx
            if dy == halo_dy:
                return halo[x + 1, 0, rows : rows + POS_ROWS, 0:128]
            if 0 <= x < planes:
                return pos[x, y + dy]
            return (pos_before if x < 0 else pos_after)[0, y + dy]

        def write(start, size, b, value):
            agg[plane, start : start + size, width * b : width * (b + 1)] = value

        aggregate_row(slots, basis, near_feat, near_pos, pos[plane, y], write)
    value = jnp.dot(
        agg[...].reshape(planes * rows, basis * width), w[...], preferred_element_type=F32
    )
    value = jax.nn.silu(value).reshape(planes, rows, width)
    for plane in range(planes):
        out[y, plane] = feat[plane, y].astype(F32) + turn(value[plane], slots)


def short_call(kernel, name, lines, basis, args, base):
    planes, cols, rows, width = args[0].shape
    whole = pl.BlockSpec(memory_space=VMEM)
    aliases = {}
    if base is not None:
        aliases = {len(args): 0}
        args = (*args, base)
    return pl.pallas_call(
        kernel,
        in_specs=[whole] * len(args),
        out_specs=whole,
        out_shape=jax.ShapeDtypeStruct((cols, planes, rows, width), F32),
        scratch_shapes=[VMEM((lines, rows, basis * width), BF16)],
        input_output_aliases=aliases,
        compiler_params=pltpu.CompilerParams(vmem_limit_bytes=16 << 20),
        cost_estimate=pl.CostEstimate(
            flops=lines * rows * width * 8 * (basis * 384 + basis * width),
            bytes_accessed=4 << 20,
            transcendentals=lines * rows * 384 * (basis + 1),
        ),
        name=name,
    )(*args)


def field_kernel(ph_all, weighted, w_out, base, pos, out, ph, rhs, held, in_sems, out_sems):
    tiles, width, _ = weighted.shape
    cols, planes, rows, _ = base.shape
    count, size, _ = held.shape
    lines = size // rows
    loads = []
    for i in range(count):
        part = pl.ds(size * i, size)
        load = pltpu.make_async_copy(
            ph_all.at[:, :, part, :], ph.at[:, :, part, :], in_sems.at[i]
        )
        load.start()
        loads.append(load)
    for t in range(tiles):
        rhs[t * KTILE : (t + 1) * KTILE, :] = weighted[t].T
    sub = lax.broadcasted_iota(jnp.int32, (POS_ROWS, width), 0)
    select = jnp.where(sub == OCC_ROW, 1.0, 0.0).astype(BF16)
    stores = []
    for i in range(count):
        loads[i].wait()
        lhs = jnp.concatenate(
            [ph[t // 2, t % 2, size * i : size * (i + 1), :] for t in range(tiles)], axis=1
        )
        recip = jnp.dot(lhs, rhs[...], preferred_element_type=F32)
        far = jnp.dot(recip.astype(BF16), w_out[...], preferred_element_type=F32)
        for j in range(lines):
            x, y = divmod(lines * i + j, cols)
            occ = lax.dot_general(pos[x, y], select, TN, preferred_element_type=F32)
            value = base[y, x] + far[rows * j : rows * (j + 1)]
            held[i, rows * j : rows * (j + 1), :] = jnp.where(occ > 0.0, value, 0.0).astype(BF16)
        store = pltpu.make_async_copy(held.at[i], out.at[pl.ds(size * i, size), :], out_sems.at[i])
        store.start()
        stores.append(store)
    for store in stores:
        store.wait()


def field_call(ph, weighted, w_out, base, pos, lines=4):
    atoms = ph.shape[2]
    tiles, width, _ = weighted.shape
    cols, planes, rows, _ = base.shape
    count = planes * cols // lines
    whole = pl.BlockSpec(memory_space=VMEM)
    return pl.pallas_call(
        field_kernel,
        in_specs=[pl.BlockSpec(memory_space=pltpu.HBM)] + [whole] * 4,
        out_specs=pl.BlockSpec(memory_space=pltpu.HBM),
        out_shape=jax.ShapeDtypeStruct((atoms, width), BF16),
        scratch_shapes=[
            VMEM(ph.shape, BF16),
            VMEM((tiles * KTILE, width), BF16),
            VMEM((count, lines * rows, width), BF16),
            pltpu.SemaphoreType.DMA((count,)),
            pltpu.SemaphoreType.DMA((count,)),
        ],
        compiler_params=pltpu.CompilerParams(vmem_limit_bytes=24 << 20),
        cost_estimate=pl.CostEstimate(
            flops=2 * atoms * tiles * KTILE * width, bytes_accessed=4 << 20, transcendentals=0
        ),
        name="field",
    )(pltpu.with_memory_space_constraint(ph, pltpu.HBM), weighted, w_out, base, pos)


def my_index():
    return lax.axis_index("gx") * lax.axis_size("gy") + lax.axis_index("gy")


def swap(value, mask):
    count = lax.axis_size("gx") * lax.axis_size("gy")
    return lax.ppermute(value, AXES, [(i, i ^ mask) for i in range(count)])


def tied(*values):
    return lax.optimization_barrier(values)


def no_work():
    return ()


class Exchange:
    def __init__(self):
        size_y = lax.axis_size("gy")
        count = lax.axis_size("gx") * size_y
        bits = [1 << i for i in range(count.bit_length() - 1)]
        low = [b for b in bits if b < size_y]
        self.halved = low[:2]
        self.direct = low[2:4]
        self.whole = low[4:] + [b for b in bits if b >= size_y]
        self.masks = [0]
        for b in self.direct:
            self.masks = self.masks + [m ^ b for m in self.masks]

    def place(self):
        return sum(((my_index() // b) % 2) << k for k, b in enumerate(self.direct))

    def halve(self, value, bit, work=no_work):
        half = value.shape[0] // 2
        mine = (my_index() // bit) % 2
        keep = lax.dynamic_slice_in_dim(value, mine * half, half, 0)
        give = lax.dynamic_slice_in_dim(value, (1 - mine) * half, half, 0).astype(BF16)
        (got,), done = run_under([give], [bit], work)
        return keep + got.astype(F32), done

    def spread_sum(self, value, work):
        count = len(self.masks)
        value = value.reshape((count, -1) + value.shape[1:])
        me = self.place()
        keep = lax.dynamic_index_in_dim(value, me, 0, False)
        gives = [
            lax.dynamic_index_in_dim(value, me ^ j, 0, False).astype(BF16) for j in range(1, count)
        ]
        gives, done = run_under(gives, self.masks[1:], work)
        for got in gives:
            keep = keep + got.astype(F32)
        return keep, done

    def whole_sum(self, value, bit, work=no_work):
        (got,), done = run_under([value.astype(BF16)], [bit], work)
        return value + got.astype(F32), done

    def spread(self, value, work):
        count = len(self.masks)
        got, done = run_under([value] * (count - 1), self.masks[1:], work)
        parts = jnp.stack([value] + got)
        me = self.place()
        for k in range(len(self.direct)):
            b = 1 << k
            cut = parts.reshape((count // (2 * b), 2, b) + value.shape)
            parts = jnp.where((me >> k) & 1 == 0, cut, cut[:, ::-1]).reshape(parts.shape)
        return parts.reshape((-1,) + value.shape[1:]), done

    def double(self, value, bit, work=no_work):
        mine = (my_index() // bit) % 2
        (other,), done = run_under([value], [bit], work)
        return (
            jnp.where(
                mine == 0, jnp.concatenate([value, other]), jnp.concatenate([other, value])
            ),
            done,
        )


def run_under(gives, masks, work):
    inputs = work.inputs if work is not no_work else ()
    gives, inputs = tied(list(gives), inputs)
    got = [swap(give, mask) for give, mask in zip(gives, masks)]
    done = work(*inputs) if work is not no_work else ()
    return tied(got, done)


class Work:
    def __init__(self, call, *inputs):
        self.call = call
        self.inputs = inputs

    def __call__(self, *inputs):
        return self.call(*inputs)


def from_before(cells, axis, dim):
    count = lax.axis_size(axis)
    size = cells.shape[dim]
    tail = lax.slice_in_dim(cells, size - 1, size, axis=dim)
    return lax.ppermute(tail, axis, [(i, (i + 1) % count) for i in range(count)])


def from_after(cells, axis, dim):
    count = lax.axis_size(axis)
    head = lax.slice_in_dim(cells, 0, 1, axis=dim)
    return lax.ppermute(head, axis, [((i + 1) % count, i) for i in range(count)])


def edge_rows(feat_planes, pos_planes, y):
    parts = []
    for f, q in zip(feat_planes, pos_planes):
        q = jnp.pad(q[:, y : y + 1], ((0, 0), (0, 0), (0, 0), (0, f.shape[3] - q.shape[3])))
        parts.append(jnp.concatenate([f[:, y : y + 1], q], axis=2))
    return jnp.concatenate(parts, axis=0)


def on_device(features, fractions, counts, k_index, w_short, w_charge, w_out):
    planes, cols, depth, slots, width = features.shape
    basis = w_short.shape[0]
    vectors = k_index.shape[0]
    rows = depth * slots
    atoms = planes * cols * rows
    size_x, size_y = lax.axis_size("gx"), lax.axis_size("gy")
    grid_all = (planes * size_x, cols * size_y, depth)
    assert rows == 128 and slots == 8 and planes == 2 and cols == 8 and width == KTILE
    assert vectors % KTILE == 0
    for extent in grid_all:
        assert extent & (extent - 1) == 0 and extent <= 256
    scale_all = math.sqrt(vectors / (grid_all[0] * grid_all[1] * grid_all[2] * slots))

    feat = features.reshape(planes, cols, rows, width)
    before = from_before(feat, "gx", 0)

    occupied = (jnp.arange(slots, dtype=jnp.int32) < counts[..., None]).astype(BF16)
    frac = jnp.transpose(fractions, (0, 1, 4, 2, 3)).reshape(planes, cols, 3, rows)
    pos = jnp.concatenate(
        [
            frac,
            occupied.reshape(planes, cols, 1, rows),
            jnp.zeros((planes, cols, POS_ROWS - 4, rows), BF16),
        ],
        axis=2,
    )
    pos_before = from_before(pos, "gx", 0)
    pos_after = from_after(pos, "gx", 0)

    ph, partial = factor_call(
        pos, k_index.T, feat.reshape(atoms, width), w_charge, grid_all, scale_all
    )
    partial, before, pos_before, pos_after = tied(partial, before, pos_before, pos_after)
    after = from_after(feat, "gx", 0)

    w_flat = w_short.reshape(basis * width, width)
    exchange = Exchange()

    def plane_work(plane, first, count, base, *sides):
        kernel = functools.partial(plane_kernel, slots, basis, plane, first, count)
        call = lambda *args: short_call(
            kernel, "plane", count, basis, args[:5], args[5] if len(args) > 5 else None
        )
        inputs = (feat, pos, *sides, w_flat) + (() if base is None else (base,))
        return Work(call, *inputs)

    def edges(*args):
        feat, pos, before, pos_before, after, pos_after, low, high, w, base = args
        common = (feat, pos, before, pos_before, after, pos_after)
        for name, y, dy, halo in (("low", 0, -1, low), ("high", cols - 1, 1, high)):
            kernel = functools.partial(edge_kernel, slots, basis, y, dy)
            base = short_call(kernel, name, planes, basis, (*common, halo, w), base)
        return base

    value, _ = exchange.halve(partial, exchange.halved[0])
    value, base = exchange.halve(
        value, exchange.halved[1], plane_work(0, 1, 3, None, before, pos_before)
    )
    value, base = exchange.spread_sum(value, plane_work(0, 4, 3, base, before, pos_before))
    value, base, after = tied(value, base, after)
    feat_planes = (before, feat, after)
    pos_planes = (pos_before, pos, pos_after)
    low = from_before(edge_rows(feat_planes, pos_planes, cols - 1), "gy", 1)
    high = from_after(edge_rows(feat_planes, pos_planes, 0), "gy", 1)
    for i, bit in enumerate(exchange.whole):
        if i == 0:
            value, base = exchange.whole_sum(
                value, bit, plane_work(1, 1, 3, base, after, pos_after)
            )
        else:
            value, _ = exchange.whole_sum(value, bit)
    value = value.astype(BF16)
    value, base = exchange.spread(value, plane_work(1, 4, 3, base, after, pos_after))
    value, base = exchange.double(
        value,
        exchange.halved[1],
        Work(edges, feat, pos, before, pos_before, after, pos_after, low, high, w_flat, base),
    )
    value, _ = exchange.double(value, exchange.halved[0])
    weighted = value.reshape(2 * vectors // KTILE, width, KTILE)
    out = field_call(ph, weighted, w_out, base, pos)
    return out.reshape(features.shape)


def solution(mesh):
    return jax.shard_map(
        on_device,
        mesh=mesh,
        in_specs=(
            P("gx", "gy", None, None, None),
            P("gx", "gy", None, None, None),
            P("gx", "gy", None),
            P(),
            P(),
            P(),
            P(),
        ),
        out_specs=P("gx", "gy", None, None, None),
        check_vma=False,
    )
```

```python
import functools
import math

import jax
import jax.numpy as jnp
from jax import lax
from jax.experimental import pallas as pl
from jax.experimental.pallas import tpu as pltpu
from jax.sharding import PartitionSpec as P

TWO_PI = 2.0 * math.pi
SHARPNESS = 600.0
CENTER_LOW = 0.2
CENTER_SPAN = 0.5
SCREEN = 16.0
FAR = 8.0
BF16 = jnp.bfloat16
F32 = jnp.float32
AXES = ("gx", "gy")
KTILE = 256

HALF_COS = (
    1.4142134965644628,
    -6.978850988150233,
    5.739461168545313,
    -1.8835629713129327,
    0.3106981552009573,
)
HALF_SIN = (4.442867902918289, -7.307443416752583, 3.594788034903934, -0.7843739144750123)
NT = (((1,), (1,)), ((), ()))
TN = (((0,), (0,)), ((), ()))
TT = (((0,), (1,)), ((), ()))
OCC_ROW = 3
CELL_ROW = 4
POS_ROWS = 16
VMEM = pltpu.VMEM


def pinned(*values):
    return [pltpu.with_memory_space_constraint(value, VMEM) for value in values]


def horner(coefs, s):
    value = coefs[-1] * s + coefs[-2]
    for c in coefs[-3::-1]:
        value = value * s + c
    return value


def factor_kernel(grid_all, scale_all, pos, kidx, feat, wc, ph_out, fac, ph, charges, where_at, sems):
    planes, cols, _, rows = pos.shape
    copies = []
    steps = ph.shape[0]
    atoms, width = feat.shape

    sub = lax.broadcasted_iota(jnp.int32, (POS_ROWS, KTILE), 0)
    kmat, screened = [], []
    for step in range(steps):
        value = jnp.zeros((POS_ROWS, KTILE), F32)
        k_sq = jnp.zeros((1, KTILE), F32)
        for d in range(3):
            k = kidx[d : d + 1, step * KTILE : (step + 1) * KTILE].astype(F32) * (1.0 / grid_all[d])
            hit = (sub == d) | (sub == CELL_ROW + d)
            value = jnp.where(hit, jnp.broadcast_to(k, value.shape), value)
            k_sq = k_sq + (TWO_PI * k) * (TWO_PI * k)
        kmat.append(value.astype(BF16))
        screened.append(jnp.exp(-k_sq / (4.0 * SCREEN)) / k_sq)
    total = sum(jnp.sum(part, axis=1, keepdims=True) for part in screened)

    sub = lax.broadcasted_iota(jnp.int32, (POS_ROWS, rows), 0)
    depth = (lax.broadcasted_iota(jnp.int32, (POS_ROWS, rows), 1) // 8).astype(F32)
    x0 = (lax.axis_index("gx") * planes).astype(F32)
    y0 = (lax.axis_index("gy") * cols).astype(F32)
    for x in range(planes):
        for y in range(cols):
            j = (x * cols + y) * rows
            tile = pos[x, y].astype(F32)
            tile = jnp.where(sub == CELL_ROW, x0 + float(x), tile)
            tile = jnp.where(sub == CELL_ROW + 1, y0 + float(y), tile)
            tile = jnp.where(sub == CELL_ROW + 2, depth, tile)
            where_at[j : j + rows, :] = tile.T.astype(BF16)
    turned = wc[...].T

    size = 2 * rows
    for step in range(steps + 1):
        sums = [None, None]
        for j in range(0, atoms, size):
            if step < steps:
                t_all = jnp.dot(
                    where_at[j : j + size, :], kmat[step], preferred_element_type=F32
                )
                for i in range(0, size, 16):
                    t = t_all[i : i + 16]
                    r = t - jnp.round(t)
                    s = r * r
                    half_c = horner(HALF_COS, s)
                    half_s = horner(HALF_SIN, s) * r
                    ph[step, 0, j + i : j + i + 16, :] = (1.0 - half_s * half_s).astype(BF16)
                    ph[step, 1, j + i : j + i + 16, :] = (half_s * half_c).astype(BF16)
            if step == 0:
                c = lax.dot_general(turned, feat[j : j + size, :], NT, preferred_element_type=F32)
                line = j // rows
                occ = [
                    pos[n // cols, n % cols, OCC_ROW : OCC_ROW + 1, :].astype(F32)
                    for n in range(line, line + 2)
                ]
                charges[:, j : j + size] = (c * jnp.concatenate(occ, axis=1)).astype(BF16)
            if step > 0:
                for p in range(2):
                    part = jnp.dot(
                        charges[:, j : j + size],
                        ph[step - 1, p, j : j + size, :],
                        preferred_element_type=F32,
                    )
                    sums[p] = part if sums[p] is None else sums[p] + part
        if step < steps:
            copy = pltpu.make_async_copy(ph.at[step], ph_out.at[step], sems.at[step])
            copy.start()
            copies.append(copy)
        if step > 0:
            weight = screened[step - 1] / total * scale_all
            for p in range(2):
                row = (2 * (step - 1) + p) * width
                fac[row : row + width, :] = sums[p] * weight
    for copy in copies:
        copy.wait()


def factor_call(pos, kidx, feat, wc, grid_all, scale_all):
    atoms, width = feat.shape
    vectors = kidx.shape[1]
    steps = vectors // KTILE
    whole = pl.BlockSpec(memory_space=VMEM)
    return pl.pallas_call(
        functools.partial(factor_kernel, grid_all, scale_all),
        in_specs=[whole] * 4,
        out_specs=[pl.BlockSpec(memory_space=pltpu.HBM), whole],
        out_shape=[
            pltpu.HBM((steps, 2, atoms, KTILE), BF16),
            VMEM((steps * 2 * width, KTILE), F32),
        ],
        scratch_shapes=[
            VMEM((steps, 2, atoms, KTILE), BF16),
            VMEM((width, atoms), BF16),
            VMEM((atoms, POS_ROWS), BF16),
            pltpu.SemaphoreType.DMA((steps,)),
        ],
        compiler_params=pltpu.CompilerParams(vmem_limit_bytes=24 << 20),
        cost_estimate=pl.CostEstimate(
            flops=24 * atoms * vectors * width, bytes_accessed=4 << 20, transcendentals=0
        ),
        name="factor",
    )(*pinned(pos, kidx, feat, wc))


def aggregate_row(slots, basis, near_feat, near_pos, own_pos, write):
    rows = 128
    pairs = rows // (2 * slots)
    two = 2 * slots
    window = 4 * slots
    sub = lax.broadcasted_iota(jnp.int32, (8, 128), 0)
    lane = lax.broadcasted_iota(jnp.int32, (8, 128), 1)
    lane_block = lane // window
    cell_in_window = (lane % window) // slots
    z_off = jnp.where(sub == 2, (cell_in_window - 1).astype(F32), 0.0)
    columns = [(dx, dy) for dx in (-1, 0, 1) for dy in (-1, 0, 1) if (dx, dy) != (0, 0)]
    columns.append((0, 0))
    select = jnp.where(
        lax.broadcasted_iota(jnp.int32, (POS_ROWS, 384), 0)
        == lax.broadcasted_iota(jnp.int32, (POS_ROWS, 384), 1) // 128,
        1.0,
        0.0,
    ).astype(BF16)
    stretch = math.sqrt(SHARPNESS)
    centers = [stretch * (CENTER_LOW + b * (CENTER_SPAN / (basis - 1))) for b in range(basis)]

    placed = []
    for dx, dy in columns:
        coords = near_pos(dx, dy).astype(F32)[0:8]
        occ = jnp.broadcast_to(coords[OCC_ROW : OCC_ROW + 1, :], coords.shape)
        shift = jnp.where(sub == 0, float(dx), jnp.where(sub == 1, float(dy), 0.0))
        placed.append(jnp.where(occ > 0.0, coords + shift, FAR))
    own_all = lax.dot_general(own_pos, select, TN, preferred_element_type=F32)
    for p in range(pairs):
        packed = []
        for h in range(3):
            merged = None
            for c in range(4 * h, min(4 * h + 4, 9)):
                amount = (window * (c % 4) - two * p) % 128
                moved = pltpu.roll(placed[c], amount, axis=1) if amount else placed[c]
                merged = moved if merged is None else jnp.where(lane_block == c % 4, moved, merged)
            merged = merged + z_off
            if h == 2:
                merged = jnp.where(lane_block == 0, merged, FAR)
            packed.append([jnp.broadcast_to(merged[d : d + 1, :], (8, 128)) for d in range(3)])
        parts = [[None, None] for _ in range(3)]
        for h in range(3):
            for q in range(2):
                r0 = (two * p + slots * (1 + q)) % rows
                d2 = None
                for d in range(3):
                    mine = own_all[r0 : r0 + slots, 128 * d : 128 * d + 128]
                    if d == 2 and q == 1:
                        mine = mine + 1.0
                    delta = packed[h][d] - mine
                    d2 = delta * delta if d2 is None else d2 + delta * delta
                env = jnp.maximum(1.0 - d2, 0.0)
                env = env * env
                if h == 2:
                    env = jnp.where(lane == sub + slots * (1 + q), 0.0, env)
                ar = (d2 * stretch) * lax.rsqrt(jnp.maximum(d2, 1e-30))
                values = []
                for b in range(basis):
                    u = ar - centers[b]
                    values.append(jnp.exp(u * (centers[b] - ar)) * env)
                parts[h][q] = values
        lhs = []
        for h in range(3):
            lhs.append(
                jnp.concatenate(
                    [
                        jnp.concatenate([parts[h][0][b], parts[h][1][b]], axis=0).astype(BF16)
                        for b in range(basis)
                    ],
                    axis=0,
                )
            )
        near = []
        nxt = two * ((p + 1) % pairs)
        for dx, dy in columns:
            near.append(near_feat(dx, dy, two * p, two))
            near.append(near_feat(dx, dy, nxt, two))
        near.append(jnp.zeros((384 - 9 * window, near[0].shape[1]), BF16))
        total = jnp.dot(
            jnp.concatenate(lhs, axis=1),
            jnp.concatenate(near, axis=0),
            preferred_element_type=F32,
        ).astype(BF16)
        for b in range(basis):
            write(two * p, two, b, total[two * b : two * b + two])


def turn(value, slots):
    return jnp.concatenate([value[128 - slots :], value[: 128 - slots]], axis=0)


def plane_kernel(slots, basis, plane, first, count, feat, pos, side_feat, side_pos, w, *rest):
    out, agg = rest[-2:]
    planes, _, rows, width = feat.shape

    def pick(ref, side, dx):
        x = plane + dx
        return (ref, x) if 0 <= x < planes else (side, 0)

    def body(i, carry):
        y = first + i

        def near_feat(dx, dy, start, size):
            ref, x = pick(feat, side_feat, dx)
            return ref[x, y + dy, start : start + size, :]

        def near_pos(dx, dy):
            ref, x = pick(pos, side_pos, dx)
            return ref[x, y + dy]

        def write(start, size, b, value):
            agg[i, start : start + size, width * b : width * (b + 1)] = value

        aggregate_row(slots, basis, near_feat, near_pos, pos[plane, y], write)
        return carry

    lax.fori_loop(0, count, body, 0)
    value = jnp.dot(
        agg[...].reshape(count * rows, basis * width), w[...], preferred_element_type=F32
    )
    value = jax.nn.silu(value).reshape(count, rows, width)
    for i in range(count):
        out[first + i, plane] = feat[plane, first + i].astype(F32) + turn(value[i], slots)


def edge_kernel(
    slots, basis, y, halo_dy, feat, pos, before, pos_before, after, pos_after, halo, w, *rest
):
    out, agg = rest[-2:]
    planes, _, rows, width = feat.shape
    for plane in range(planes):

        def near_feat(dx, dy, start, size):
            x = plane + dx
            if dy == halo_dy:
                return halo[x + 1, 0, start : start + size, :]
            if 0 <= x < planes:
                return feat[x, y + dy, start : start + size, :]
            return (before if x < 0 else after)[0, y + dy, start : start + size, :]

        def near_pos(dx, dy):
            x = plane + dx
            if dy == halo_dy:
                return halo[x + 1, 0, rows : rows + POS_ROWS, 0:128]
            if 0 <= x < planes:
                return pos[x, y + dy]
            return (pos_before if x < 0 else pos_after)[0, y + dy]

        def write(start, size, b, value):
            agg[plane, start : start + size, width * b : width * (b + 1)] = value

        aggregate_row(slots, basis, near_feat, near_pos, pos[plane, y], write)
    value = jnp.dot(
        agg[...].reshape(planes * rows, basis * width), w[...], preferred_element_type=F32
    )
    value = jax.nn.silu(value).reshape(planes, rows, width)
    for plane in range(planes):
        out[y, plane] = feat[plane, y].astype(F32) + turn(value[plane], slots)


def short_call(kernel, name, lines, basis, args, base):
    planes, cols, rows, width = args[0].shape
    whole = pl.BlockSpec(memory_space=VMEM)
    aliases = {}
    if base is not None:
        aliases = {len(args): 0}
        args = (*args, base)
    return pl.pallas_call(
        kernel,
        in_specs=[whole] * len(args),
        out_specs=whole,
        out_shape=VMEM((cols, planes, rows, width), F32),
        scratch_shapes=[VMEM((lines, rows, basis * width), BF16)],
        input_output_aliases=aliases,
        compiler_params=pltpu.CompilerParams(vmem_limit_bytes=16 << 20),
        cost_estimate=pl.CostEstimate(
            flops=lines * rows * width * 8 * (basis * 384 + basis * width),
            bytes_accessed=4 << 20,
            transcendentals=lines * rows * 384 * (basis + 1),
        ),
        name=name,
    )(*pinned(*args))


def field_kernel(ph_all, weighted, w_out, base, pos, out, ph, rhs, held, in_sems, out_sems):
    tiles, width, _ = weighted.shape
    cols, planes, rows, _ = base.shape
    count, size, _ = held.shape
    lines = size // rows
    loads = []
    for i in range(count):
        part = pl.ds(size * i, size)
        load = pltpu.make_async_copy(
            ph_all.at[:, :, part, :], ph.at[:, :, part, :], in_sems.at[i]
        )
        load.start()
        loads.append(load)
    for t in range(tiles):
        rhs[t * KTILE : (t + 1) * KTILE, :] = weighted[t].T
    sub = lax.broadcasted_iota(jnp.int32, (POS_ROWS, width), 0)
    select = jnp.where(sub == OCC_ROW, 1.0, 0.0).astype(BF16)
    stores = []
    for i in range(count):
        loads[i].wait()
        lhs = jnp.concatenate(
            [ph[t // 2, t % 2, size * i : size * (i + 1), :] for t in range(tiles)], axis=1
        )
        recip = jnp.dot(lhs, rhs[...], preferred_element_type=F32)
        far = jnp.dot(recip.astype(BF16), w_out[...], preferred_element_type=F32)
        for j in range(lines):
            x, y = divmod(lines * i + j, cols)
            occ = lax.dot_general(pos[x, y], select, TN, preferred_element_type=F32)
            value = base[y, x] + far[rows * j : rows * (j + 1)]
            held[i, rows * j : rows * (j + 1), :] = jnp.where(occ > 0.0, value, 0.0).astype(BF16)
        store = pltpu.make_async_copy(held.at[i], out.at[pl.ds(size * i, size), :], out_sems.at[i])
        store.start()
        stores.append(store)
    for store in stores:
        store.wait()


def field_call(ph, weighted, w_out, base, pos, lines=4):
    atoms = ph.shape[2]
    tiles, width, _ = weighted.shape
    cols, planes, rows, _ = base.shape
    count = planes * cols // lines
    whole = pl.BlockSpec(memory_space=VMEM)
    return pl.pallas_call(
        field_kernel,
        in_specs=[pl.BlockSpec(memory_space=pltpu.HBM)] + [whole] * 4,
        out_specs=pl.BlockSpec(memory_space=pltpu.HBM),
        out_shape=jax.ShapeDtypeStruct((atoms, width), BF16),
        scratch_shapes=[
            VMEM(ph.shape, BF16),
            VMEM((tiles * KTILE, width), BF16),
            VMEM((count, lines * rows, width), BF16),
            pltpu.SemaphoreType.DMA((count,)),
            pltpu.SemaphoreType.DMA((count,)),
        ],
        compiler_params=pltpu.CompilerParams(vmem_limit_bytes=24 << 20),
        cost_estimate=pl.CostEstimate(
            flops=2 * atoms * tiles * KTILE * width, bytes_accessed=4 << 20, transcendentals=0
        ),
        name="field",
    )(pltpu.with_memory_space_constraint(ph, pltpu.HBM), *pinned(weighted, w_out, base, pos))


def my_index():
    return lax.axis_index("gx") * lax.axis_size("gy") + lax.axis_index("gy")


def swap(value, mask):
    count = lax.axis_size("gx") * lax.axis_size("gy")
    return lax.ppermute(value, AXES, [(i, i ^ mask) for i in range(count)])


def tied(*values):
    return lax.optimization_barrier(values)


def no_work():
    return ()


class Exchange:
    def __init__(self):
        size_y = lax.axis_size("gy")
        count = lax.axis_size("gx") * size_y
        bits = [1 << i for i in range(count.bit_length() - 1)]
        low = [b for b in bits if b < size_y]
        self.halved = low[:2]
        self.direct = low[2:4]
        self.whole = low[4:] + [b for b in bits if b >= size_y]
        self.masks = [0]
        for b in self.direct:
            self.masks = self.masks + [m ^ b for m in self.masks]

    def place(self):
        return sum(((my_index() // b) % 2) << k for k, b in enumerate(self.direct))

    def halve(self, value, bit, work=no_work):
        half = value.shape[0] // 2
        mine = (my_index() // bit) % 2
        keep = lax.dynamic_slice_in_dim(value, mine * half, half, 0)
        give = lax.dynamic_slice_in_dim(value, (1 - mine) * half, half, 0).astype(BF16)
        (got,), done = run_under([give], [bit], work)
        return keep + got.astype(F32), done

    def spread_sum(self, value, work):
        count = len(self.masks)
        value = value.reshape((count, -1) + value.shape[1:])
        me = self.place()
        keep = lax.dynamic_index_in_dim(value, me, 0, False)
        gives = [
            lax.dynamic_index_in_dim(value, me ^ j, 0, False).astype(BF16) for j in range(1, count)
        ]
        gives, done = run_under(gives, self.masks[1:], work)
        for got in gives:
            keep = keep + got.astype(F32)
        return keep, done

    def whole_sum(self, value, bit, work=no_work):
        (got,), done = run_under([value.astype(BF16)], [bit], work)
        return value + got.astype(F32), done

    def spread(self, value, work):
        count = len(self.masks)
        got, done = run_under([value] * (count - 1), self.masks[1:], work)
        parts = jnp.stack([value] + got)
        me = self.place()
        for k in range(len(self.direct)):
            b = 1 << k
            cut = parts.reshape((count // (2 * b), 2, b) + value.shape)
            parts = jnp.where((me >> k) & 1 == 0, cut, cut[:, ::-1]).reshape(parts.shape)
        return parts.reshape((-1,) + value.shape[1:]), done

    def double(self, value, bit, work=no_work):
        mine = (my_index() // bit) % 2
        (other,), done = run_under([value], [bit], work)
        return (
            jnp.where(
                mine == 0, jnp.concatenate([value, other]), jnp.concatenate([other, value])
            ),
            done,
        )


def run_under(gives, masks, work):
    inputs = work.inputs if work is not no_work else ()
    gives, inputs = tied(list(gives), inputs)
    got = [swap(give, mask) for give, mask in zip(gives, masks)]
    done = work(*inputs) if work is not no_work else ()
    return tied(got, done)


class Work:
    def __init__(self, call, *inputs):
        self.call = call
        self.inputs = inputs

    def __call__(self, *inputs):
        return self.call(*inputs)


def from_before(cells, axis, dim):
    count = lax.axis_size(axis)
    size = cells.shape[dim]
    tail = lax.slice_in_dim(cells, size - 1, size, axis=dim)
    return lax.ppermute(tail, axis, [(i, (i + 1) % count) for i in range(count)])


def from_after(cells, axis, dim):
    count = lax.axis_size(axis)
    head = lax.slice_in_dim(cells, 0, 1, axis=dim)
    return lax.ppermute(head, axis, [((i + 1) % count, i) for i in range(count)])


def edge_rows(feat_planes, pos_planes, y):
    parts = []
    for f, q in zip(feat_planes, pos_planes):
        q = jnp.pad(q[:, y : y + 1], ((0, 0), (0, 0), (0, 0), (0, f.shape[3] - q.shape[3])))
        parts.append(jnp.concatenate([f[:, y : y + 1], q], axis=2))
    return jnp.concatenate(parts, axis=0)


def on_device(features, fractions, counts, k_index, w_short, w_charge, w_out):
    planes, cols, depth, slots, width = features.shape
    basis = w_short.shape[0]
    vectors = k_index.shape[0]
    rows = depth * slots
    atoms = planes * cols * rows
    size_x, size_y = lax.axis_size("gx"), lax.axis_size("gy")
    grid_all = (planes * size_x, cols * size_y, depth)
    assert rows == 128 and slots == 8 and planes == 2 and cols == 8 and width == KTILE
    assert vectors % KTILE == 0
    for extent in grid_all:
        assert extent & (extent - 1) == 0 and extent <= 256
    scale_all = math.sqrt(vectors / (grid_all[0] * grid_all[1] * grid_all[2] * slots))

    feat = features.reshape(planes, cols, rows, width)
    before = from_before(feat, "gx", 0)

    occupied = (jnp.arange(slots, dtype=jnp.int32) < counts[..., None]).astype(BF16)
    frac = jnp.transpose(fractions, (0, 1, 4, 2, 3)).reshape(planes, cols, 3, rows)
    pos = jnp.concatenate(
        [
            frac,
            occupied.reshape(planes, cols, 1, rows),
            jnp.zeros((planes, cols, POS_ROWS - 4, rows), BF16),
        ],
        axis=2,
    )
    ph, partial = factor_call(
        pos, k_index.T, feat.reshape(atoms, width), w_charge, grid_all, scale_all
    )
    partial, before, head, pos_late = tied(partial, before, feat[:1], pos)
    after = from_after(head, "gx", 0)
    pos_before = from_before(pos_late, "gx", 0)
    pos_after = from_after(pos_late, "gx", 0)

    w_flat = w_short.reshape(basis * width, width)
    exchange = Exchange()

    def plane_work(plane, first, count, base, *sides):
        kernel = functools.partial(plane_kernel, slots, basis, plane, first, count)
        call = lambda *args: short_call(
            kernel, "plane", count, basis, args[:5], args[5] if len(args) > 5 else None
        )
        inputs = (feat, pos, *sides, w_flat) + (() if base is None else (base,))
        return Work(call, *inputs)

    def edges(*args):
        feat, pos, before, pos_before, after, pos_after, low, high, w, base = args
        common = (feat, pos, before, pos_before, after, pos_after)
        for name, y, dy, halo in (("low", 0, -1, low), ("high", cols - 1, 1, high)):
            kernel = functools.partial(edge_kernel, slots, basis, y, dy)
            base = short_call(kernel, name, planes, basis, (*common, halo, w), base)
        return base

    value, _ = exchange.halve(partial, exchange.halved[0])
    value, before, pos_before = tied(value, before, pos_before)
    value, base = exchange.halve(
        value, exchange.halved[1], plane_work(0, 1, 3, None, before, pos_before)
    )
    value, base = exchange.spread_sum(value, plane_work(0, 4, 3, base, before, pos_before))
    value, base, after, pos_after = tied(value, base, after, pos_after)
    feat_planes = (before, feat, after)
    pos_planes = (pos_before, pos, pos_after)
    low = from_before(edge_rows(feat_planes, pos_planes, cols - 1), "gy", 1)
    high = from_after(edge_rows(feat_planes, pos_planes, 0), "gy", 1)
    for i, bit in enumerate(exchange.whole):
        if i == 0:
            value, base = exchange.whole_sum(
                value, bit, plane_work(1, 1, 3, base, after, pos_after)
            )
        else:
            value, _ = exchange.whole_sum(value, bit)
    value = value.astype(BF16)
    value, base = exchange.spread(value, plane_work(1, 4, 3, base, after, pos_after))
    value, base = exchange.double(
        value,
        exchange.halved[1],
        Work(edges, feat, pos, before, pos_before, after, pos_after, low, high, w_flat, base),
    )
    value, _ = exchange.double(value, exchange.halved[0])
    weighted = value.reshape(2 * vectors // KTILE, width, KTILE)
    out = field_call(ph, weighted, w_out, base, pos)
    return out.reshape(features.shape)


def solution(mesh):
    return jax.shard_map(
        on_device,
        mesh=mesh,
        in_specs=(
            P("gx", "gy", None, None, None),
            P("gx", "gy", None, None, None),
            P("gx", "gy", None),
            P(),
            P(),
            P(),
            P(),
        ),
        out_specs=P("gx", "gy", None, None, None),
        check_vma=False,
    )
```

```python
import functools
import math

import jax
import jax.numpy as jnp
from jax import lax
from jax.experimental import pallas as pl
from jax.experimental.pallas import tpu as pltpu
from jax.sharding import PartitionSpec as P

TWO_PI = 2.0 * math.pi
SHARPNESS = 600.0
CENTER_LOW = 0.2
CENTER_SPAN = 0.5
SCREEN = 16.0
FAR = 8.0
BF16 = jnp.bfloat16
F32 = jnp.float32
AXES = ("gx", "gy")
KTILE = 256

HALF_COS = (
    1.4142134965644628,
    -6.978850988150233,
    5.739461168545313,
    -1.8835629713129327,
    0.3106981552009573,
)
HALF_SIN = (4.442867902918289, -7.307443416752583, 3.594788034903934, -0.7843739144750123)
NT = (((1,), (1,)), ((), ()))
TN = (((0,), (0,)), ((), ()))
TT = (((0,), (1,)), ((), ()))
OCC_ROW = 3
CELL_ROW = 4
POS_ROWS = 16
VMEM = pltpu.VMEM


def pinned(*values):
    return [pltpu.with_memory_space_constraint(value, VMEM) for value in values]


def horner(coefs, s):
    value = coefs[-1] * s + coefs[-2]
    for c in coefs[-3::-1]:
        value = value * s + c
    return value


def factor_kernel(grid_all, scale_all, pos, kidx, feat, wc, ph_out, fac, head_out, ph, head, charges, where_at, sems):
    planes, cols, _, rows = pos.shape
    steps = ph.shape[0]
    atoms, width = feat.shape

    sub = lax.broadcasted_iota(jnp.int32, (POS_ROWS, KTILE), 0)
    kmat, screened = [], []
    for step in range(steps):
        value = jnp.zeros((POS_ROWS, KTILE), F32)
        k_sq = jnp.zeros((1, KTILE), F32)
        for d in range(3):
            k = kidx[d : d + 1, step * KTILE : (step + 1) * KTILE].astype(F32) * (1.0 / grid_all[d])
            hit = (sub == d) | (sub == CELL_ROW + d)
            value = jnp.where(hit, jnp.broadcast_to(k, value.shape), value)
            k_sq = k_sq + (TWO_PI * k) * (TWO_PI * k)
        kmat.append(value.astype(BF16))
        screened.append(jnp.exp(-k_sq / (4.0 * SCREEN)) / k_sq)
    total = sum(jnp.sum(part, axis=1, keepdims=True) for part in screened)

    sub = lax.broadcasted_iota(jnp.int32, (POS_ROWS, rows), 0)
    depth = (lax.broadcasted_iota(jnp.int32, (POS_ROWS, rows), 1) // 8).astype(F32)
    x0 = (lax.axis_index("gx") * planes).astype(F32)
    y0 = (lax.axis_index("gy") * cols).astype(F32)
    for x in range(planes):
        for y in range(cols):
            j = (x * cols + y) * rows
            tile = pos[x, y].astype(F32)
            tile = jnp.where(sub == CELL_ROW, x0 + float(x), tile)
            tile = jnp.where(sub == CELL_ROW + 1, y0 + float(y), tile)
            tile = jnp.where(sub == CELL_ROW + 2, depth, tile)
            where_at[j : j + rows, :] = tile.T.astype(BF16)
    for y in range(cols):
        head[0, y, 0:rows, :] = feat[y * rows : (y + 1) * rows, :]
        head[0, y, rows : rows + POS_ROWS, 0:rows] = pos[0, y]
        head[0, y, rows : rows + POS_ROWS, rows:width] = pos[0, y]
    copies = [pltpu.make_async_copy(head, head_out, sems.at[steps])]
    copies[0].start()
    turned = wc[...].T

    size = 2 * rows
    for step in range(steps + 1):
        sums = [None, None]
        for j in range(0, atoms, size):
            if step < steps:
                t_all = jnp.dot(
                    where_at[j : j + size, :], kmat[step], preferred_element_type=F32
                )
                for i in range(0, size, 16):
                    t = t_all[i : i + 16]
                    r = t - jnp.round(t)
                    s = r * r
                    half_c = horner(HALF_COS, s)
                    half_s = horner(HALF_SIN, s) * r
                    ph[step, 0, j + i : j + i + 16, :] = (1.0 - half_s * half_s).astype(BF16)
                    ph[step, 1, j + i : j + i + 16, :] = (half_s * half_c).astype(BF16)
            if step == 0:
                c = lax.dot_general(turned, feat[j : j + size, :], NT, preferred_element_type=F32)
                line = j // rows
                occ = [
                    pos[n // cols, n % cols, OCC_ROW : OCC_ROW + 1, :].astype(F32)
                    for n in range(line, line + 2)
                ]
                charges[:, j : j + size] = (c * jnp.concatenate(occ, axis=1)).astype(BF16)
            if step > 0:
                for p in range(2):
                    part = jnp.dot(
                        charges[:, j : j + size],
                        ph[step - 1, p, j : j + size, :],
                        preferred_element_type=F32,
                    )
                    sums[p] = part if sums[p] is None else sums[p] + part
        if step < steps:
            copy = pltpu.make_async_copy(ph.at[step], ph_out.at[step], sems.at[step])
            copy.start()
            copies.append(copy)
        if step > 0:
            weight = screened[step - 1] / total * scale_all
            for p in range(2):
                row = (2 * (step - 1) + p) * width
                fac[row : row + width, :] = sums[p] * weight
    for copy in copies:
        copy.wait()


def factor_call(pos, kidx, feat, wc, grid_all, scale_all):
    atoms, width = feat.shape
    _, cols, _, rows = pos.shape
    vectors = kidx.shape[1]
    steps = vectors // KTILE
    whole = pl.BlockSpec(memory_space=VMEM)
    in_hbm = pl.BlockSpec(memory_space=pltpu.HBM)
    phases = (steps, 2, atoms, KTILE)
    head = (1, cols, rows + POS_ROWS, width)
    return pl.pallas_call(
        functools.partial(factor_kernel, grid_all, scale_all),
        in_specs=[whole] * 4,
        out_specs=[in_hbm, whole, in_hbm],
        out_shape=[
            pltpu.HBM(phases, BF16),
            VMEM((steps * 2 * width, KTILE), F32),
            pltpu.HBM(head, BF16),
        ],
        scratch_shapes=[
            VMEM(phases, BF16),
            VMEM(head, BF16),
            VMEM((width, atoms), BF16),
            VMEM((atoms, POS_ROWS), BF16),
            pltpu.SemaphoreType.DMA((steps + 1,)),
        ],
        compiler_params=pltpu.CompilerParams(vmem_limit_bytes=24 << 20),
        cost_estimate=pl.CostEstimate(
            flops=24 * atoms * vectors * width, bytes_accessed=4 << 20, transcendentals=0
        ),
        name="factor",
    )(*pinned(pos, kidx, feat, wc))


def aggregate_row(slots, basis, near_feat, near_pos, own_pos, write):
    rows = 128
    pairs = rows // (2 * slots)
    two = 2 * slots
    window = 4 * slots
    sub = lax.broadcasted_iota(jnp.int32, (8, 128), 0)
    lane = lax.broadcasted_iota(jnp.int32, (8, 128), 1)
    lane_block = lane // window
    cell_in_window = (lane % window) // slots
    z_off = jnp.where(sub == 2, (cell_in_window - 1).astype(F32), 0.0)
    columns = [(dx, dy) for dx in (-1, 0, 1) for dy in (-1, 0, 1) if (dx, dy) != (0, 0)]
    columns.append((0, 0))
    select = jnp.where(
        lax.broadcasted_iota(jnp.int32, (POS_ROWS, 384), 0)
        == lax.broadcasted_iota(jnp.int32, (POS_ROWS, 384), 1) // 128,
        1.0,
        0.0,
    ).astype(BF16)
    stretch = math.sqrt(SHARPNESS)
    centers = [stretch * (CENTER_LOW + b * (CENTER_SPAN / (basis - 1))) for b in range(basis)]

    placed = []
    for dx, dy in columns:
        coords = near_pos(dx, dy).astype(F32)[0:8]
        occ = jnp.broadcast_to(coords[OCC_ROW : OCC_ROW + 1, :], coords.shape)
        shift = jnp.where(sub == 0, float(dx), jnp.where(sub == 1, float(dy), 0.0))
        placed.append(jnp.where(occ > 0.0, coords + shift, FAR))
    own_all = lax.dot_general(own_pos, select, TN, preferred_element_type=F32)
    for p in range(pairs):
        packed = []
        for h in range(3):
            merged = None
            for c in range(4 * h, min(4 * h + 4, 9)):
                amount = (window * (c % 4) - two * p) % 128
                moved = pltpu.roll(placed[c], amount, axis=1) if amount else placed[c]
                merged = moved if merged is None else jnp.where(lane_block == c % 4, moved, merged)
            merged = merged + z_off
            if h == 2:
                merged = jnp.where(lane_block == 0, merged, FAR)
            packed.append([jnp.broadcast_to(merged[d : d + 1, :], (8, 128)) for d in range(3)])
        parts = [[None, None] for _ in range(3)]
        for h in range(3):
            for q in range(2):
                r0 = (two * p + slots * (1 + q)) % rows
                d2 = None
                for d in range(3):
                    mine = own_all[r0 : r0 + slots, 128 * d : 128 * d + 128]
                    if d == 2 and q == 1:
                        mine = mine + 1.0
                    delta = packed[h][d] - mine
                    d2 = delta * delta if d2 is None else d2 + delta * delta
                env = jnp.maximum(1.0 - d2, 0.0)
                env = env * env
                if h == 2:
                    env = jnp.where(lane == sub + slots * (1 + q), 0.0, env)
                ar = (d2 * stretch) * lax.rsqrt(jnp.maximum(d2, 1e-30))
                values = []
                for b in range(basis):
                    u = ar - centers[b]
                    values.append(jnp.exp(u * (centers[b] - ar)) * env)
                parts[h][q] = values
        lhs = []
        for h in range(3):
            lhs.append(
                jnp.concatenate(
                    [
                        jnp.concatenate([parts[h][0][b], parts[h][1][b]], axis=0).astype(BF16)
                        for b in range(basis)
                    ],
                    axis=0,
                )
            )
        near = []
        nxt = two * ((p + 1) % pairs)
        for dx, dy in columns:
            near.append(near_feat(dx, dy, two * p, two))
            near.append(near_feat(dx, dy, nxt, two))
        near.append(jnp.zeros((384 - 9 * window, near[0].shape[1]), BF16))
        total = jnp.dot(
            jnp.concatenate(lhs, axis=1),
            jnp.concatenate(near, axis=0),
            preferred_element_type=F32,
        ).astype(BF16)
        for b in range(basis):
            write(two * p, two, b, total[two * b : two * b + two])


def turn(value, slots):
    return jnp.concatenate([value[128 - slots :], value[: 128 - slots]], axis=0)


def plane_kernel(slots, basis, plane, first, count, fetch, feat, pos, w, *rest):
    planes, _, rows, width = feat.shape
    sides = list(rest[: 2 if plane == 0 else 1])
    if fetch:
        out, held, agg, sem = rest[-4:]
        copy = pltpu.make_async_copy(sides[0], held, sem)
        copy.start()
        copy.wait()
        sides[0] = held
    else:
        out, agg = rest[-2:]

    def body(i, carry):
        y = first + i

        def near_feat(dx, dy, start, size):
            x = plane + dx
            if 0 <= x < planes:
                return feat[x, y + dy, start : start + size, :]
            return sides[0][0, y + dy, start : start + size, :]

        def near_pos(dx, dy):
            x = plane + dx
            if 0 <= x < planes:
                return pos[x, y + dy]
            if x < 0:
                return sides[1][0, y + dy]
            return sides[0][0, y + dy, rows : rows + POS_ROWS, 0:rows]

        def write(start, size, b, value):
            agg[i, start : start + size, width * b : width * (b + 1)] = value

        aggregate_row(slots, basis, near_feat, near_pos, pos[plane, y], write)
        return carry

    lax.fori_loop(0, count, body, 0)
    value = jnp.dot(
        agg[...].reshape(count * rows, basis * width), w[...], preferred_element_type=F32
    )
    value = jax.nn.silu(value).reshape(count, rows, width)
    for i in range(count):
        out[first + i, plane] = feat[plane, first + i].astype(F32) + turn(value[i], slots)


def edge_kernel(
    slots, basis, y, halo_dy, feat, pos, w, before, pos_before, after, halo, *rest
):
    out, agg = rest[-2:]
    planes, _, rows, width = feat.shape
    for plane in range(planes):

        def near_feat(dx, dy, start, size):
            x = plane + dx
            if dy == halo_dy:
                return halo[x + 1, 0, start : start + size, :]
            if 0 <= x < planes:
                return feat[x, y + dy, start : start + size, :]
            return (before if x < 0 else after)[0, y + dy, start : start + size, :]

        def near_pos(dx, dy):
            x = plane + dx
            if dy == halo_dy:
                return halo[x + 1, 0, rows : rows + POS_ROWS, 0:128]
            if 0 <= x < planes:
                return pos[x, y + dy]
            if x < 0:
                return pos_before[0, y + dy]
            return after[0, y + dy, rows : rows + POS_ROWS, 0:rows]

        def write(start, size, b, value):
            agg[plane, start : start + size, width * b : width * (b + 1)] = value

        aggregate_row(slots, basis, near_feat, near_pos, pos[plane, y], write)
    value = jnp.dot(
        agg[...].reshape(planes * rows, basis * width), w[...], preferred_element_type=F32
    )
    value = jax.nn.silu(value).reshape(planes, rows, width)
    for plane in range(planes):
        out[y, plane] = feat[plane, y].astype(F32) + turn(value[plane], slots)


def short_call(kernel, name, lines, basis, args, base, fetch=None):
    planes, cols, rows, width = args[0].shape
    whole = pl.BlockSpec(memory_space=VMEM)
    in_specs = [whole] * len(args)
    operands = pinned(*args)
    out_specs = [whole]
    out_shape = [VMEM((cols, planes, rows, width), F32)]
    scratch = [VMEM((lines, rows, basis * width), BF16)]
    aliases = {}
    if fetch is not None:
        in_specs[fetch] = pl.BlockSpec(memory_space=pltpu.HBM)
        operands[fetch] = pltpu.with_memory_space_constraint(args[fetch], pltpu.HBM)
        out_specs.append(whole)
        out_shape.append(VMEM(args[fetch].shape, BF16))
        scratch.append(pltpu.SemaphoreType.DMA)
    if base is not None:
        aliases = {len(args): 0}
        in_specs.append(whole)
        operands += pinned(base)
    return pl.pallas_call(
        kernel,
        in_specs=in_specs,
        out_specs=out_specs,
        out_shape=out_shape,
        scratch_shapes=scratch,
        input_output_aliases=aliases,
        compiler_params=pltpu.CompilerParams(vmem_limit_bytes=16 << 20),
        cost_estimate=pl.CostEstimate(
            flops=lines * rows * width * 8 * (basis * 384 + basis * width),
            bytes_accessed=4 << 20,
            transcendentals=lines * rows * 384 * (basis + 1),
        ),
        name=name,
    )(*operands)


def field_kernel(ph_all, weighted, w_out, base, pos, out, ph, rhs, held, in_sems, out_sems):
    tiles, width, _ = weighted.shape
    cols, planes, rows, _ = base.shape
    count, size, _ = held.shape
    lines = size // rows
    loads = []
    for i in range(count):
        part = pl.ds(size * i, size)
        load = pltpu.make_async_copy(
            ph_all.at[:, :, part, :], ph.at[:, :, part, :], in_sems.at[i]
        )
        load.start()
        loads.append(load)
    for t in range(tiles):
        rhs[t * KTILE : (t + 1) * KTILE, :] = weighted[t].T
    sub = lax.broadcasted_iota(jnp.int32, (POS_ROWS, width), 0)
    select = jnp.where(sub == OCC_ROW, 1.0, 0.0).astype(BF16)
    stores = []
    for i in range(count):
        loads[i].wait()
        lhs = jnp.concatenate(
            [ph[t // 2, t % 2, size * i : size * (i + 1), :] for t in range(tiles)], axis=1
        )
        recip = jnp.dot(lhs, rhs[...], preferred_element_type=F32)
        far = jnp.dot(recip.astype(BF16), w_out[...], preferred_element_type=F32)
        for j in range(lines):
            x, y = divmod(lines * i + j, cols)
            occ = lax.dot_general(pos[x, y], select, TN, preferred_element_type=F32)
            value = base[y, x] + far[rows * j : rows * (j + 1)]
            held[i, rows * j : rows * (j + 1), :] = jnp.where(occ > 0.0, value, 0.0).astype(BF16)
        store = pltpu.make_async_copy(held.at[i], out.at[pl.ds(size * i, size), :], out_sems.at[i])
        store.start()
        stores.append(store)
    for store in stores:
        store.wait()


def field_call(ph, weighted, w_out, base, pos, lines=4):
    atoms = ph.shape[2]
    tiles, width, _ = weighted.shape
    cols, planes, rows, _ = base.shape
    count = planes * cols // lines
    whole = pl.BlockSpec(memory_space=VMEM)
    return pl.pallas_call(
        field_kernel,
        in_specs=[pl.BlockSpec(memory_space=pltpu.HBM)] + [whole] * 4,
        out_specs=pl.BlockSpec(memory_space=pltpu.HBM),
        out_shape=jax.ShapeDtypeStruct((atoms, width), BF16),
        scratch_shapes=[
            VMEM(ph.shape, BF16),
            VMEM((tiles * KTILE, width), BF16),
            VMEM((count, lines * rows, width), BF16),
            pltpu.SemaphoreType.DMA((count,)),
            pltpu.SemaphoreType.DMA((count,)),
        ],
        compiler_params=pltpu.CompilerParams(vmem_limit_bytes=24 << 20),
        cost_estimate=pl.CostEstimate(
            flops=2 * atoms * tiles * KTILE * width, bytes_accessed=4 << 20, transcendentals=0
        ),
        name="field",
    )(pltpu.with_memory_space_constraint(ph, pltpu.HBM), *pinned(weighted, w_out, base, pos))


def my_index():
    return lax.axis_index("gx") * lax.axis_size("gy") + lax.axis_index("gy")


def swap(value, mask):
    count = lax.axis_size("gx") * lax.axis_size("gy")
    return lax.ppermute(value, AXES, [(i, i ^ mask) for i in range(count)])


def tied(*values):
    return lax.optimization_barrier(values)


def no_work():
    return ()


class Exchange:
    def __init__(self):
        size_y = lax.axis_size("gy")
        count = lax.axis_size("gx") * size_y
        bits = [1 << i for i in range(count.bit_length() - 1)]
        low = [b for b in bits if b < size_y]
        self.halved = low[:2]
        self.direct = low[2:4]
        self.whole = low[4:] + [b for b in bits if b >= size_y]
        self.masks = [0]
        for b in self.direct:
            self.masks = self.masks + [m ^ b for m in self.masks]

    def place(self):
        return sum(((my_index() // b) % 2) << k for k, b in enumerate(self.direct))

    def halve(self, value, bit, work=no_work):
        half = value.shape[0] // 2
        mine = (my_index() // bit) % 2
        keep = lax.dynamic_slice_in_dim(value, mine * half, half, 0)
        give = lax.dynamic_slice_in_dim(value, (1 - mine) * half, half, 0).astype(BF16)
        (got,), done = run_under([give], [bit], work)
        return keep + got.astype(F32), done

    def spread_sum(self, value, work):
        count = len(self.masks)
        value = value.reshape((count, -1) + value.shape[1:])
        me = self.place()
        keep = lax.dynamic_index_in_dim(value, me, 0, False)
        gives = [
            lax.dynamic_index_in_dim(value, me ^ j, 0, False).astype(BF16) for j in range(1, count)
        ]
        gives, done = run_under(gives, self.masks[1:], work)
        for got in gives:
            keep = keep + got.astype(F32)
        return keep, done

    def whole_sum(self, value, bit, work=no_work):
        (got,), done = run_under([value.astype(BF16)], [bit], work)
        return value + got.astype(F32), done

    def spread(self, value, work):
        count = len(self.masks)
        got, done = run_under([value] * (count - 1), self.masks[1:], work)
        parts = jnp.stack([value] + got)
        me = self.place()
        for k in range(len(self.direct)):
            b = 1 << k
            cut = parts.reshape((count // (2 * b), 2, b) + value.shape)
            parts = jnp.where((me >> k) & 1 == 0, cut, cut[:, ::-1]).reshape(parts.shape)
        return parts.reshape((-1,) + value.shape[1:]), done

    def double(self, value, bit, work=no_work):
        mine = (my_index() // bit) % 2
        (other,), done = run_under([value], [bit], work)
        return (
            jnp.where(
                mine == 0, jnp.concatenate([value, other]), jnp.concatenate([other, value])
            ),
            done,
        )


def run_under(gives, masks, work):
    inputs = work.inputs if work is not no_work else ()
    gives, inputs = tied(list(gives), inputs)
    got = [swap(give, mask) for give, mask in zip(gives, masks)]
    done = work(*inputs) if work is not no_work else ()
    return tied(got, done)


class Work:
    def __init__(self, call, *inputs):
        self.call = call
        self.inputs = inputs

    def __call__(self, *inputs):
        return self.call(*inputs)


def from_before(cells, axis, dim):
    count = lax.axis_size(axis)
    size = cells.shape[dim]
    tail = lax.slice_in_dim(cells, size - 1, size, axis=dim)
    return lax.ppermute(tail, axis, [(i, (i + 1) % count) for i in range(count)])


def from_after(cells, axis, dim):
    count = lax.axis_size(axis)
    head = lax.slice_in_dim(cells, 0, 1, axis=dim)
    return lax.ppermute(head, axis, [((i + 1) % count, i) for i in range(count)])


def edge_rows(feat, pos, before, pos_before, after, y):
    parts = []
    for f, q in ((before, pos_before), (feat, pos)):
        q = jnp.pad(q[:, y : y + 1], ((0, 0), (0, 0), (0, 0), (0, f.shape[3] - q.shape[3])))
        parts.append(jnp.concatenate([f[:, y : y + 1], q], axis=2))
    return jnp.concatenate(parts + [after[:, y : y + 1]], axis=0)


def on_device(features, fractions, counts, k_index, w_short, w_charge, w_out):
    planes, cols, depth, slots, width = features.shape
    basis = w_short.shape[0]
    vectors = k_index.shape[0]
    rows = depth * slots
    atoms = planes * cols * rows
    size_x, size_y = lax.axis_size("gx"), lax.axis_size("gy")
    grid_all = (planes * size_x, cols * size_y, depth)
    assert rows == 128 and slots == 8 and planes == 2 and cols == 8 and width == KTILE
    assert vectors % KTILE == 0
    for extent in grid_all:
        assert extent & (extent - 1) == 0 and extent <= 256
    scale_all = math.sqrt(vectors / (grid_all[0] * grid_all[1] * grid_all[2] * slots))

    feat = features.reshape(planes, cols, rows, width)
    before = from_before(feat, "gx", 0)

    occupied = (jnp.arange(slots, dtype=jnp.int32) < counts[..., None]).astype(BF16)
    frac = jnp.transpose(fractions, (0, 1, 4, 2, 3)).reshape(planes, cols, 3, rows)
    pos = jnp.concatenate(
        [
            frac,
            occupied.reshape(planes, cols, 1, rows),
            jnp.zeros((planes, cols, POS_ROWS - 4, rows), BF16),
        ],
        axis=2,
    )
    ph, partial, head = factor_call(
        pos, k_index.T, feat.reshape(atoms, width), w_charge, grid_all, scale_all
    )
    partial, before, pos_late = tied(partial, before, pos)
    after = from_after(head, "gx", 0)
    pos_before = from_before(pos_late, "gx", 0)

    w_flat = w_short.reshape(basis * width, width)
    exchange = Exchange()

    own = (feat, pos, w_flat)

    def plane_work(plane, first, count, fetch, base, *sides):
        kernel = functools.partial(plane_kernel, slots, basis, plane, first, count, fetch)

        def call(*args):
            split = len(own) + len(sides)
            return short_call(
                kernel,
                "plane",
                count,
                basis,
                args[:split],
                args[split] if args[split:] else None,
                len(own) if fetch else None,
            )

        return Work(call, *own, *sides, *(() if base is None else (base,)))

    def edges(*args):
        *common, low, high, base = args
        for name, y, dy, halo in (("low", 0, -1, low), ("high", cols - 1, 1, high)):
            kernel = functools.partial(edge_kernel, slots, basis, y, dy)
            (base,) = short_call(kernel, name, planes, basis, (*common, halo), base)
        return base

    value, _ = exchange.halve(partial, exchange.halved[0])
    value, before, pos_before = tied(value, before, pos_before)
    value, (base, before_held) = exchange.halve(
        value, exchange.halved[1], plane_work(0, 1, 3, True, None, before, pos_before)
    )
    value, (base,) = exchange.spread_sum(
        value, plane_work(0, 4, 3, False, base, before_held, pos_before)
    )
    value, base, after = tied(value, base, after)
    near = (feat, pos, before, pos_before, after)
    low = from_before(edge_rows(*near, cols - 1), "gy", 1)
    high = from_after(edge_rows(*near, 0), "gy", 1)
    for i, bit in enumerate(exchange.whole):
        if i == 0:
            value, (base, after_held) = exchange.whole_sum(
                value, bit, plane_work(1, 1, 3, True, base, after)
            )
        else:
            value, _ = exchange.whole_sum(value, bit)
    value = value.astype(BF16)
    value, (base,) = exchange.spread(value, plane_work(1, 4, 3, False, base, after_held))
    value, base = exchange.double(
        value,
        exchange.halved[1],
        Work(edges, *own, before_held, pos_before, after_held, low, high, base),
    )
    value, _ = exchange.double(value, exchange.halved[0])
    weighted = value.reshape(2 * vectors // KTILE, width, KTILE)
    out = field_call(ph, weighted, w_out, base, pos)
    return out.reshape(features.shape)


def solution(mesh):
    return jax.shard_map(
        on_device,
        mesh=mesh,
        in_specs=(
            P("gx", "gy", None, None, None),
            P("gx", "gy", None, None, None),
            P("gx", "gy", None),
            P(),
            P(),
            P(),
            P(),
        ),
        out_specs=P("gx", "gy", None, None, None),
        check_vma=False,
    )
```

```python
import functools
import math

import jax
import jax.numpy as jnp
from jax import lax
from jax.experimental import pallas as pl
from jax.experimental.pallas import tpu as pltpu
from jax.sharding import PartitionSpec as P

TWO_PI = 2.0 * math.pi
SHARPNESS = 600.0
CENTER_LOW = 0.2
CENTER_SPAN = 0.5
SCREEN = 16.0
FAR = 8.0
BF16 = jnp.bfloat16
F32 = jnp.float32
AXES = ("gx", "gy")
KTILE = 256

HALF_COS = (
    1.4142134965644628,
    -6.978850988150233,
    5.739461168545313,
    -1.8835629713129327,
    0.3106981552009573,
)
HALF_SIN = (4.442867902918289, -7.307443416752583, 3.594788034903934, -0.7843739144750123)
NT = (((1,), (1,)), ((), ()))
TN = (((0,), (0,)), ((), ()))
TT = (((0,), (1,)), ((), ()))
OCC_ROW = 3
CELL_ROW = 4
POS_ROWS = 16
VMEM = pltpu.VMEM


def pinned(*values):
    return [pltpu.with_memory_space_constraint(value, VMEM) for value in values]


def horner(coefs, s):
    value = coefs[-1] * s + coefs[-2]
    for c in coefs[-3::-1]:
        value = value * s + c
    return value


def factor_kernel(grid_all, scale_all, pos, kidx, feat, wc, ph_out, fac, head_out, ph, head, charges, where_at, sems):
    planes, cols, _, rows = pos.shape
    steps = ph.shape[0]
    atoms, width = feat.shape

    sub = lax.broadcasted_iota(jnp.int32, (POS_ROWS, KTILE), 0)
    kmat, screened = [], []
    for step in range(steps):
        value = jnp.zeros((POS_ROWS, KTILE), F32)
        k_sq = jnp.zeros((1, KTILE), F32)
        for d in range(3):
            k = kidx[d : d + 1, step * KTILE : (step + 1) * KTILE].astype(F32) * (1.0 / grid_all[d])
            hit = (sub == d) | (sub == CELL_ROW + d)
            value = jnp.where(hit, jnp.broadcast_to(k, value.shape), value)
            k_sq = k_sq + (TWO_PI * k) * (TWO_PI * k)
        kmat.append(value.astype(BF16))
        screened.append(jnp.exp(-k_sq / (4.0 * SCREEN)) / k_sq)
    total = sum(jnp.sum(part, axis=1, keepdims=True) for part in screened)

    sub = lax.broadcasted_iota(jnp.int32, (POS_ROWS, rows), 0)
    depth = (lax.broadcasted_iota(jnp.int32, (POS_ROWS, rows), 1) // 8).astype(F32)
    x0 = (lax.axis_index("gx") * planes).astype(F32)
    y0 = (lax.axis_index("gy") * cols).astype(F32)
    for x in range(planes):
        for y in range(cols):
            j = (x * cols + y) * rows
            tile = pos[x, y].astype(F32)
            tile = jnp.where(sub == CELL_ROW, x0 + float(x), tile)
            tile = jnp.where(sub == CELL_ROW + 1, y0 + float(y), tile)
            tile = jnp.where(sub == CELL_ROW + 2, depth, tile)
            where_at[j : j + rows, :] = tile.T.astype(BF16)
    for y in range(cols):
        head[0, y, 0:rows, :] = feat[y * rows : (y + 1) * rows, :]
        head[0, y, rows : rows + POS_ROWS, 0:rows] = pos[0, y]
        head[0, y, rows : rows + POS_ROWS, rows:width] = pos[0, y]
    copies = [pltpu.make_async_copy(head, head_out, sems.at[steps])]
    copies[0].start()
    turned = wc[...].T

    size = 2 * rows
    for step in range(steps + 1):
        sums = [None, None]
        for j in range(0, atoms, size):
            if step < steps:
                t_all = jnp.dot(
                    where_at[j : j + size, :], kmat[step], preferred_element_type=F32
                )
                for i in range(0, size, 16):
                    t = t_all[i : i + 16]
                    r = t - jnp.round(t)
                    s = r * r
                    half_c = horner(HALF_COS, s)
                    half_s = horner(HALF_SIN, s) * r
                    ph[step, 0, j + i : j + i + 16, :] = (1.0 - half_s * half_s).astype(BF16)
                    ph[step, 1, j + i : j + i + 16, :] = (half_s * half_c).astype(BF16)
            if step == 0:
                c = lax.dot_general(turned, feat[j : j + size, :], NT, preferred_element_type=F32)
                line = j // rows
                occ = [
                    pos[n // cols, n % cols, OCC_ROW : OCC_ROW + 1, :].astype(F32)
                    for n in range(line, line + 2)
                ]
                charges[:, j : j + size] = (c * jnp.concatenate(occ, axis=1)).astype(BF16)
            if step > 0:
                for p in range(2):
                    part = jnp.dot(
                        charges[:, j : j + size],
                        ph[step - 1, p, j : j + size, :],
                        preferred_element_type=F32,
                    )
                    sums[p] = part if sums[p] is None else sums[p] + part
        if step < steps:
            copy = pltpu.make_async_copy(ph.at[step], ph_out.at[step], sems.at[step])
            copy.start()
            copies.append(copy)
        if step > 0:
            weight = screened[step - 1] / total * scale_all
            for p in range(2):
                row = (2 * (step - 1) + p) * width
                fac[row : row + width, :] = sums[p] * weight
    for copy in copies:
        copy.wait()


def factor_call(pos, kidx, feat, wc, grid_all, scale_all):
    atoms, width = feat.shape
    _, cols, _, rows = pos.shape
    vectors = kidx.shape[1]
    steps = vectors // KTILE
    whole = pl.BlockSpec(memory_space=VMEM)
    in_hbm = pl.BlockSpec(memory_space=pltpu.HBM)
    phases = (steps, 2, atoms, KTILE)
    head = (1, cols, rows + POS_ROWS, width)
    return pl.pallas_call(
        functools.partial(factor_kernel, grid_all, scale_all),
        in_specs=[whole] * 4,
        out_specs=[in_hbm, whole, in_hbm],
        out_shape=[
            pltpu.HBM(phases, BF16),
            VMEM((steps * 2 * width, KTILE), F32),
            pltpu.HBM(head, BF16),
        ],
        scratch_shapes=[
            VMEM(phases, BF16),
            VMEM(head, BF16),
            VMEM((width, atoms), BF16),
            VMEM((atoms, POS_ROWS), BF16),
            pltpu.SemaphoreType.DMA((steps + 1,)),
        ],
        compiler_params=pltpu.CompilerParams(vmem_limit_bytes=24 << 20),
        cost_estimate=pl.CostEstimate(
            flops=24 * atoms * vectors * width, bytes_accessed=4 << 20, transcendentals=0
        ),
        name="factor",
    )(*pinned(pos, kidx, feat, wc))


def aggregate_row(slots, basis, near_feat, near_pos, own_pos, write):
    rows = 128
    pairs = rows // (2 * slots)
    two = 2 * slots
    window = 4 * slots
    sub = lax.broadcasted_iota(jnp.int32, (8, 128), 0)
    lane = lax.broadcasted_iota(jnp.int32, (8, 128), 1)
    lane_block = lane // window
    cell_in_window = (lane % window) // slots
    z_off = jnp.where(sub == 2, (cell_in_window - 1).astype(F32), 0.0)
    columns = [(dx, dy) for dx in (-1, 0, 1) for dy in (-1, 0, 1) if (dx, dy) != (0, 0)]
    columns.append((0, 0))
    select = jnp.where(
        lax.broadcasted_iota(jnp.int32, (POS_ROWS, 384), 0)
        == lax.broadcasted_iota(jnp.int32, (POS_ROWS, 384), 1) // 128,
        1.0,
        0.0,
    ).astype(BF16)
    stretch = math.sqrt(SHARPNESS)
    centers = [stretch * (CENTER_LOW + b * (CENTER_SPAN / (basis - 1))) for b in range(basis)]

    placed = []
    for dx, dy in columns:
        coords = near_pos(dx, dy).astype(F32)[0:8]
        occ = jnp.broadcast_to(coords[OCC_ROW : OCC_ROW + 1, :], coords.shape)
        shift = jnp.where(sub == 0, float(dx), jnp.where(sub == 1, float(dy), 0.0))
        placed.append(jnp.where(occ > 0.0, coords + shift, FAR))
    own_all = lax.dot_general(own_pos, select, TN, preferred_element_type=F32)
    for p in range(pairs):
        packed = []
        for h in range(3):
            merged = None
            for c in range(4 * h, min(4 * h + 4, 9)):
                amount = (window * (c % 4) - two * p) % 128
                moved = pltpu.roll(placed[c], amount, axis=1) if amount else placed[c]
                merged = moved if merged is None else jnp.where(lane_block == c % 4, moved, merged)
            merged = merged + z_off
            if h == 2:
                merged = jnp.where(lane_block == 0, merged, FAR)
            packed.append([jnp.broadcast_to(merged[d : d + 1, :], (8, 128)) for d in range(3)])
        parts = [[None, None] for _ in range(3)]
        for h in range(3):
            for q in range(2):
                r0 = (two * p + slots * (1 + q)) % rows
                d2 = None
                for d in range(3):
                    mine = own_all[r0 : r0 + slots, 128 * d : 128 * d + 128]
                    if d == 2 and q == 1:
                        mine = mine + 1.0
                    delta = packed[h][d] - mine
                    d2 = delta * delta if d2 is None else d2 + delta * delta
                env = jnp.maximum(1.0 - d2, 0.0)
                env = env * env
                if h == 2:
                    env = jnp.where(lane == sub + slots * (1 + q), 0.0, env)
                ar = (d2 * stretch) * lax.rsqrt(jnp.maximum(d2, 1e-30))
                values = []
                for b in range(basis):
                    u = ar - centers[b]
                    values.append(jnp.exp(u * (centers[b] - ar)) * env)
                parts[h][q] = values
        lhs = []
        for h in range(3):
            lhs.append(
                jnp.concatenate(
                    [
                        jnp.concatenate([parts[h][0][b], parts[h][1][b]], axis=0).astype(BF16)
                        for b in range(basis)
                    ],
                    axis=0,
                )
            )
        near = []
        nxt = two * ((p + 1) % pairs)
        for dx, dy in columns:
            near.append(near_feat(dx, dy, two * p, two))
            near.append(near_feat(dx, dy, nxt, two))
        near.append(jnp.zeros((384 - 9 * window, near[0].shape[1]), BF16))
        total = jnp.dot(
            jnp.concatenate(lhs, axis=1),
            jnp.concatenate(near, axis=0),
            preferred_element_type=F32,
        ).astype(BF16)
        for b in range(basis):
            write(two * p, two, b, total[two * b : two * b + two])


def turn(value, slots):
    return jnp.concatenate([value[128 - slots :], value[: 128 - slots]], axis=0)


def plane_kernel(slots, basis, plane, first, count, fetch, feat, pos, w, *rest):
    planes, _, rows, width = feat.shape
    sides = list(rest[: 2 if plane == 0 else 1])
    if fetch:
        out, held, agg, sem = rest[-4:]
        copy = pltpu.make_async_copy(sides[0], held, sem)
        copy.start()
        copy.wait()
        sides[0] = held
    else:
        out, agg = rest[-2:]

    def body(i, carry):
        y = first + i

        def near_feat(dx, dy, start, size):
            x = plane + dx
            if 0 <= x < planes:
                return feat[x, y + dy, start : start + size, :]
            return sides[0][0, y + dy, start : start + size, :]

        def near_pos(dx, dy):
            x = plane + dx
            if 0 <= x < planes:
                return pos[x, y + dy]
            if x < 0:
                return sides[1][0, y + dy]
            return sides[0][0, y + dy, rows : rows + POS_ROWS, 0:rows]

        def write(start, size, b, value):
            agg[i, start : start + size, width * b : width * (b + 1)] = value

        aggregate_row(slots, basis, near_feat, near_pos, pos[plane, y], write)
        return carry

    lax.fori_loop(0, count, body, 0)
    value = jnp.dot(
        agg[...].reshape(count * rows, basis * width), w[...], preferred_element_type=F32
    )
    value = jax.nn.silu(value).reshape(count, rows, width)
    for i in range(count):
        out[first + i, plane] = feat[plane, first + i].astype(F32) + turn(value[i], slots)


def edge_kernel(
    slots, basis, y, halo_dy, feat, pos, w, before, pos_before, after, halo, *rest
):
    out, agg = rest[-2:]
    planes, _, rows, width = feat.shape
    for plane in range(planes):

        def near_feat(dx, dy, start, size):
            x = plane + dx
            if dy == halo_dy:
                return halo[x + 1, 0, start : start + size, :]
            if 0 <= x < planes:
                return feat[x, y + dy, start : start + size, :]
            return (before if x < 0 else after)[0, y + dy, start : start + size, :]

        def near_pos(dx, dy):
            x = plane + dx
            if dy == halo_dy:
                return halo[x + 1, 0, rows : rows + POS_ROWS, 0:128]
            if 0 <= x < planes:
                return pos[x, y + dy]
            if x < 0:
                return pos_before[0, y + dy]
            return after[0, y + dy, rows : rows + POS_ROWS, 0:rows]

        def write(start, size, b, value):
            agg[plane, start : start + size, width * b : width * (b + 1)] = value

        aggregate_row(slots, basis, near_feat, near_pos, pos[plane, y], write)
    value = jnp.dot(
        agg[...].reshape(planes * rows, basis * width), w[...], preferred_element_type=F32
    )
    value = jax.nn.silu(value).reshape(planes, rows, width)
    for plane in range(planes):
        out[y, plane] = feat[plane, y].astype(F32) + turn(value[plane], slots)


def short_call(kernel, name, lines, basis, args, base, fetch=None):
    planes, cols, rows, width = args[0].shape
    whole = pl.BlockSpec(memory_space=VMEM)
    in_specs = [whole] * len(args)
    operands = pinned(*args)
    out_specs = [whole]
    out_shape = [VMEM((cols, planes, rows, width), F32)]
    scratch = [VMEM((lines, rows, basis * width), BF16)]
    aliases = {}
    if fetch is not None:
        in_specs[fetch] = pl.BlockSpec(memory_space=pltpu.HBM)
        operands[fetch] = pltpu.with_memory_space_constraint(args[fetch], pltpu.HBM)
        out_specs.append(whole)
        out_shape.append(VMEM(args[fetch].shape, BF16))
        scratch.append(pltpu.SemaphoreType.DMA)
    if base is not None:
        aliases = {len(args): 0}
        in_specs.append(whole)
        operands += pinned(base)
    return pl.pallas_call(
        kernel,
        in_specs=in_specs,
        out_specs=out_specs,
        out_shape=out_shape,
        scratch_shapes=scratch,
        input_output_aliases=aliases,
        compiler_params=pltpu.CompilerParams(vmem_limit_bytes=16 << 20),
        cost_estimate=pl.CostEstimate(
            flops=lines * rows * width * 8 * (basis * 384 + basis * width),
            bytes_accessed=4 << 20,
            transcendentals=lines * rows * 384 * (basis + 1),
        ),
        name=name,
    )(*operands)


def field_kernel(ph_all, weighted, w_out, base, pos, out, ph, rhs, held, in_sems, out_sems):
    tiles, width, _ = weighted.shape
    cols, planes, rows, _ = base.shape
    count, size, _ = held.shape
    lines = size // rows
    loads = []
    for i in range(count):
        part = pl.ds(size * i, size)
        load = pltpu.make_async_copy(
            ph_all.at[:, :, part, :], ph.at[:, :, part, :], in_sems.at[i]
        )
        load.start()
        loads.append(load)
    for t in range(tiles):
        rhs[t * KTILE : (t + 1) * KTILE, :] = weighted[t].T
    sub = lax.broadcasted_iota(jnp.int32, (POS_ROWS, width), 0)
    select = jnp.where(sub == OCC_ROW, 1.0, 0.0).astype(BF16)
    stores = []
    for i in range(count):
        loads[i].wait()
        lhs = jnp.concatenate(
            [ph[t // 2, t % 2, size * i : size * (i + 1), :] for t in range(tiles)], axis=1
        )
        recip = jnp.dot(lhs, rhs[...], preferred_element_type=F32)
        far = jnp.dot(recip.astype(BF16), w_out[...], preferred_element_type=F32)
        for j in range(lines):
            x, y = divmod(lines * i + j, cols)
            occ = lax.dot_general(pos[x, y], select, TN, preferred_element_type=F32)
            value = base[y, x] + far[rows * j : rows * (j + 1)]
            held[i, rows * j : rows * (j + 1), :] = jnp.where(occ > 0.0, value, 0.0).astype(BF16)
        store = pltpu.make_async_copy(held.at[i], out.at[pl.ds(size * i, size), :], out_sems.at[i])
        store.start()
        stores.append(store)
    for store in stores:
        store.wait()


def field_call(ph, weighted, w_out, base, pos, lines=4):
    atoms = ph.shape[2]
    tiles, width, _ = weighted.shape
    cols, planes, rows, _ = base.shape
    count = planes * cols // lines
    whole = pl.BlockSpec(memory_space=VMEM)
    return pl.pallas_call(
        field_kernel,
        in_specs=[pl.BlockSpec(memory_space=pltpu.HBM)] + [whole] * 4,
        out_specs=pl.BlockSpec(memory_space=pltpu.HBM),
        out_shape=jax.ShapeDtypeStruct((atoms, width), BF16),
        scratch_shapes=[
            VMEM(ph.shape, BF16),
            VMEM((tiles * KTILE, width), BF16),
            VMEM((count, lines * rows, width), BF16),
            pltpu.SemaphoreType.DMA((count,)),
            pltpu.SemaphoreType.DMA((count,)),
        ],
        compiler_params=pltpu.CompilerParams(vmem_limit_bytes=24 << 20),
        cost_estimate=pl.CostEstimate(
            flops=2 * atoms * tiles * KTILE * width, bytes_accessed=4 << 20, transcendentals=0
        ),
        name="field",
    )(pltpu.with_memory_space_constraint(ph, pltpu.HBM), *pinned(weighted, w_out, base, pos))


def my_index():
    return lax.axis_index("gx") * lax.axis_size("gy") + lax.axis_index("gy")


def swap(value, mask):
    count = lax.axis_size("gx") * lax.axis_size("gy")
    return lax.ppermute(value, AXES, [(i, i ^ mask) for i in range(count)])


def tied(*values):
    return lax.optimization_barrier(values)


def no_work():
    return ()


class Exchange:
    def __init__(self):
        size_y = lax.axis_size("gy")
        count = lax.axis_size("gx") * size_y
        bits = [1 << i for i in range(count.bit_length() - 1)]
        low = [b for b in bits if b < size_y]
        self.halved = low[:2]
        self.direct = low[2:4]
        self.whole = low[4:] + [b for b in bits if b >= size_y]
        self.masks = [0]
        for b in self.direct:
            self.masks = self.masks + [m ^ b for m in self.masks]

    def place(self):
        return sum(((my_index() // b) % 2) << k for k, b in enumerate(self.direct))

    def halve(self, value, bit, work=no_work):
        half = value.shape[0] // 2
        mine = (my_index() // bit) % 2
        keep = lax.dynamic_slice_in_dim(value, mine * half, half, 0)
        give = lax.dynamic_slice_in_dim(value, (1 - mine) * half, half, 0).astype(BF16)
        (got,), done = run_under([give], [bit], work)
        return keep + got.astype(F32), done

    def spread_sum(self, value, work):
        count = len(self.masks)
        value = value.reshape((count, -1) + value.shape[1:])
        me = self.place()
        keep = lax.dynamic_index_in_dim(value, me, 0, False)
        gives = [
            lax.dynamic_index_in_dim(value, me ^ j, 0, False).astype(BF16) for j in range(1, count)
        ]
        gives, done = run_under(gives, self.masks[1:], work)
        for got in gives:
            keep = keep + got.astype(F32)
        return keep, done

    def whole_sum(self, value, bit, work=no_work):
        (got,), done = run_under([value.astype(BF16)], [bit], work)
        return value + got.astype(F32), done

    def spread(self, value, work):
        count = len(self.masks)
        got, done = run_under([value] * (count - 1), self.masks[1:], work)
        parts = jnp.stack([value] + got)
        me = self.place()
        for k in range(len(self.direct)):
            b = 1 << k
            cut = parts.reshape((count // (2 * b), 2, b) + value.shape)
            parts = jnp.where((me >> k) & 1 == 0, cut, cut[:, ::-1]).reshape(parts.shape)
        return parts.reshape((-1,) + value.shape[1:]), done

    def double(self, value, bit, work=no_work):
        mine = (my_index() // bit) % 2
        (other,), done = run_under([value], [bit], work)
        return (
            jnp.where(
                mine == 0, jnp.concatenate([value, other]), jnp.concatenate([other, value])
            ),
            done,
        )


def run_under(gives, masks, work):
    inputs = work.inputs if work is not no_work else ()
    gives, inputs = tied(list(gives), inputs)
    got = [swap(give, mask) for give, mask in zip(gives, masks)]
    done = work(*inputs) if work is not no_work else ()
    return tied(got, done)


class Work:
    def __init__(self, call, *inputs):
        self.call = call
        self.inputs = inputs

    def __call__(self, *inputs):
        return self.call(*inputs)


def from_before(cells, axis, dim):
    count = lax.axis_size(axis)
    size = cells.shape[dim]
    tail = lax.slice_in_dim(cells, size - 1, size, axis=dim)
    return lax.ppermute(tail, axis, [(i, (i + 1) % count) for i in range(count)])


def from_after(cells, axis, dim):
    count = lax.axis_size(axis)
    head = lax.slice_in_dim(cells, 0, 1, axis=dim)
    return lax.ppermute(head, axis, [((i + 1) % count, i) for i in range(count)])


def edge_rows(feat, pos, before, pos_before, after, y):
    parts = []
    for f, q in ((before, pos_before), (feat, pos)):
        q = jnp.pad(q[:, y : y + 1], ((0, 0), (0, 0), (0, 0), (0, f.shape[3] - q.shape[3])))
        parts.append(jnp.concatenate([f[:, y : y + 1], q], axis=2))
    return jnp.concatenate(parts + [after[:, y : y + 1]], axis=0)


def on_device(features, fractions, counts, k_index, w_short, w_charge, w_out):
    planes, cols, depth, slots, width = features.shape
    basis = w_short.shape[0]
    vectors = k_index.shape[0]
    rows = depth * slots
    atoms = planes * cols * rows
    size_x, size_y = lax.axis_size("gx"), lax.axis_size("gy")
    grid_all = (planes * size_x, cols * size_y, depth)
    assert rows == 128 and slots == 8 and planes == 2 and cols == 8 and width == KTILE
    assert vectors % KTILE == 0
    for extent in grid_all:
        assert extent & (extent - 1) == 0 and extent <= 256
    scale_all = math.sqrt(vectors / (grid_all[0] * grid_all[1] * grid_all[2] * slots))

    feat = features.reshape(planes, cols, rows, width)
    before = from_before(feat, "gx", 0)

    occupied = (jnp.arange(slots, dtype=jnp.int32) < counts[..., None]).astype(BF16)
    frac = jnp.transpose(fractions, (0, 1, 4, 2, 3)).reshape(planes, cols, 3, rows)
    pos = jnp.concatenate(
        [
            frac,
            occupied.reshape(planes, cols, 1, rows),
            jnp.zeros((planes, cols, POS_ROWS - 4, rows), BF16),
        ],
        axis=2,
    )
    ph, partial, head = factor_call(
        pos, k_index.T, feat.reshape(atoms, width), w_charge, grid_all, scale_all
    )
    partial, before, pos_late = tied(partial, before, pos)
    pos_before = from_before(pos_late, "gx", 0)
    head, pos_before = tied(head, pos_before)
    after = from_after(head, "gx", 0)

    w_flat = w_short.reshape(basis * width, width)
    exchange = Exchange()

    own = (feat, pos, w_flat)

    def plane_work(plane, first, count, fetch, base, *sides):
        kernel = functools.partial(plane_kernel, slots, basis, plane, first, count, fetch)

        def call(*args):
            split = len(own) + len(sides)
            return short_call(
                kernel,
                "plane",
                count,
                basis,
                args[:split],
                args[split] if args[split:] else None,
                len(own) if fetch else None,
            )

        return Work(call, *own, *sides, *(() if base is None else (base,)))

    def edges(*args):
        *common, low, high, base = args
        for name, y, dy, halo in (("low", 0, -1, low), ("high", cols - 1, 1, high)):
            kernel = functools.partial(edge_kernel, slots, basis, y, dy)
            (base,) = short_call(kernel, name, planes, basis, (*common, halo), base)
        return base

    value, _ = exchange.halve(partial, exchange.halved[0])
    value, before, pos_before = tied(value, before, pos_before)
    value, (base, before_held) = exchange.halve(
        value, exchange.halved[1], plane_work(0, 1, 3, True, None, before, pos_before)
    )
    value, (base,) = exchange.spread_sum(
        value, plane_work(0, 4, 3, False, base, before_held, pos_before)
    )
    value, base, after = tied(value, base, after)
    near = (feat, pos, before, pos_before, after)
    low = from_before(edge_rows(*near, cols - 1), "gy", 1)
    high = from_after(edge_rows(*near, 0), "gy", 1)
    for i, bit in enumerate(exchange.whole):
        if i == 0:
            value, (base, after_held) = exchange.whole_sum(
                value, bit, plane_work(1, 1, 3, True, base, after)
            )
        else:
            value, _ = exchange.whole_sum(value, bit)
    value = value.astype(BF16)
    value, (base,) = exchange.spread(value, plane_work(1, 4, 3, False, base, after_held))
    value, base = exchange.double(
        value,
        exchange.halved[1],
        Work(edges, *own, before_held, pos_before, after_held, low, high, base),
    )
    value, _ = exchange.double(value, exchange.halved[0])
    weighted = value.reshape(2 * vectors // KTILE, width, KTILE)
    out = field_call(ph, weighted, w_out, base, pos)
    return out.reshape(features.shape)


def solution(mesh):
    return jax.shard_map(
        on_device,
        mesh=mesh,
        in_specs=(
            P("gx", "gy", None, None, None),
            P("gx", "gy", None, None, None),
            P("gx", "gy", None),
            P(),
            P(),
            P(),
            P(),
        ),
        out_specs=P("gx", "gy", None, None, None),
        check_vma=False,
    )
```

```python
import functools
import math

import jax
import jax.numpy as jnp
from jax import lax
from jax.experimental import pallas as pl
from jax.experimental.pallas import tpu as pltpu
from jax.sharding import PartitionSpec as P

TWO_PI = 2.0 * math.pi
SHARPNESS = 600.0
CENTER_LOW = 0.2
CENTER_SPAN = 0.5
SCREEN = 16.0
FAR = 8.0
BF16 = jnp.bfloat16
F32 = jnp.float32
AXES = ("gx", "gy")
KTILE = 256

HALF_COS = (
    1.4142134965644628,
    -6.978850988150233,
    5.739461168545313,
    -1.8835629713129327,
    0.3106981552009573,
)
HALF_SIN = (4.442867902918289, -7.307443416752583, 3.594788034903934, -0.7843739144750123)
NT = (((1,), (1,)), ((), ()))
TN = (((0,), (0,)), ((), ()))
TT = (((0,), (1,)), ((), ()))
OCC_ROW = 3
CELL_ROW = 4
POS_ROWS = 16
VMEM = pltpu.VMEM


def pinned(*values):
    return [pltpu.with_memory_space_constraint(value, VMEM) for value in values]


def horner(coefs, s):
    value = coefs[-1] * s + coefs[-2]
    for c in coefs[-3::-1]:
        value = value * s + c
    return value


def factor_kernel(grid_all, scale_all, pos, kidx_in, feat_in, wc_in, ph_out, fac, head_out, kidx, feat, wc, ph, head, charges, where_at, sems):
    planes, cols, _, rows = pos.shape
    steps = ph.shape[0]
    atoms, width = feat.shape
    loads = [
        pltpu.make_async_copy(kidx_in, kidx, sems.at[steps + 2]),
        pltpu.make_async_copy(feat_in, feat, sems.at[steps + 3]),
        pltpu.make_async_copy(wc_in, wc, sems.at[steps + 4]),
    ]
    for load in loads:
        load.start()

    for y in range(cols):
        head[0, y, :, 0:rows] = pos[0, y]
        head[0, y, :, rows:width] = pos[0, y]
    sub = lax.broadcasted_iota(jnp.int32, (POS_ROWS, rows), 0)
    depth = (lax.broadcasted_iota(jnp.int32, (POS_ROWS, rows), 1) // 8).astype(F32)
    x0 = (lax.axis_index("gx") * planes).astype(F32)
    y0 = (lax.axis_index("gy") * cols).astype(F32)
    for x in range(planes):
        for y in range(cols):
            j = (x * cols + y) * rows
            tile = pos[x, y].astype(F32)
            tile = jnp.where(sub == CELL_ROW, x0 + float(x), tile)
            tile = jnp.where(sub == CELL_ROW + 1, y0 + float(y), tile)
            tile = jnp.where(sub == CELL_ROW + 2, depth, tile)
            where_at[j : j + rows, :] = tile.T.astype(BF16)
    loads[0].wait()
    sub = lax.broadcasted_iota(jnp.int32, (POS_ROWS, KTILE), 0)
    kmat, screened = [], []
    for step in range(steps):
        value = jnp.zeros((POS_ROWS, KTILE), F32)
        k_sq = jnp.zeros((1, KTILE), F32)
        for d in range(3):
            k = kidx[d : d + 1, step * KTILE : (step + 1) * KTILE].astype(F32) * (1.0 / grid_all[d])
            hit = (sub == d) | (sub == CELL_ROW + d)
            value = jnp.where(hit, jnp.broadcast_to(k, value.shape), value)
            k_sq = k_sq + (TWO_PI * k) * (TWO_PI * k)
        kmat.append(value.astype(BF16))
        screened.append(jnp.exp(-k_sq / (4.0 * SCREEN)) / k_sq)
    total = sum(jnp.sum(part, axis=1, keepdims=True) for part in screened)

    loads[1].wait()
    loads[2].wait()
    copies = [
        pltpu.make_async_copy(head, head_out.at[:, :, pl.ds(rows, POS_ROWS), :], sems.at[steps]),
    ]
    for y in range(cols):
        copies.append(
            pltpu.make_async_copy(
                feat.at[pl.ds(y * rows, rows), :],
                head_out.at[0, y, pl.ds(0, rows), :],
                sems.at[steps + 5 + y],
            )
        )
    for copy in copies:
        copy.start()
    turned = wc[...].T

    size = 2 * rows
    for step in range(steps + 1):
        sums = [None, None]
        for j in range(0, atoms, size):
            if step < steps:
                t_all = jnp.dot(
                    where_at[j : j + size, :], kmat[step], preferred_element_type=F32
                )
                for i in range(0, size, 16):
                    t = t_all[i : i + 16]
                    r = t - jnp.round(t)
                    s = r * r
                    half_c = horner(HALF_COS, s)
                    half_s = horner(HALF_SIN, s) * r
                    ph[step, 0, j + i : j + i + 16, :] = (1.0 - half_s * half_s).astype(BF16)
                    ph[step, 1, j + i : j + i + 16, :] = (half_s * half_c).astype(BF16)
            if step == 0:
                c = lax.dot_general(turned, feat[j : j + size, :], NT, preferred_element_type=F32)
                line = j // rows
                occ = [
                    pos[n // cols, n % cols, OCC_ROW : OCC_ROW + 1, :].astype(F32)
                    for n in range(line, line + 2)
                ]
                charges[:, j : j + size] = (c * jnp.concatenate(occ, axis=1)).astype(BF16)
            if step > 0:
                for p in range(2):
                    part = jnp.dot(
                        charges[:, j : j + size],
                        ph[step - 1, p, j : j + size, :],
                        preferred_element_type=F32,
                    )
                    sums[p] = part if sums[p] is None else sums[p] + part
        if step < steps:
            copy = pltpu.make_async_copy(ph.at[step], ph_out.at[step], sems.at[step])
            copy.start()
            copies.append(copy)
        if step > 0:
            weight = screened[step - 1] / total * scale_all
            for p in range(2):
                row = (2 * (step - 1) + p) * width
                fac[row : row + width, :] = sums[p] * weight
    for copy in copies:
        copy.wait()


def factor_call(pos, kidx, feat, wc, grid_all, scale_all):
    atoms, width = feat.shape
    _, cols, _, rows = pos.shape
    vectors = kidx.shape[1]
    steps = vectors // KTILE
    whole = pl.BlockSpec(memory_space=VMEM)
    in_hbm = pl.BlockSpec(memory_space=pltpu.HBM)
    phases = (steps, 2, atoms, KTILE)
    head = (1, cols, rows + POS_ROWS, width)
    return pl.pallas_call(
        functools.partial(factor_kernel, grid_all, scale_all),
        in_specs=[whole] + [in_hbm] * 3,
        out_specs=[in_hbm, whole, in_hbm],
        out_shape=[
            pltpu.HBM(phases, BF16),
            VMEM((steps * 2 * width, KTILE), F32),
            pltpu.HBM(head, BF16),
        ],
        scratch_shapes=[
            VMEM(kidx.shape, jnp.int32),
            VMEM(feat.shape, BF16),
            VMEM(wc.shape, BF16),
            VMEM(phases, BF16),
            VMEM((1, cols, POS_ROWS, width), BF16),
            VMEM((width, atoms), BF16),
            VMEM((atoms, POS_ROWS), BF16),
            pltpu.SemaphoreType.DMA((steps + 5 + cols,)),
        ],
        compiler_params=pltpu.CompilerParams(vmem_limit_bytes=24 << 20),
        cost_estimate=pl.CostEstimate(
            flops=24 * atoms * vectors * width, bytes_accessed=4 << 20, transcendentals=0
        ),
        name="factor",
    )(
        *pinned(pos),
        *[pltpu.with_memory_space_constraint(value, pltpu.HBM) for value in (kidx, feat, wc)],
    )


def aggregate_row(slots, basis, near_feat, near_pos, own_pos, write):
    rows = 128
    pairs = rows // (2 * slots)
    two = 2 * slots
    window = 4 * slots
    sub = lax.broadcasted_iota(jnp.int32, (8, 128), 0)
    lane = lax.broadcasted_iota(jnp.int32, (8, 128), 1)
    lane_block = lane // window
    cell_in_window = (lane % window) // slots
    z_off = jnp.where(sub == 2, (cell_in_window - 1).astype(F32), 0.0)
    columns = [(dx, dy) for dx in (-1, 0, 1) for dy in (-1, 0, 1) if (dx, dy) != (0, 0)]
    columns.append((0, 0))
    select = jnp.where(
        lax.broadcasted_iota(jnp.int32, (POS_ROWS, 384), 0)
        == lax.broadcasted_iota(jnp.int32, (POS_ROWS, 384), 1) // 128,
        1.0,
        0.0,
    ).astype(BF16)
    stretch = math.sqrt(SHARPNESS)
    centers = [stretch * (CENTER_LOW + b * (CENTER_SPAN / (basis - 1))) for b in range(basis)]

    placed = []
    for dx, dy in columns:
        coords = near_pos(dx, dy).astype(F32)[0:8]
        occ = jnp.broadcast_to(coords[OCC_ROW : OCC_ROW + 1, :], coords.shape)
        shift = jnp.where(sub == 0, float(dx), jnp.where(sub == 1, float(dy), 0.0))
        placed.append(jnp.where(occ > 0.0, coords + shift, FAR))
    own_all = lax.dot_general(own_pos, select, TN, preferred_element_type=F32)
    for p in range(pairs):
        packed = []
        for h in range(3):
            merged = None
            for c in range(4 * h, min(4 * h + 4, 9)):
                amount = (window * (c % 4) - two * p) % 128
                moved = pltpu.roll(placed[c], amount, axis=1) if amount else placed[c]
                merged = moved if merged is None else jnp.where(lane_block == c % 4, moved, merged)
            merged = merged + z_off
            if h == 2:
                merged = jnp.where(lane_block == 0, merged, FAR)
            packed.append([jnp.broadcast_to(merged[d : d + 1, :], (8, 128)) for d in range(3)])
        parts = [[None, None] for _ in range(3)]
        for h in range(3):
            for q in range(2):
                r0 = (two * p + slots * (1 + q)) % rows
                d2 = None
                for d in range(3):
                    mine = own_all[r0 : r0 + slots, 128 * d : 128 * d + 128]
                    if d == 2 and q == 1:
                        mine = mine + 1.0
                    delta = packed[h][d] - mine
                    d2 = delta * delta if d2 is None else d2 + delta * delta
                env = jnp.maximum(1.0 - d2, 0.0)
                env = env * env
                if h == 2:
                    env = jnp.where(lane == sub + slots * (1 + q), 0.0, env)
                ar = (d2 * stretch) * lax.rsqrt(jnp.maximum(d2, 1e-30))
                values = []
                for b in range(basis):
                    u = ar - centers[b]
                    values.append(jnp.exp(u * (centers[b] - ar)) * env)
                parts[h][q] = values
        lhs = []
        for h in range(3):
            lhs.append(
                jnp.concatenate(
                    [
                        jnp.concatenate([parts[h][0][b], parts[h][1][b]], axis=0).astype(BF16)
                        for b in range(basis)
                    ],
                    axis=0,
                )
            )
        near = []
        nxt = two * ((p + 1) % pairs)
        for dx, dy in columns:
            near.append(near_feat(dx, dy, two * p, two))
            near.append(near_feat(dx, dy, nxt, two))
        near.append(jnp.zeros((384 - 9 * window, near[0].shape[1]), BF16))
        total = jnp.dot(
            jnp.concatenate(lhs, axis=1),
            jnp.concatenate(near, axis=0),
            preferred_element_type=F32,
        ).astype(BF16)
        for b in range(basis):
            write(two * p, two, b, total[two * b : two * b + two])


def turn(value, slots):
    return jnp.concatenate([value[128 - slots :], value[: 128 - slots]], axis=0)


def plane_kernel(slots, basis, plane, first, count, fetch, feat, pos, w, *rest):
    planes, _, rows, width = feat.shape
    sides = list(rest[: 2 if plane == 0 else 1])
    if fetch:
        out, held, agg, sem = rest[-4:]
        copy = pltpu.make_async_copy(sides[0], held, sem)
        copy.start()
        copy.wait()
        sides[0] = held
    else:
        out, agg = rest[-2:]

    def body(i, carry):
        y = first + i

        def near_feat(dx, dy, start, size):
            x = plane + dx
            if 0 <= x < planes:
                return feat[x, y + dy, start : start + size, :]
            return sides[0][0, y + dy, start : start + size, :]

        def near_pos(dx, dy):
            x = plane + dx
            if 0 <= x < planes:
                return pos[x, y + dy]
            if x < 0:
                return sides[1][0, y + dy]
            return sides[0][0, y + dy, rows : rows + POS_ROWS, 0:rows]

        def write(start, size, b, value):
            agg[i, start : start + size, width * b : width * (b + 1)] = value

        aggregate_row(slots, basis, near_feat, near_pos, pos[plane, y], write)
        return carry

    lax.fori_loop(0, count, body, 0)
    value = jnp.dot(
        agg[...].reshape(count * rows, basis * width), w[...], preferred_element_type=F32
    )
    value = jax.nn.silu(value).reshape(count, rows, width)
    for i in range(count):
        out[first + i, plane] = feat[plane, first + i].astype(F32) + turn(value[i], slots)


def edge_kernel(
    slots, basis, y, halo_dy, feat, pos, w, before, pos_before, after, halo, *rest
):
    out, agg = rest[-2:]
    planes, _, rows, width = feat.shape
    for plane in range(planes):

        def near_feat(dx, dy, start, size):
            x = plane + dx
            if dy == halo_dy:
                return halo[x + 1, 0, start : start + size, :]
            if 0 <= x < planes:
                return feat[x, y + dy, start : start + size, :]
            return (before if x < 0 else after)[0, y + dy, start : start + size, :]

        def near_pos(dx, dy):
            x = plane + dx
            if dy == halo_dy:
                return halo[x + 1, 0, rows : rows + POS_ROWS, 0:128]
            if 0 <= x < planes:
                return pos[x, y + dy]
            if x < 0:
                return pos_before[0, y + dy]
            return after[0, y + dy, rows : rows + POS_ROWS, 0:rows]

        def write(start, size, b, value):
            agg[plane, start : start + size, width * b : width * (b + 1)] = value

        aggregate_row(slots, basis, near_feat, near_pos, pos[plane, y], write)
    value = jnp.dot(
        agg[...].reshape(planes * rows, basis * width), w[...], preferred_element_type=F32
    )
    value = jax.nn.silu(value).reshape(planes, rows, width)
    for plane in range(planes):
        out[y, plane] = feat[plane, y].astype(F32) + turn(value[plane], slots)


def short_call(kernel, name, lines, basis, args, base, fetch=None):
    planes, cols, rows, width = args[0].shape
    whole = pl.BlockSpec(memory_space=VMEM)
    in_specs = [whole] * len(args)
    operands = pinned(*args)
    out_specs = [whole]
    out_shape = [VMEM((cols, planes, rows, width), F32)]
    scratch = [VMEM((lines, rows, basis * width), BF16)]
    aliases = {}
    if fetch is not None:
        in_specs[fetch] = pl.BlockSpec(memory_space=pltpu.HBM)
        operands[fetch] = pltpu.with_memory_space_constraint(args[fetch], pltpu.HBM)
        out_specs.append(whole)
        out_shape.append(VMEM(args[fetch].shape, BF16))
        scratch.append(pltpu.SemaphoreType.DMA)
    if base is not None:
        aliases = {len(args): 0}
        in_specs.append(whole)
        operands += pinned(base)
    return pl.pallas_call(
        kernel,
        in_specs=in_specs,
        out_specs=out_specs,
        out_shape=out_shape,
        scratch_shapes=scratch,
        input_output_aliases=aliases,
        compiler_params=pltpu.CompilerParams(vmem_limit_bytes=16 << 20),
        cost_estimate=pl.CostEstimate(
            flops=lines * rows * width * 8 * (basis * 384 + basis * width),
            bytes_accessed=4 << 20,
            transcendentals=lines * rows * 384 * (basis + 1),
        ),
        name=name,
    )(*operands)


def field_kernel(ph_all, weighted, w_out, base, pos, out, ph, rhs, held, in_sems, out_sems):
    tiles, width, _ = weighted.shape
    cols, planes, rows, _ = base.shape
    count, size, _ = held.shape
    lines = size // rows
    loads = []
    for i in range(count):
        part = pl.ds(size * i, size)
        load = pltpu.make_async_copy(
            ph_all.at[:, :, part, :], ph.at[:, :, part, :], in_sems.at[i]
        )
        load.start()
        loads.append(load)
    for t in range(tiles):
        rhs[t * KTILE : (t + 1) * KTILE, :] = weighted[t].T
    sub = lax.broadcasted_iota(jnp.int32, (POS_ROWS, width), 0)
    select = jnp.where(sub == OCC_ROW, 1.0, 0.0).astype(BF16)
    stores = []
    for i in range(count):
        loads[i].wait()
        lhs = jnp.concatenate(
            [ph[t // 2, t % 2, size * i : size * (i + 1), :] for t in range(tiles)], axis=1
        )
        recip = jnp.dot(lhs, rhs[...], preferred_element_type=F32)
        far = jnp.dot(recip.astype(BF16), w_out[...], preferred_element_type=F32)
        for j in range(lines):
            x, y = divmod(lines * i + j, cols)
            occ = lax.dot_general(pos[x, y], select, TN, preferred_element_type=F32)
            value = base[y, x] + far[rows * j : rows * (j + 1)]
            held[i, rows * j : rows * (j + 1), :] = jnp.where(occ > 0.0, value, 0.0).astype(BF16)
        store = pltpu.make_async_copy(held.at[i], out.at[pl.ds(size * i, size), :], out_sems.at[i])
        store.start()
        stores.append(store)
    for store in stores:
        store.wait()


def field_call(ph, weighted, w_out, base, pos, lines=4):
    atoms = ph.shape[2]
    tiles, width, _ = weighted.shape
    cols, planes, rows, _ = base.shape
    count = planes * cols // lines
    whole = pl.BlockSpec(memory_space=VMEM)
    return pl.pallas_call(
        field_kernel,
        in_specs=[pl.BlockSpec(memory_space=pltpu.HBM)] + [whole] * 4,
        out_specs=pl.BlockSpec(memory_space=pltpu.HBM),
        out_shape=jax.ShapeDtypeStruct((atoms, width), BF16),
        scratch_shapes=[
            VMEM(ph.shape, BF16),
            VMEM((tiles * KTILE, width), BF16),
            VMEM((count, lines * rows, width), BF16),
            pltpu.SemaphoreType.DMA((count,)),
            pltpu.SemaphoreType.DMA((count,)),
        ],
        compiler_params=pltpu.CompilerParams(vmem_limit_bytes=24 << 20),
        cost_estimate=pl.CostEstimate(
            flops=2 * atoms * tiles * KTILE * width, bytes_accessed=4 << 20, transcendentals=0
        ),
        name="field",
    )(pltpu.with_memory_space_constraint(ph, pltpu.HBM), *pinned(weighted, w_out, base, pos))


def my_index():
    return lax.axis_index("gx") * lax.axis_size("gy") + lax.axis_index("gy")


def swap(value, mask):
    count = lax.axis_size("gx") * lax.axis_size("gy")
    return lax.ppermute(value, AXES, [(i, i ^ mask) for i in range(count)])


def tied(*values):
    return lax.optimization_barrier(values)


def no_work():
    return ()


class Exchange:
    def __init__(self):
        size_y = lax.axis_size("gy")
        count = lax.axis_size("gx") * size_y
        bits = [1 << i for i in range(count.bit_length() - 1)]
        low = [b for b in bits if b < size_y]
        self.halved = low[:2]
        self.direct = low[2:4]
        self.whole = low[4:] + [b for b in bits if b >= size_y]
        self.masks = [0]
        for b in self.direct:
            self.masks = self.masks + [m ^ b for m in self.masks]

    def place(self):
        return sum(((my_index() // b) % 2) << k for k, b in enumerate(self.direct))

    def halve(self, value, bit, work=no_work):
        half = value.shape[0] // 2
        mine = (my_index() // bit) % 2
        keep = lax.dynamic_slice_in_dim(value, mine * half, half, 0)
        give = lax.dynamic_slice_in_dim(value, (1 - mine) * half, half, 0).astype(BF16)
        (got,), done = run_under([give], [bit], work)
        return keep + got.astype(F32), done

    def spread_sum(self, value, work):
        count = len(self.masks)
        value = value.reshape((count, -1) + value.shape[1:])
        me = self.place()
        keep = lax.dynamic_index_in_dim(value, me, 0, False)
        gives = [
            lax.dynamic_index_in_dim(value, me ^ j, 0, False).astype(BF16) for j in range(1, count)
        ]
        gives, done = run_under(gives, self.masks[1:], work)
        for got in gives:
            keep = keep + got.astype(F32)
        return keep, done

    def whole_sum(self, value, bit, work=no_work):
        (got,), done = run_under([value.astype(BF16)], [bit], work)
        return value + got.astype(F32), done

    def spread(self, value, work):
        count = len(self.masks)
        got, done = run_under([value] * (count - 1), self.masks[1:], work)
        parts = jnp.stack([value] + got)
        me = self.place()
        for k in range(len(self.direct)):
            b = 1 << k
            cut = parts.reshape((count // (2 * b), 2, b) + value.shape)
            parts = jnp.where((me >> k) & 1 == 0, cut, cut[:, ::-1]).reshape(parts.shape)
        return parts.reshape((-1,) + value.shape[1:]), done

    def double(self, value, bit, work=no_work):
        mine = (my_index() // bit) % 2
        (other,), done = run_under([value], [bit], work)
        return (
            jnp.where(
                mine == 0, jnp.concatenate([value, other]), jnp.concatenate([other, value])
            ),
            done,
        )


def run_under(gives, masks, work):
    inputs = work.inputs if work is not no_work else ()
    gives, inputs = tied(list(gives), inputs)
    got = [swap(give, mask) for give, mask in zip(gives, masks)]
    done = work(*inputs) if work is not no_work else ()
    return tied(got, done)


class Work:
    def __init__(self, call, *inputs):
        self.call = call
        self.inputs = inputs

    def __call__(self, *inputs):
        return self.call(*inputs)


def from_before(cells, axis, dim):
    count = lax.axis_size(axis)
    size = cells.shape[dim]
    tail = lax.slice_in_dim(cells, size - 1, size, axis=dim)
    return lax.ppermute(tail, axis, [(i, (i + 1) % count) for i in range(count)])


def from_after(cells, axis, dim):
    count = lax.axis_size(axis)
    head = lax.slice_in_dim(cells, 0, 1, axis=dim)
    return lax.ppermute(head, axis, [((i + 1) % count, i) for i in range(count)])


def edge_rows(feat, pos, before, pos_before, after, y):
    parts = []
    for f, q in ((before, pos_before), (feat, pos)):
        q = jnp.pad(q[:, y : y + 1], ((0, 0), (0, 0), (0, 0), (0, f.shape[3] - q.shape[3])))
        parts.append(jnp.concatenate([f[:, y : y + 1], q], axis=2))
    return jnp.concatenate(parts + [after[:, y : y + 1]], axis=0)


def on_device(features, fractions, counts, k_index, w_short, w_charge, w_out):
    planes, cols, depth, slots, width = features.shape
    basis = w_short.shape[0]
    vectors = k_index.shape[0]
    rows = depth * slots
    atoms = planes * cols * rows
    size_x, size_y = lax.axis_size("gx"), lax.axis_size("gy")
    grid_all = (planes * size_x, cols * size_y, depth)
    assert rows == 128 and slots == 8 and planes == 2 and cols == 8 and width == KTILE
    assert vectors % KTILE == 0
    for extent in grid_all:
        assert extent & (extent - 1) == 0 and extent <= 256
    scale_all = math.sqrt(vectors / (grid_all[0] * grid_all[1] * grid_all[2] * slots))

    feat = features.reshape(planes, cols, rows, width)
    before = from_before(feat, "gx", 0)

    occupied = (jnp.arange(slots, dtype=jnp.int32) < counts[..., None]).astype(BF16)
    frac = jnp.transpose(fractions, (0, 1, 4, 2, 3)).reshape(planes, cols, 3, rows)
    pos = jnp.concatenate(
        [
            frac,
            occupied.reshape(planes, cols, 1, rows),
            jnp.zeros((planes, cols, POS_ROWS - 4, rows), BF16),
        ],
        axis=2,
    )
    pos_before = from_before(pos, "gx", 0)

    ph, partial, head = factor_call(
        pos, k_index.T, feat.reshape(atoms, width), w_charge, grid_all, scale_all
    )
    partial, before, pos_before = tied(partial, before, pos_before)
    after = from_after(head, "gx", 0)

    w_flat = w_short.reshape(basis * width, width)
    exchange = Exchange()

    own = (feat, pos, w_flat)

    def plane_work(plane, first, count, fetch, base, *sides):
        kernel = functools.partial(plane_kernel, slots, basis, plane, first, count, fetch)

        def call(*args):
            split = len(own) + len(sides)
            return short_call(
                kernel,
                "plane",
                count,
                basis,
                args[:split],
                args[split] if args[split:] else None,
                len(own) if fetch else None,
            )

        return Work(call, *own, *sides, *(() if base is None else (base,)))

    def edges(*args):
        *common, low, high, base = args
        for name, y, dy, halo in (("low", 0, -1, low), ("high", cols - 1, 1, high)):
            kernel = functools.partial(edge_kernel, slots, basis, y, dy)
            (base,) = short_call(kernel, name, planes, basis, (*common, halo), base)
        return base

    value, _ = exchange.halve(partial, exchange.halved[0])
    value, before, pos_before = tied(value, before, pos_before)
    value, (base, before_held) = exchange.halve(
        value, exchange.halved[1], plane_work(0, 1, 3, True, None, before, pos_before)
    )
    value, (base,) = exchange.spread_sum(
        value, plane_work(0, 4, 3, False, base, before_held, pos_before)
    )
    value, base, after = tied(value, base, after)
    near = (feat, pos, before, pos_before, after)
    low = from_before(edge_rows(*near, cols - 1), "gy", 1)
    high = from_after(edge_rows(*near, 0), "gy", 1)
    for i, bit in enumerate(exchange.whole):
        if i == 0:
            value, (base, after_held) = exchange.whole_sum(
                value, bit, plane_work(1, 1, 3, True, base, after)
            )
        else:
            value, _ = exchange.whole_sum(value, bit)
    value = value.astype(BF16)
    value, (base,) = exchange.spread(value, plane_work(1, 4, 3, False, base, after_held))
    value, base = exchange.double(
        value,
        exchange.halved[1],
        Work(edges, *own, before_held, pos_before, after_held, low, high, base),
    )
    value, _ = exchange.double(value, exchange.halved[0])
    weighted = value.reshape(2 * vectors // KTILE, width, KTILE)
    out = field_call(ph, weighted, w_out, base, pos)
    return out.reshape(features.shape)


def solution(mesh):
    return jax.shard_map(
        on_device,
        mesh=mesh,
        in_specs=(
            P("gx", "gy", None, None, None),
            P("gx", "gy", None, None, None),
            P("gx", "gy", None),
            P(),
            P(),
            P(),
            P(),
        ),
        out_specs=P("gx", "gy", None, None, None),
        check_vma=False,
    )
```

```python
import functools
import math

import jax
import jax.numpy as jnp
from jax import lax
from jax.experimental import pallas as pl
from jax.experimental.pallas import tpu as pltpu
from jax.sharding import PartitionSpec as P

TWO_PI = 2.0 * math.pi
SHARPNESS = 600.0
CENTER_LOW = 0.2
CENTER_SPAN = 0.5
SCREEN = 16.0
FAR = 8.0
BF16 = jnp.bfloat16
F32 = jnp.float32
AXES = ("gx", "gy")
KTILE = 256

HALF_COS = (
    1.4142134965644628,
    -6.978850988150233,
    5.739461168545313,
    -1.8835629713129327,
    0.3106981552009573,
)
HALF_SIN = (4.442867902918289, -7.307443416752583, 3.594788034903934, -0.7843739144750123)
NT = (((1,), (1,)), ((), ()))
TN = (((0,), (0,)), ((), ()))
TT = (((0,), (1,)), ((), ()))
OCC_ROW = 3
CELL_ROW = 4
POS_ROWS = 16
VMEM = pltpu.VMEM


def pinned(*values):
    return [pltpu.with_memory_space_constraint(value, VMEM) for value in values]


def horner(coefs, s):
    value = coefs[-1] * s + coefs[-2]
    for c in coefs[-3::-1]:
        value = value * s + c
    return value


def factor_kernel(grid_all, scale_all, pos, kidx, feat, wc, ph_out, fac, ph, charges, where_at, sems):
    planes, cols, _, rows = pos.shape
    copies = []
    steps = ph.shape[0]
    atoms, width = feat.shape

    sub = lax.broadcasted_iota(jnp.int32, (POS_ROWS, KTILE), 0)
    kmat, screened = [], []
    for step in range(steps):
        value = jnp.zeros((POS_ROWS, KTILE), F32)
        k_sq = jnp.zeros((1, KTILE), F32)
        for d in range(3):
            k = kidx[d : d + 1, step * KTILE : (step + 1) * KTILE].astype(F32) * (1.0 / grid_all[d])
            hit = (sub == d) | (sub == CELL_ROW + d)
            value = jnp.where(hit, jnp.broadcast_to(k, value.shape), value)
            k_sq = k_sq + (TWO_PI * k) * (TWO_PI * k)
        kmat.append(value.astype(BF16))
        screened.append(jnp.exp(-k_sq / (4.0 * SCREEN)) / k_sq)
    total = sum(jnp.sum(part, axis=1, keepdims=True) for part in screened)

    sub = lax.broadcasted_iota(jnp.int32, (POS_ROWS, rows), 0)
    depth = (lax.broadcasted_iota(jnp.int32, (POS_ROWS, rows), 1) // 8).astype(F32)
    x0 = (lax.axis_index("gx") * planes).astype(F32)
    y0 = (lax.axis_index("gy") * cols).astype(F32)
    for x in range(planes):
        for y in range(cols):
            j = (x * cols + y) * rows
            tile = pos[x, y].astype(F32)
            tile = jnp.where(sub == CELL_ROW, x0 + float(x), tile)
            tile = jnp.where(sub == CELL_ROW + 1, y0 + float(y), tile)
            tile = jnp.where(sub == CELL_ROW + 2, depth, tile)
            where_at[j : j + rows, :] = tile.T.astype(BF16)
    turned = wc[...].T

    size = 2 * rows
    for step in range(steps + 1):
        sums = [None, None]
        for j in range(0, atoms, size):
            if step < steps:
                t_all = jnp.dot(
                    where_at[j : j + size, :], kmat[step], preferred_element_type=F32
                )
                for i in range(0, size, 16):
                    t = t_all[i : i + 16]
                    r = t - jnp.round(t)
                    s = r * r
                    half_c = horner(HALF_COS, s)
                    half_s = horner(HALF_SIN, s) * r
                    ph[step, 0, j + i : j + i + 16, :] = (1.0 - half_s * half_s).astype(BF16)
                    ph[step, 1, j + i : j + i + 16, :] = (half_s * half_c).astype(BF16)
            if step == 0:
                c = lax.dot_general(turned, feat[j : j + size, :], NT, preferred_element_type=F32)
                line = j // rows
                occ = [
                    pos[n // cols, n % cols, OCC_ROW : OCC_ROW + 1, :].astype(F32)
                    for n in range(line, line + 2)
                ]
                charges[:, j : j + size] = (c * jnp.concatenate(occ, axis=1)).astype(BF16)
            if step > 0:
                for p in range(2):
                    part = jnp.dot(
                        charges[:, j : j + size],
                        ph[step - 1, p, j : j + size, :],
                        preferred_element_type=F32,
                    )
                    sums[p] = part if sums[p] is None else sums[p] + part
        if step < steps:
            copy = pltpu.make_async_copy(ph.at[step], ph_out.at[step], sems.at[step])
            copy.start()
            copies.append(copy)
        if step > 0:
            weight = screened[step - 1] / total * scale_all
            for p in range(2):
                row = (2 * (step - 1) + p) * width
                fac[row : row + width, :] = sums[p] * weight
    for copy in copies:
        copy.wait()


def factor_call(pos, kidx, feat, wc, grid_all, scale_all):
    atoms, width = feat.shape
    vectors = kidx.shape[1]
    steps = vectors // KTILE
    whole = pl.BlockSpec(memory_space=VMEM)
    return pl.pallas_call(
        functools.partial(factor_kernel, grid_all, scale_all),
        in_specs=[whole] * 4,
        out_specs=[pl.BlockSpec(memory_space=pltpu.HBM), whole],
        out_shape=[
            pltpu.HBM((steps, 2, atoms, KTILE), BF16),
            VMEM((steps * 2 * width, KTILE), F32),
        ],
        scratch_shapes=[
            VMEM((steps, 2, atoms, KTILE), BF16),
            VMEM((width, atoms), BF16),
            VMEM((atoms, POS_ROWS), BF16),
            pltpu.SemaphoreType.DMA((steps,)),
        ],
        compiler_params=pltpu.CompilerParams(vmem_limit_bytes=24 << 20),
        cost_estimate=pl.CostEstimate(
            flops=24 * atoms * vectors * width, bytes_accessed=4 << 20, transcendentals=0
        ),
        name="factor",
    )(*pinned(pos, kidx, feat, wc))


def aggregate_row(slots, basis, near_feat, near_pos, own_pos, write):
    rows = 128
    pairs = rows // (2 * slots)
    two = 2 * slots
    window = 4 * slots
    sub = lax.broadcasted_iota(jnp.int32, (8, 128), 0)
    lane = lax.broadcasted_iota(jnp.int32, (8, 128), 1)
    lane_block = lane // window
    cell_in_window = (lane % window) // slots
    z_off = jnp.where(sub == 2, (cell_in_window - 1).astype(F32), 0.0)
    columns = [(dx, dy) for dx in (-1, 0, 1) for dy in (-1, 0, 1) if (dx, dy) != (0, 0)]
    columns.append((0, 0))
    select = jnp.where(
        lax.broadcasted_iota(jnp.int32, (POS_ROWS, 384), 0)
        == lax.broadcasted_iota(jnp.int32, (POS_ROWS, 384), 1) // 128,
        1.0,
        0.0,
    ).astype(BF16)
    stretch = math.sqrt(SHARPNESS)
    centers = [stretch * (CENTER_LOW + b * (CENTER_SPAN / (basis - 1))) for b in range(basis)]

    placed = []
    for dx, dy in columns:
        coords = near_pos(dx, dy).astype(F32)[0:8]
        occ = jnp.broadcast_to(coords[OCC_ROW : OCC_ROW + 1, :], coords.shape)
        shift = jnp.where(sub == 0, float(dx), jnp.where(sub == 1, float(dy), 0.0))
        placed.append(jnp.where(occ > 0.0, coords + shift, FAR))
    own_all = lax.dot_general(own_pos, select, TN, preferred_element_type=F32)
    for p in range(pairs):
        packed = []
        for h in range(3):
            merged = None
            for c in range(4 * h, min(4 * h + 4, 9)):
                amount = (window * (c % 4) - two * p) % 128
                moved = pltpu.roll(placed[c], amount, axis=1) if amount else placed[c]
                merged = moved if merged is None else jnp.where(lane_block == c % 4, moved, merged)
            merged = merged + z_off
            if h == 2:
                merged = jnp.where(lane_block == 0, merged, FAR)
            packed.append([jnp.broadcast_to(merged[d : d + 1, :], (8, 128)) for d in range(3)])
        parts = [[None, None] for _ in range(3)]
        for h in range(3):
            for q in range(2):
                r0 = (two * p + slots * (1 + q)) % rows
                d2 = None
                for d in range(3):
                    mine = own_all[r0 : r0 + slots, 128 * d : 128 * d + 128]
                    if d == 2 and q == 1:
                        mine = mine + 1.0
                    delta = packed[h][d] - mine
                    d2 = delta * delta if d2 is None else d2 + delta * delta
                env = jnp.maximum(1.0 - d2, 0.0)
                env = env * env
                if h == 2:
                    env = jnp.where(lane == sub + slots * (1 + q), 0.0, env)
                ar = (d2 * stretch) * lax.rsqrt(jnp.maximum(d2, 1e-30))
                values = []
                for b in range(basis):
                    u = ar - centers[b]
                    values.append(jnp.exp(u * (centers[b] - ar)) * env)
                parts[h][q] = values
        lhs = []
        for h in range(3):
            lhs.append(
                jnp.concatenate(
                    [
                        jnp.concatenate([parts[h][0][b], parts[h][1][b]], axis=0).astype(BF16)
                        for b in range(basis)
                    ],
                    axis=0,
                )
            )
        near = []
        nxt = two * ((p + 1) % pairs)
        for dx, dy in columns:
            near.append(near_feat(dx, dy, two * p, two))
            near.append(near_feat(dx, dy, nxt, two))
        near.append(jnp.zeros((384 - 9 * window, near[0].shape[1]), BF16))
        total = jnp.dot(
            jnp.concatenate(lhs, axis=1),
            jnp.concatenate(near, axis=0),
            preferred_element_type=F32,
        ).astype(BF16)
        for b in range(basis):
            write(two * p, two, b, total[two * b : two * b + two])


def turn(value, slots):
    return jnp.concatenate([value[128 - slots :], value[: 128 - slots]], axis=0)


def plane_kernel(slots, basis, plane, first, count, feat, pos, side_feat, side_pos, w, *rest):
    out, agg = rest[-2:]
    planes, _, rows, width = feat.shape

    def pick(ref, side, dx):
        x = plane + dx
        return (ref, x) if 0 <= x < planes else (side, 0)

    def body(i, carry):
        y = first + i

        def near_feat(dx, dy, start, size):
            ref, x = pick(feat, side_feat, dx)
            return ref[x, y + dy, start : start + size, :]

        def near_pos(dx, dy):
            ref, x = pick(pos, side_pos, dx)
            return ref[x, y + dy]

        def write(start, size, b, value):
            agg[i, start : start + size, width * b : width * (b + 1)] = value

        aggregate_row(slots, basis, near_feat, near_pos, pos[plane, y], write)
        return carry

    lax.fori_loop(0, count, body, 0)
    value = jnp.dot(
        agg[...].reshape(count * rows, basis * width), w[...], preferred_element_type=F32
    )
    value = jax.nn.silu(value).reshape(count, rows, width)
    for i in range(count):
        out[first + i, plane] = feat[plane, first + i].astype(F32) + turn(value[i], slots)


def edge_kernel(
    slots, basis, y, halo_dy, feat, pos, before, pos_before, after, pos_after, halo, w, *rest
):
    out, agg = rest[-2:]
    planes, _, rows, width = feat.shape
    for plane in range(planes):

        def near_feat(dx, dy, start, size):
            x = plane + dx
            if dy == halo_dy:
                return halo[x + 1, 0, start : start + size, :]
            if 0 <= x < planes:
                return feat[x, y + dy, start : start + size, :]
            return (before if x < 0 else after)[0, y + dy, start : start + size, :]

        def near_pos(dx, dy):
            x = plane + dx
            if dy == halo_dy:
                return halo[x + 1, 0, rows : rows + POS_ROWS, 0:128]
            if 0 <= x < planes:
                return pos[x, y + dy]
            return (pos_before if x < 0 else pos_after)[0, y + dy]

        def write(start, size, b, value):
            agg[plane, start : start + size, width * b : width * (b + 1)] = value

        aggregate_row(slots, basis, near_feat, near_pos, pos[plane, y], write)
    value = jnp.dot(
        agg[...].reshape(planes * rows, basis * width), w[...], preferred_element_type=F32
    )
    value = jax.nn.silu(value).reshape(planes, rows, width)
    for plane in range(planes):
        out[y, plane] = feat[plane, y].astype(F32) + turn(value[plane], slots)


def short_call(kernel, name, lines, basis, args, base):
    planes, cols, rows, width = args[0].shape
    whole = pl.BlockSpec(memory_space=VMEM)
    aliases = {}
    if base is not None:
        aliases = {len(args): 0}
        args = (*args, base)
    return pl.pallas_call(
        kernel,
        in_specs=[whole] * len(args),
        out_specs=whole,
        out_shape=VMEM((cols, planes, rows, width), F32),
        scratch_shapes=[VMEM((lines, rows, basis * width), BF16)],
        input_output_aliases=aliases,
        compiler_params=pltpu.CompilerParams(vmem_limit_bytes=16 << 20),
        cost_estimate=pl.CostEstimate(
            flops=lines * rows * width * 8 * (basis * 384 + basis * width),
            bytes_accessed=4 << 20,
            transcendentals=lines * rows * 384 * (basis + 1),
        ),
        name=name,
    )(*pinned(*args))


def phase_loads(ph_all, ph, sems, half, lines):
    size = ph.shape[2] // lines
    loads = []
    for i in range(lines):
        part = pl.ds(size * i, size)
        load = pltpu.make_async_copy(
            ph_all.at[pl.ds(half * ph.shape[0], ph.shape[0]), :, part, :],
            ph.at[:, :, part, :],
            sems.at[i],
        )
        load.start()
        loads.append(load)
    return loads


def half_field(ph, rhs, tiles, part):
    lhs = jnp.concatenate([ph[t // 2, t % 2, part, :] for t in range(tiles)], axis=1)
    return jnp.dot(lhs, rhs[...], preferred_element_type=F32)


def near_field_kernel(lines, ph_all, weighted, out, ph, rhs, in_sems):
    tiles = weighted.shape[0]
    loads = phase_loads(ph_all, ph, in_sems, lax.rem(lax.axis_index("gy"), 2), lines)
    for t in range(tiles):
        rhs[t * KTILE : (t + 1) * KTILE, :] = weighted[t].T
    size = ph.shape[2] // lines
    for i in range(lines):
        loads[i].wait()
        part = slice(size * i, size * (i + 1))
        out[part, :] = half_field(ph, rhs, tiles, part)


def far_field_kernel(
    lines, ph_all, weighted, partial, w_out, base, pos, out, ph, rhs, held, in_sems, out_sems
):
    tiles, width, _ = weighted.shape
    cols, planes, rows, _ = base.shape
    loads = phase_loads(ph_all, ph, in_sems, 1 - lax.rem(lax.axis_index("gy"), 2), lines)
    for t in range(tiles):
        rhs[t * KTILE : (t + 1) * KTILE, :] = weighted[t].T
    sub = lax.broadcasted_iota(jnp.int32, (POS_ROWS, width), 0)
    select = jnp.where(sub == OCC_ROW, 1.0, 0.0).astype(BF16)
    size = ph.shape[2] // lines
    each = size // rows
    stores = []
    for i in range(lines):
        loads[i].wait()
        part = slice(size * i, size * (i + 1))
        recip = partial[part, :] + half_field(ph, rhs, tiles, part)
        far = jnp.dot(recip.astype(BF16), w_out[...], preferred_element_type=F32)
        for j in range(each):
            x, y = divmod(each * i + j, cols)
            occ = lax.dot_general(pos[x, y], select, TN, preferred_element_type=F32)
            value = base[y, x] + far[rows * j : rows * (j + 1)]
            held[i, rows * j : rows * (j + 1), :] = jnp.where(occ > 0.0, value, 0.0).astype(BF16)
        store = pltpu.make_async_copy(held.at[i], out.at[pl.ds(size * i, size), :], out_sems.at[i])
        store.start()
        stores.append(store)
    for store in stores:
        store.wait()


def field_call(kernel, name, out_shape, extra, ph, weighted, *args, lines=4):
    steps, _, atoms, _ = ph.shape
    tiles, width, _ = weighted.shape
    whole = pl.BlockSpec(memory_space=VMEM)
    in_hbm = pl.BlockSpec(memory_space=pltpu.HBM)
    return pl.pallas_call(
        functools.partial(kernel, lines),
        in_specs=[in_hbm] + [whole] * (1 + len(args)),
        out_specs=in_hbm if extra else whole,
        out_shape=out_shape,
        scratch_shapes=[
            VMEM((steps // 2,) + ph.shape[1:], BF16),
            VMEM((tiles * KTILE, width), BF16),
            *([VMEM((lines, atoms // lines, width), BF16)] if extra else []),
            pltpu.SemaphoreType.DMA((lines,)),
            *([pltpu.SemaphoreType.DMA((lines,))] if extra else []),
        ],
        compiler_params=pltpu.CompilerParams(vmem_limit_bytes=16 << 20),
        cost_estimate=pl.CostEstimate(
            flops=4 * atoms * tiles * KTILE * width, bytes_accessed=4 << 20, transcendentals=0
        ),
        name=name,
    )(pltpu.with_memory_space_constraint(ph, pltpu.HBM), *pinned(weighted, *args))


def my_index():
    return lax.axis_index("gx") * lax.axis_size("gy") + lax.axis_index("gy")


def swap(value, mask):
    count = lax.axis_size("gx") * lax.axis_size("gy")
    return lax.ppermute(value, AXES, [(i, i ^ mask) for i in range(count)])


def tied(*values):
    return lax.optimization_barrier(values)


def no_work():
    return ()


class Exchange:
    def __init__(self):
        size_y = lax.axis_size("gy")
        count = lax.axis_size("gx") * size_y
        bits = [1 << i for i in range(count.bit_length() - 1)]
        low = [b for b in bits if b < size_y]
        self.halved = low[:2]
        self.direct = low[2:4]
        self.whole = low[4:] + [b for b in bits if b >= size_y]
        self.masks = [0]
        for b in self.direct:
            self.masks = self.masks + [m ^ b for m in self.masks]

    def place(self):
        return sum(((my_index() // b) % 2) << k for k, b in enumerate(self.direct))

    def halve(self, value, bit, work=no_work):
        half = value.shape[0] // 2
        mine = (my_index() // bit) % 2
        keep = lax.dynamic_slice_in_dim(value, mine * half, half, 0)
        give = lax.dynamic_slice_in_dim(value, (1 - mine) * half, half, 0).astype(BF16)
        (got,), done = run_under([give], [bit], work)
        return keep + got.astype(F32), done

    def spread_sum(self, value, work):
        count = len(self.masks)
        value = value.reshape((count, -1) + value.shape[1:])
        me = self.place()
        keep = lax.dynamic_index_in_dim(value, me, 0, False)
        gives = [
            lax.dynamic_index_in_dim(value, me ^ j, 0, False).astype(BF16) for j in range(1, count)
        ]
        gives, done = run_under(gives, self.masks[1:], work)
        for got in gives:
            keep = keep + got.astype(F32)
        return keep, done

    def whole_sum(self, value, bit, work=no_work):
        (got,), done = run_under([value.astype(BF16)], [bit], work)
        return value + got.astype(F32), done

    def spread(self, value, work):
        count = len(self.masks)
        got, done = run_under([value] * (count - 1), self.masks[1:], work)
        parts = jnp.stack([value] + got)
        me = self.place()
        for k in range(len(self.direct)):
            b = 1 << k
            cut = parts.reshape((count // (2 * b), 2, b) + value.shape)
            parts = jnp.where((me >> k) & 1 == 0, cut, cut[:, ::-1]).reshape(parts.shape)
        return parts.reshape((-1,) + value.shape[1:]), done

    def double(self, value, bit, work=no_work):
        mine = (my_index() // bit) % 2
        (other,), done = run_under([value], [bit], work)
        return (
            jnp.where(
                mine == 0, jnp.concatenate([value, other]), jnp.concatenate([other, value])
            ),
            done,
        )


def run_under(gives, masks, work):
    inputs = work.inputs if work is not no_work else ()
    gives, inputs = tied(list(gives), inputs)
    got = [swap(give, mask) for give, mask in zip(gives, masks)]
    done = work(*inputs) if work is not no_work else ()
    return tied(got, done)


class Work:
    def __init__(self, call, *inputs):
        self.call = call
        self.inputs = inputs

    def __call__(self, *inputs):
        return self.call(*inputs)


def from_before(cells, axis, dim):
    count = lax.axis_size(axis)
    size = cells.shape[dim]
    tail = lax.slice_in_dim(cells, size - 1, size, axis=dim)
    return lax.ppermute(tail, axis, [(i, (i + 1) % count) for i in range(count)])


def from_after(cells, axis, dim):
    count = lax.axis_size(axis)
    head = lax.slice_in_dim(cells, 0, 1, axis=dim)
    return lax.ppermute(head, axis, [((i + 1) % count, i) for i in range(count)])


def edge_rows(feat_planes, pos_planes, y):
    parts = []
    for f, q in zip(feat_planes, pos_planes):
        q = jnp.pad(q[:, y : y + 1], ((0, 0), (0, 0), (0, 0), (0, f.shape[3] - q.shape[3])))
        parts.append(jnp.concatenate([f[:, y : y + 1], q], axis=2))
    return jnp.concatenate(parts, axis=0)


def on_device(features, fractions, counts, k_index, w_short, w_charge, w_out):
    planes, cols, depth, slots, width = features.shape
    basis = w_short.shape[0]
    vectors = k_index.shape[0]
    rows = depth * slots
    atoms = planes * cols * rows
    size_x, size_y = lax.axis_size("gx"), lax.axis_size("gy")
    grid_all = (planes * size_x, cols * size_y, depth)
    assert rows == 128 and slots == 8 and planes == 2 and cols == 8 and width == KTILE
    assert vectors % KTILE == 0
    for extent in grid_all:
        assert extent & (extent - 1) == 0 and extent <= 256
    scale_all = math.sqrt(vectors / (grid_all[0] * grid_all[1] * grid_all[2] * slots))

    feat = features.reshape(planes, cols, rows, width)
    before = from_before(feat, "gx", 0)

    occupied = (jnp.arange(slots, dtype=jnp.int32) < counts[..., None]).astype(BF16)
    frac = jnp.transpose(fractions, (0, 1, 4, 2, 3)).reshape(planes, cols, 3, rows)
    pos = jnp.concatenate(
        [
            frac,
            occupied.reshape(planes, cols, 1, rows),
            jnp.zeros((planes, cols, POS_ROWS - 4, rows), BF16),
        ],
        axis=2,
    )
    ph, partial = factor_call(
        pos, k_index.T, feat.reshape(atoms, width), w_charge, grid_all, scale_all
    )
    partial, before, head, pos_late = tied(partial, before, feat[:1], pos)
    after = from_after(head, "gx", 0)
    pos_before = from_before(pos_late, "gx", 0)
    pos_after = from_after(pos_late, "gx", 0)

    w_flat = w_short.reshape(basis * width, width)
    exchange = Exchange()

    def plane_work(plane, first, count, base, *sides):
        kernel = functools.partial(plane_kernel, slots, basis, plane, first, count)
        call = lambda *args: short_call(
            kernel, "plane", count, basis, args[:5], args[5] if len(args) > 5 else None
        )
        inputs = (feat, pos, *sides, w_flat) + (() if base is None else (base,))
        return Work(call, *inputs)

    def edges(*args):
        feat, pos, before, pos_before, after, pos_after, low, high, w, base = args
        common = (feat, pos, before, pos_before, after, pos_after)
        for name, y, dy, halo in (("low", 0, -1, low), ("high", cols - 1, 1, high)):
            kernel = functools.partial(edge_kernel, slots, basis, y, dy)
            base = short_call(kernel, name, planes, basis, (*common, halo, w), base)
        return base

    value, _ = exchange.halve(partial, exchange.halved[0])
    value, before, pos_before = tied(value, before, pos_before)
    value, base = exchange.halve(
        value, exchange.halved[1], plane_work(0, 1, 3, None, before, pos_before)
    )
    value, base = exchange.spread_sum(value, plane_work(0, 4, 3, base, before, pos_before))
    value, base, after, pos_after = tied(value, base, after, pos_after)
    feat_planes = (before, feat, after)
    pos_planes = (pos_before, pos, pos_after)
    low = from_before(edge_rows(feat_planes, pos_planes, cols - 1), "gy", 1)
    high = from_after(edge_rows(feat_planes, pos_planes, 0), "gy", 1)
    for i, bit in enumerate(exchange.whole):
        if i == 0:
            value, base = exchange.whole_sum(
                value, bit, plane_work(1, 1, 3, base, after, pos_after)
            )
        else:
            value, _ = exchange.whole_sum(value, bit)
    value = value.astype(BF16)
    value, base = exchange.spread(value, plane_work(1, 4, 3, base, after, pos_after))
    value, base = exchange.double(
        value,
        exchange.halved[1],
        Work(edges, feat, pos, before, pos_before, after, pos_after, low, high, w_flat, base),
    )
    assert exchange.halved[0] == 1 and (vectors // KTILE) % 2 == 0
    half = (vectors // KTILE, width, KTILE)

    def near_field(ph, value):
        return field_call(
            near_field_kernel, "near", VMEM((atoms, width), F32), False, ph, value.reshape(half)
        )

    (other,), partial = run_under([value], [exchange.halved[0]], Work(near_field, ph, value))
    out = field_call(
        far_field_kernel,
        "far",
        jax.ShapeDtypeStruct((atoms, width), BF16),
        True,
        ph,
        other.reshape(half),
        partial,
        w_out,
        base,
        pos,
    )
    return out.reshape(features.shape)


def solution(mesh):
    return jax.shard_map(
        on_device,
        mesh=mesh,
        in_specs=(
            P("gx", "gy", None, None, None),
            P("gx", "gy", None, None, None),
            P("gx", "gy", None),
            P(),
            P(),
            P(),
            P(),
        ),
        out_specs=P("gx", "gy", None, None, None),
        check_vma=False,
    )
```

```python
import functools
import math

import jax
import jax.numpy as jnp
from jax import lax
from jax.experimental import pallas as pl
from jax.experimental.pallas import tpu as pltpu
from jax.sharding import PartitionSpec as P

TWO_PI = 2.0 * math.pi
SHARPNESS = 600.0
CENTER_LOW = 0.2
CENTER_SPAN = 0.5
SCREEN = 16.0
FAR = 8.0
BF16 = jnp.bfloat16
F32 = jnp.float32
AXES = ("gx", "gy")
KTILE = 256

HALF_COS = (
    1.4142134965644628,
    -6.978850988150233,
    5.739461168545313,
    -1.8835629713129327,
    0.3106981552009573,
)
HALF_SIN = (4.442867902918289, -7.307443416752583, 3.594788034903934, -0.7843739144750123)
NT = (((1,), (1,)), ((), ()))
TN = (((0,), (0,)), ((), ()))
TT = (((0,), (1,)), ((), ()))
OCC_ROW = 3
CELL_ROW = 4
POS_ROWS = 16
VMEM = pltpu.VMEM


def pinned(*values):
    return [pltpu.with_memory_space_constraint(value, VMEM) for value in values]


def horner(coefs, s):
    value = coefs[-1] * s + coefs[-2]
    for c in coefs[-3::-1]:
        value = value * s + c
    return value


def factor_kernel(grid_all, scale_all, pos, kidx, feat, wc, ph_out, fac, ph, charges, where_at, sems):
    planes, cols, _, rows = pos.shape
    copies = []
    steps = ph.shape[0]
    atoms, width = feat.shape

    sub = lax.broadcasted_iota(jnp.int32, (POS_ROWS, KTILE), 0)
    kmat, screened = [], []
    for step in range(steps):
        value = jnp.zeros((POS_ROWS, KTILE), F32)
        k_sq = jnp.zeros((1, KTILE), F32)
        for d in range(3):
            k = kidx[d : d + 1, step * KTILE : (step + 1) * KTILE].astype(F32) * (1.0 / grid_all[d])
            hit = (sub == d) | (sub == CELL_ROW + d)
            value = jnp.where(hit, jnp.broadcast_to(k, value.shape), value)
            k_sq = k_sq + (TWO_PI * k) * (TWO_PI * k)
        kmat.append(value.astype(BF16))
        screened.append(jnp.exp(-k_sq / (4.0 * SCREEN)) / k_sq)
    total = sum(jnp.sum(part, axis=1, keepdims=True) for part in screened)

    sub = lax.broadcasted_iota(jnp.int32, (POS_ROWS, rows), 0)
    depth = (lax.broadcasted_iota(jnp.int32, (POS_ROWS, rows), 1) // 8).astype(F32)
    x0 = (lax.axis_index("gx") * planes).astype(F32)
    y0 = (lax.axis_index("gy") * cols).astype(F32)
    for x in range(planes):
        for y in range(cols):
            j = (x * cols + y) * rows
            tile = pos[x, y].astype(F32)
            tile = jnp.where(sub == CELL_ROW, x0 + float(x), tile)
            tile = jnp.where(sub == CELL_ROW + 1, y0 + float(y), tile)
            tile = jnp.where(sub == CELL_ROW + 2, depth, tile)
            where_at[j : j + rows, :] = tile.T.astype(BF16)
    turned = wc[...].T

    size = 2 * rows
    for step in range(steps + 1):
        sums = [None, None]
        for j in range(0, atoms, size):
            if step < steps:
                t_all = jnp.dot(
                    where_at[j : j + size, :], kmat[step], preferred_element_type=F32
                )
                for i in range(0, size, 16):
                    t = t_all[i : i + 16]
                    r = t - jnp.round(t)
                    s = r * r
                    half_c = horner(HALF_COS, s)
                    half_s = horner(HALF_SIN, s) * r
                    ph[step, 0, j + i : j + i + 16, :] = (1.0 - half_s * half_s).astype(BF16)
                    ph[step, 1, j + i : j + i + 16, :] = (half_s * half_c).astype(BF16)
            if step == 0:
                c = lax.dot_general(turned, feat[j : j + size, :], NT, preferred_element_type=F32)
                line = j // rows
                occ = [
                    pos[n // cols, n % cols, OCC_ROW : OCC_ROW + 1, :].astype(F32)
                    for n in range(line, line + 2)
                ]
                charges[:, j : j + size] = (c * jnp.concatenate(occ, axis=1)).astype(BF16)
            if step > 0:
                for p in range(2):
                    part = jnp.dot(
                        charges[:, j : j + size],
                        ph[step - 1, p, j : j + size, :],
                        preferred_element_type=F32,
                    )
                    sums[p] = part if sums[p] is None else sums[p] + part
        if step < steps:
            copy = pltpu.make_async_copy(ph.at[step], ph_out.at[step], sems.at[step])
            copy.start()
            copies.append(copy)
        if step > 0:
            weight = screened[step - 1] / total * scale_all
            for p in range(2):
                row = (2 * (step - 1) + p) * width
                fac[row : row + width, :] = sums[p] * weight
    for copy in copies:
        copy.wait()


def factor_call(pos, kidx, feat, wc, grid_all, scale_all):
    atoms, width = feat.shape
    vectors = kidx.shape[1]
    steps = vectors // KTILE
    whole = pl.BlockSpec(memory_space=VMEM)
    return pl.pallas_call(
        functools.partial(factor_kernel, grid_all, scale_all),
        in_specs=[whole] * 4,
        out_specs=[pl.BlockSpec(memory_space=pltpu.HBM), whole],
        out_shape=[
            pltpu.HBM((steps, 2, atoms, KTILE), BF16),
            VMEM((steps * 2 * width, KTILE), F32),
        ],
        scratch_shapes=[
            VMEM((steps, 2, atoms, KTILE), BF16),
            VMEM((width, atoms), BF16),
            VMEM((atoms, POS_ROWS), BF16),
            pltpu.SemaphoreType.DMA((steps,)),
        ],
        compiler_params=pltpu.CompilerParams(vmem_limit_bytes=24 << 20),
        cost_estimate=pl.CostEstimate(
            flops=24 * atoms * vectors * width, bytes_accessed=4 << 20, transcendentals=0
        ),
        name="factor",
    )(*pinned(pos, kidx, feat, wc))


def aggregate_row(slots, basis, near_feat, near_pos, own_pos, write):
    rows = 128
    pairs = rows // (2 * slots)
    two = 2 * slots
    window = 4 * slots
    sub = lax.broadcasted_iota(jnp.int32, (8, 128), 0)
    lane = lax.broadcasted_iota(jnp.int32, (8, 128), 1)
    lane_block = lane // window
    cell_in_window = (lane % window) // slots
    z_off = jnp.where(sub == 2, (cell_in_window - 1).astype(F32), 0.0)
    columns = [(dx, dy) for dx in (-1, 0, 1) for dy in (-1, 0, 1) if (dx, dy) != (0, 0)]
    columns.append((0, 0))
    select = jnp.where(
        lax.broadcasted_iota(jnp.int32, (POS_ROWS, 384), 0)
        == lax.broadcasted_iota(jnp.int32, (POS_ROWS, 384), 1) // 128,
        1.0,
        0.0,
    ).astype(BF16)
    stretch = math.sqrt(SHARPNESS)
    centers = [stretch * (CENTER_LOW + b * (CENTER_SPAN / (basis - 1))) for b in range(basis)]

    placed = []
    for dx, dy in columns:
        coords = near_pos(dx, dy).astype(F32)[0:8]
        occ = jnp.broadcast_to(coords[OCC_ROW : OCC_ROW + 1, :], coords.shape)
        shift = jnp.where(sub == 0, float(dx), jnp.where(sub == 1, float(dy), 0.0))
        placed.append(jnp.where(occ > 0.0, coords + shift, FAR))
    own_all = lax.dot_general(own_pos, select, TN, preferred_element_type=F32)
    for p in range(pairs):
        packed = []
        for h in range(3):
            merged = None
            for c in range(4 * h, min(4 * h + 4, 9)):
                amount = (window * (c % 4) - two * p) % 128
                moved = pltpu.roll(placed[c], amount, axis=1) if amount else placed[c]
                merged = moved if merged is None else jnp.where(lane_block == c % 4, moved, merged)
            merged = merged + z_off
            if h == 2:
                merged = jnp.where(lane_block == 0, merged, FAR)
            packed.append([jnp.broadcast_to(merged[d : d + 1, :], (8, 128)) for d in range(3)])
        parts = [[None, None] for _ in range(3)]
        for h in range(3):
            for q in range(2):
                r0 = (two * p + slots * (1 + q)) % rows
                d2 = None
                for d in range(3):
                    mine = own_all[r0 : r0 + slots, 128 * d : 128 * d + 128]
                    if d == 2 and q == 1:
                        mine = mine + 1.0
                    delta = packed[h][d] - mine
                    d2 = delta * delta if d2 is None else d2 + delta * delta
                env = jnp.maximum(1.0 - d2, 0.0)
                env = env * env
                if h == 2:
                    env = jnp.where(lane == sub + slots * (1 + q), 0.0, env)
                ar = (d2 * stretch) * lax.rsqrt(jnp.maximum(d2, 1e-30))
                values = []
                for b in range(basis):
                    u = ar - centers[b]
                    values.append(jnp.exp(u * (centers[b] - ar)) * env)
                parts[h][q] = values
        lhs = []
        for h in range(3):
            lhs.append(
                jnp.concatenate(
                    [
                        jnp.concatenate([parts[h][0][b], parts[h][1][b]], axis=0).astype(BF16)
                        for b in range(basis)
                    ],
                    axis=0,
                )
            )
        near = []
        nxt = two * ((p + 1) % pairs)
        for dx, dy in columns:
            near.append(near_feat(dx, dy, two * p, two))
            near.append(near_feat(dx, dy, nxt, two))
        near.append(jnp.zeros((384 - 9 * window, near[0].shape[1]), BF16))
        total = jnp.dot(
            jnp.concatenate(lhs, axis=1),
            jnp.concatenate(near, axis=0),
            preferred_element_type=F32,
        ).astype(BF16)
        for b in range(basis):
            write(two * p, two, b, total[two * b : two * b + two])


def turn(value, slots):
    return jnp.concatenate([value[128 - slots :], value[: 128 - slots]], axis=0)


def plane_kernel(slots, basis, plane, first, count, feat, pos, side_feat, side_pos, w, *rest):
    out, agg = rest[-2:]
    planes, _, rows, width = feat.shape

    def pick(ref, side, dx):
        x = plane + dx
        return (ref, x) if 0 <= x < planes else (side, 0)

    def body(i, carry):
        y = first + i

        def near_feat(dx, dy, start, size):
            ref, x = pick(feat, side_feat, dx)
            return ref[x, y + dy, start : start + size, :]

        def near_pos(dx, dy):
            ref, x = pick(pos, side_pos, dx)
            return ref[x, y + dy]

        def write(start, size, b, value):
            agg[i, start : start + size, width * b : width * (b + 1)] = value

        aggregate_row(slots, basis, near_feat, near_pos, pos[plane, y], write)
        return carry

    lax.fori_loop(0, count, body, 0)
    value = jnp.dot(
        agg[...].reshape(count * rows, basis * width), w[...], preferred_element_type=F32
    )
    value = jax.nn.silu(value).reshape(count, rows, width)
    for i in range(count):
        out[first + i, plane] = feat[plane, first + i].astype(F32) + turn(value[i], slots)


def edge_kernel(
    slots, basis, y, halo_dy, feat, pos, before, pos_before, after, pos_after, halo, w, *rest
):
    out, agg = rest[-2:]
    planes, _, rows, width = feat.shape
    for plane in range(planes):

        def near_feat(dx, dy, start, size):
            x = plane + dx
            if dy == halo_dy:
                return halo[x + 1, 0, start : start + size, :]
            if 0 <= x < planes:
                return feat[x, y + dy, start : start + size, :]
            return (before if x < 0 else after)[0, y + dy, start : start + size, :]

        def near_pos(dx, dy):
            x = plane + dx
            if dy == halo_dy:
                return halo[x + 1, 0, rows : rows + POS_ROWS, 0:128]
            if 0 <= x < planes:
                return pos[x, y + dy]
            return (pos_before if x < 0 else pos_after)[0, y + dy]

        def write(start, size, b, value):
            agg[plane, start : start + size, width * b : width * (b + 1)] = value

        aggregate_row(slots, basis, near_feat, near_pos, pos[plane, y], write)
    value = jnp.dot(
        agg[...].reshape(planes * rows, basis * width), w[...], preferred_element_type=F32
    )
    value = jax.nn.silu(value).reshape(planes, rows, width)
    for plane in range(planes):
        out[y, plane] = feat[plane, y].astype(F32) + turn(value[plane], slots)


def short_call(kernel, name, lines, basis, args, base):
    planes, cols, rows, width = args[0].shape
    whole = pl.BlockSpec(memory_space=VMEM)
    aliases = {}
    if base is not None:
        aliases = {len(args): 0}
        args = (*args, base)
    return pl.pallas_call(
        kernel,
        in_specs=[whole] * len(args),
        out_specs=whole,
        out_shape=VMEM((cols, planes, rows, width), F32),
        scratch_shapes=[VMEM((lines, rows, basis * width), BF16)],
        input_output_aliases=aliases,
        compiler_params=pltpu.CompilerParams(vmem_limit_bytes=16 << 20),
        cost_estimate=pl.CostEstimate(
            flops=lines * rows * width * 8 * (basis * 384 + basis * width),
            bytes_accessed=4 << 20,
            transcendentals=lines * rows * 384 * (basis + 1),
        ),
        name=name,
    )(*pinned(*args))


def phase_loads(ph_all, ph, sems, half, lines):
    size = ph.shape[2] // lines
    loads = []
    for i in range(lines):
        part = pl.ds(size * i, size)
        load = pltpu.make_async_copy(
            ph_all.at[pl.ds(half * ph.shape[0], ph.shape[0]), :, part, :],
            ph.at[:, :, part, :],
            sems.at[i],
        )
        load.start()
        loads.append(load)
    return loads


def half_field(ph, rhs, tiles, part):
    lhs = jnp.concatenate([ph[t // 2, t % 2, part, :] for t in range(tiles)], axis=1)
    return jnp.dot(lhs, rhs[...], preferred_element_type=F32)


def near_field_kernel(lines, ph_all, weighted, out, ph, rhs, in_sems):
    tiles = weighted.shape[0]
    loads = phase_loads(ph_all, ph, in_sems, lax.rem(lax.axis_index("gy"), 2), lines)
    for t in range(tiles):
        rhs[t * KTILE : (t + 1) * KTILE, :] = weighted[t].T
    size = ph.shape[2] // lines
    for i in range(lines):
        loads[i].wait()
        part = slice(size * i, size * (i + 1))
        out[part, :] = half_field(ph, rhs, tiles, part)


def far_field_kernel(
    lines, ph_all, weighted, partial, w_out, base, pos, out, ph, rhs, held, in_sems, out_sems
):
    tiles, width, _ = weighted.shape
    cols, planes, rows, _ = base.shape
    loads = phase_loads(ph_all, ph, in_sems, 1 - lax.rem(lax.axis_index("gy"), 2), lines)
    for t in range(tiles):
        rhs[t * KTILE : (t + 1) * KTILE, :] = weighted[t].T
    sub = lax.broadcasted_iota(jnp.int32, (POS_ROWS, width), 0)
    select = jnp.where(sub == OCC_ROW, 1.0, 0.0).astype(BF16)
    size = ph.shape[2] // lines
    each = size // rows
    stores = []
    for i in range(lines):
        loads[i].wait()
        part = slice(size * i, size * (i + 1))
        recip = partial[part, :] + half_field(ph, rhs, tiles, part)
        far = jnp.dot(recip.astype(BF16), w_out[...], preferred_element_type=F32)
        for j in range(each):
            x, y = divmod(each * i + j, cols)
            occ = lax.dot_general(pos[x, y], select, TN, preferred_element_type=F32)
            value = base[y, x] + far[rows * j : rows * (j + 1)]
            held[i, rows * j : rows * (j + 1), :] = jnp.where(occ > 0.0, value, 0.0).astype(BF16)
        store = pltpu.make_async_copy(held.at[i], out.at[pl.ds(size * i, size), :], out_sems.at[i])
        store.start()
        stores.append(store)
    for store in stores:
        store.wait()


def field_call(kernel, name, out_shape, extra, ph, weighted, *args, lines=4):
    steps, _, atoms, _ = ph.shape
    tiles, width, _ = weighted.shape
    whole = pl.BlockSpec(memory_space=VMEM)
    in_hbm = pl.BlockSpec(memory_space=pltpu.HBM)
    return pl.pallas_call(
        functools.partial(kernel, lines),
        in_specs=[in_hbm] + [whole] * (1 + len(args)),
        out_specs=in_hbm if extra else whole,
        out_shape=out_shape,
        scratch_shapes=[
            VMEM((steps // 2,) + ph.shape[1:], BF16),
            VMEM((tiles * KTILE, width), BF16),
            *([VMEM((lines, atoms // lines, width), BF16)] if extra else []),
            pltpu.SemaphoreType.DMA((lines,)),
            *([pltpu.SemaphoreType.DMA((lines,))] if extra else []),
        ],
        compiler_params=pltpu.CompilerParams(vmem_limit_bytes=16 << 20),
        cost_estimate=pl.CostEstimate(
            flops=4 * atoms * tiles * KTILE * width, bytes_accessed=4 << 20, transcendentals=0
        ),
        name=name,
    )(pltpu.with_memory_space_constraint(ph, pltpu.HBM), *pinned(weighted, *args))


def my_index():
    return lax.axis_index("gx") * lax.axis_size("gy") + lax.axis_index("gy")


def swap(value, mask):
    count = lax.axis_size("gx") * lax.axis_size("gy")
    return lax.ppermute(value, AXES, [(i, i ^ mask) for i in range(count)])


def tied(*values):
    return lax.optimization_barrier(values)


def no_work():
    return ()


class Exchange:
    def __init__(self):
        size_y = lax.axis_size("gy")
        count = lax.axis_size("gx") * size_y
        bits = [1 << i for i in range(count.bit_length() - 1)]
        low = [b for b in bits if b < size_y]
        self.halved = low[:2]
        self.direct = low[2:4]
        self.whole = low[4:] + [b for b in bits if b >= size_y]
        self.masks = [0]
        for b in self.direct:
            self.masks = self.masks + [m ^ b for m in self.masks]

    def place(self):
        return sum(((my_index() // b) % 2) << k for k, b in enumerate(self.direct))

    def halve(self, value, bit, work=no_work):
        half = value.shape[0] // 2
        mine = (my_index() // bit) % 2
        keep = lax.dynamic_slice_in_dim(value, mine * half, half, 0)
        give = lax.dynamic_slice_in_dim(value, (1 - mine) * half, half, 0).astype(BF16)
        (got,), done = run_under([give], [bit], work)
        return keep + got.astype(F32), done

    def spread_sum(self, value, work):
        count = len(self.masks)
        value = value.reshape((count, -1) + value.shape[1:])
        me = self.place()
        keep = lax.dynamic_index_in_dim(value, me, 0, False)
        gives = [
            lax.dynamic_index_in_dim(value, me ^ j, 0, False).astype(BF16) for j in range(1, count)
        ]
        gives, done = run_under(gives, self.masks[1:], work)
        for got in gives:
            keep = keep + got.astype(F32)
        return keep, done

    def whole_sum(self, value, bit, work=no_work):
        (got,), done = run_under([value.astype(BF16)], [bit], work)
        return value + got.astype(F32), done

    def spread(self, value, work):
        count = len(self.masks)
        got, done = run_under([value] * (count - 1), self.masks[1:], work)
        parts = jnp.stack([value] + got)
        me = self.place()
        for k in range(len(self.direct)):
            b = 1 << k
            cut = parts.reshape((count // (2 * b), 2, b) + value.shape)
            parts = jnp.where((me >> k) & 1 == 0, cut, cut[:, ::-1]).reshape(parts.shape)
        return parts.reshape((-1,) + value.shape[1:]), done

    def double(self, value, bit, work=no_work):
        mine = (my_index() // bit) % 2
        (other,), done = run_under([value], [bit], work)
        return (
            jnp.where(
                mine == 0, jnp.concatenate([value, other]), jnp.concatenate([other, value])
            ),
            done,
        )


def run_under(gives, masks, work):
    inputs = work.inputs if work is not no_work else ()
    gives, inputs = tied(list(gives), inputs)
    got = [swap(give, mask) for give, mask in zip(gives, masks)]
    done = work(*inputs) if work is not no_work else ()
    return tied(got, done)


class Work:
    def __init__(self, call, *inputs):
        self.call = call
        self.inputs = inputs

    def __call__(self, *inputs):
        return self.call(*inputs)


def from_before(cells, axis, dim):
    count = lax.axis_size(axis)
    size = cells.shape[dim]
    tail = lax.slice_in_dim(cells, size - 1, size, axis=dim)
    return lax.ppermute(tail, axis, [(i, (i + 1) % count) for i in range(count)])


def from_after(cells, axis, dim):
    count = lax.axis_size(axis)
    head = lax.slice_in_dim(cells, 0, 1, axis=dim)
    return lax.ppermute(head, axis, [((i + 1) % count, i) for i in range(count)])


def edge_rows(feat_planes, pos_planes, y):
    parts = []
    for f, q in zip(feat_planes, pos_planes):
        q = jnp.pad(q[:, y : y + 1], ((0, 0), (0, 0), (0, 0), (0, f.shape[3] - q.shape[3])))
        parts.append(jnp.concatenate([f[:, y : y + 1], q], axis=2))
    return jnp.concatenate(parts, axis=0)


def on_device(features, fractions, counts, k_index, w_short, w_charge, w_out):
    planes, cols, depth, slots, width = features.shape
    basis = w_short.shape[0]
    vectors = k_index.shape[0]
    rows = depth * slots
    atoms = planes * cols * rows
    size_x, size_y = lax.axis_size("gx"), lax.axis_size("gy")
    grid_all = (planes * size_x, cols * size_y, depth)
    assert rows == 128 and slots == 8 and planes == 2 and cols == 8 and width == KTILE
    assert vectors % KTILE == 0
    for extent in grid_all:
        assert extent & (extent - 1) == 0 and extent <= 256
    scale_all = math.sqrt(vectors / (grid_all[0] * grid_all[1] * grid_all[2] * slots))

    feat = features.reshape(planes, cols, rows, width)
    before = from_before(feat, "gx", 0)

    occupied = (jnp.arange(slots, dtype=jnp.int32) < counts[..., None]).astype(BF16)
    frac = jnp.transpose(fractions, (0, 1, 4, 2, 3)).reshape(planes, cols, 3, rows)
    pos = jnp.concatenate(
        [
            frac,
            occupied.reshape(planes, cols, 1, rows),
            jnp.zeros((planes, cols, POS_ROWS - 4, rows), BF16),
        ],
        axis=2,
    )
    ph, partial = factor_call(
        pos, k_index.T, feat.reshape(atoms, width), w_charge, grid_all, scale_all
    )
    partial, head, pos_late = tied(partial, feat[:1], pos)
    after = from_after(head, "gx", 0)
    pos_before = from_before(pos_late, "gx", 0)
    pos_after = from_after(pos_late, "gx", 0)

    w_flat = w_short.reshape(basis * width, width)
    exchange = Exchange()

    def plane_work(plane, first, count, base, *sides):
        kernel = functools.partial(plane_kernel, slots, basis, plane, first, count)
        call = lambda *args: short_call(
            kernel, "plane", count, basis, args[:5], args[5] if len(args) > 5 else None
        )
        inputs = (feat, pos, *sides, w_flat) + (() if base is None else (base,))
        return Work(call, *inputs)

    def edges(*args):
        feat, pos, before, pos_before, after, pos_after, low, high, w, base = args
        common = (feat, pos, before, pos_before, after, pos_after)
        for name, y, dy, halo in (("low", 0, -1, low), ("high", cols - 1, 1, high)):
            kernel = functools.partial(edge_kernel, slots, basis, y, dy)
            base = short_call(kernel, name, planes, basis, (*common, halo, w), base)
        return base

    value, before = exchange.halve(
        partial, exchange.halved[0], Work(lambda plane: plane, before)
    )
    value, before, pos_before = tied(value, before, pos_before)
    value, base = exchange.halve(
        value, exchange.halved[1], plane_work(0, 1, 3, None, before, pos_before)
    )
    value, base = exchange.spread_sum(value, plane_work(0, 4, 3, base, before, pos_before))
    value, base, after, pos_after = tied(value, base, after, pos_after)
    feat_planes = (before, feat, after)
    pos_planes = (pos_before, pos, pos_after)
    low = from_before(edge_rows(feat_planes, pos_planes, cols - 1), "gy", 1)
    high = from_after(edge_rows(feat_planes, pos_planes, 0), "gy", 1)
    for i, bit in enumerate(exchange.whole):
        if i == 0:
            value, base = exchange.whole_sum(
                value, bit, plane_work(1, 1, 3, base, after, pos_after)
            )
        else:
            value, _ = exchange.whole_sum(value, bit)
    value = value.astype(BF16)
    value, base = exchange.spread(value, plane_work(1, 4, 3, base, after, pos_after))
    value, base = exchange.double(
        value,
        exchange.halved[1],
        Work(edges, feat, pos, before, pos_before, after, pos_after, low, high, w_flat, base),
    )
    assert exchange.halved[0] == 1 and (vectors // KTILE) % 2 == 0
    half = (vectors // KTILE, width, KTILE)

    def near_field(ph, value):
        return field_call(
            near_field_kernel, "near", VMEM((atoms, width), F32), False, ph, value.reshape(half)
        )

    (other,), partial = run_under([value], [exchange.halved[0]], Work(near_field, ph, value))
    out = field_call(
        far_field_kernel,
        "far",
        jax.ShapeDtypeStruct((atoms, width), BF16),
        True,
        ph,
        other.reshape(half),
        partial,
        w_out,
        base,
        pos,
    )
    return out.reshape(features.shape)


def solution(mesh):
    return jax.shard_map(
        on_device,
        mesh=mesh,
        in_specs=(
            P("gx", "gy", None, None, None),
            P("gx", "gy", None, None, None),
            P("gx", "gy", None),
            P(),
            P(),
            P(),
            P(),
        ),
        out_specs=P("gx", "gy", None, None, None),
        check_vma=False,
    )
```

```python
import functools
import math

import jax
import jax.numpy as jnp
from jax import lax
from jax.experimental import pallas as pl
from jax.experimental.pallas import tpu as pltpu
from jax.sharding import PartitionSpec as P

TWO_PI = 2.0 * math.pi
SHARPNESS = 600.0
CENTER_LOW = 0.2
CENTER_SPAN = 0.5
SCREEN = 16.0
FAR = 8.0
BF16 = jnp.bfloat16
F32 = jnp.float32
AXES = ("gx", "gy")
KTILE = 256

HALF_COS = (
    1.4142134965644628,
    -6.978850988150233,
    5.739461168545313,
    -1.8835629713129327,
    0.3106981552009573,
)
HALF_SIN = (4.442867902918289, -7.307443416752583, 3.594788034903934, -0.7843739144750123)
NT = (((1,), (1,)), ((), ()))
TN = (((0,), (0,)), ((), ()))
TT = (((0,), (1,)), ((), ()))
OCC_ROW = 3
CELL_ROW = 4
POS_ROWS = 16
VMEM = pltpu.VMEM


def pinned(*values):
    return [pltpu.with_memory_space_constraint(value, VMEM) for value in values]


def horner(coefs, s):
    value = coefs[-1] * s + coefs[-2]
    for c in coefs[-3::-1]:
        value = value * s + c
    return value


def factor_kernel(grid_all, scale_all, pos, kidx, feat, wc, ph_out, fac, ph, charges, where_at, sems):
    planes, cols, _, rows = pos.shape
    copies = []
    steps = ph.shape[0]
    atoms, width = feat.shape

    sub = lax.broadcasted_iota(jnp.int32, (POS_ROWS, KTILE), 0)
    kmat, screened = [], []
    for step in range(steps):
        value = jnp.zeros((POS_ROWS, KTILE), F32)
        k_sq = jnp.zeros((1, KTILE), F32)
        for d in range(3):
            k = kidx[d : d + 1, step * KTILE : (step + 1) * KTILE].astype(F32) * (1.0 / grid_all[d])
            hit = (sub == d) | (sub == CELL_ROW + d)
            value = jnp.where(hit, jnp.broadcast_to(k, value.shape), value)
            k_sq = k_sq + (TWO_PI * k) * (TWO_PI * k)
        kmat.append(value.astype(BF16))
        screened.append(jnp.exp(-k_sq / (4.0 * SCREEN)) / k_sq)
    total = sum(jnp.sum(part, axis=1, keepdims=True) for part in screened)

    sub = lax.broadcasted_iota(jnp.int32, (POS_ROWS, rows), 0)
    depth = (lax.broadcasted_iota(jnp.int32, (POS_ROWS, rows), 1) // 8).astype(F32)
    x0 = (lax.axis_index("gx") * planes).astype(F32)
    y0 = (lax.axis_index("gy") * cols).astype(F32)
    for x in range(planes):
        for y in range(cols):
            j = (x * cols + y) * rows
            tile = pos[x, y].astype(F32)
            tile = jnp.where(sub == CELL_ROW, x0 + float(x), tile)
            tile = jnp.where(sub == CELL_ROW + 1, y0 + float(y), tile)
            tile = jnp.where(sub == CELL_ROW + 2, depth, tile)
            where_at[j : j + rows, :] = tile.T.astype(BF16)
    turned = wc[...].T

    size = 2 * rows
    for step in range(steps + 1):
        sums = [None, None]
        for j in range(0, atoms, size):
            if step < steps:
                t_all = jnp.dot(
                    where_at[j : j + size, :], kmat[step], preferred_element_type=F32
                )
                for i in range(0, size, 16):
                    t = t_all[i : i + 16]
                    r = t - jnp.round(t)
                    s = r * r
                    half_c = horner(HALF_COS, s)
                    half_s = horner(HALF_SIN, s) * r
                    ph[step, 0, j + i : j + i + 16, :] = (1.0 - half_s * half_s).astype(BF16)
                    ph[step, 1, j + i : j + i + 16, :] = (half_s * half_c).astype(BF16)
            if step == 0:
                c = lax.dot_general(turned, feat[j : j + size, :], NT, preferred_element_type=F32)
                line = j // rows
                occ = [
                    pos[n // cols, n % cols, OCC_ROW : OCC_ROW + 1, :].astype(F32)
                    for n in range(line, line + 2)
                ]
                charges[:, j : j + size] = (c * jnp.concatenate(occ, axis=1)).astype(BF16)
            if step > 0:
                for p in range(2):
                    part = jnp.dot(
                        charges[:, j : j + size],
                        ph[step - 1, p, j : j + size, :],
                        preferred_element_type=F32,
                    )
                    sums[p] = part if sums[p] is None else sums[p] + part
        if step < steps:
            copy = pltpu.make_async_copy(ph.at[step], ph_out.at[step], sems.at[step])
            copy.start()
            copies.append(copy)
        if step > 0:
            weight = screened[step - 1] / total * scale_all
            for p in range(2):
                row = (2 * (step - 1) + p) * width
                fac[row : row + width, :] = sums[p] * weight
    for copy in copies:
        copy.wait()


def factor_call(pos, kidx, feat, wc, grid_all, scale_all):
    atoms, width = feat.shape
    vectors = kidx.shape[1]
    steps = vectors // KTILE
    whole = pl.BlockSpec(memory_space=VMEM)
    return pl.pallas_call(
        functools.partial(factor_kernel, grid_all, scale_all),
        in_specs=[whole] * 4,
        out_specs=[pl.BlockSpec(memory_space=pltpu.HBM), whole],
        out_shape=[
            pltpu.HBM((steps, 2, atoms, KTILE), BF16),
            VMEM((steps * 2 * width, KTILE), F32),
        ],
        scratch_shapes=[
            VMEM((steps, 2, atoms, KTILE), BF16),
            VMEM((width, atoms), BF16),
            VMEM((atoms, POS_ROWS), BF16),
            pltpu.SemaphoreType.DMA((steps,)),
        ],
        compiler_params=pltpu.CompilerParams(vmem_limit_bytes=24 << 20),
        cost_estimate=pl.CostEstimate(
            flops=24 * atoms * vectors * width, bytes_accessed=4 << 20, transcendentals=0
        ),
        name="factor",
    )(*pinned(pos, kidx, feat, wc))


def aggregate_row(slots, basis, near_feat, near_pos, own_pos, write):
    rows = 128
    pairs = rows // (2 * slots)
    two = 2 * slots
    window = 4 * slots
    sub = lax.broadcasted_iota(jnp.int32, (8, 128), 0)
    lane = lax.broadcasted_iota(jnp.int32, (8, 128), 1)
    lane_block = lane // window
    cell_in_window = (lane % window) // slots
    z_off = jnp.where(sub == 2, (cell_in_window - 1).astype(F32), 0.0)
    columns = [(dx, dy) for dx in (-1, 0, 1) for dy in (-1, 0, 1) if (dx, dy) != (0, 0)]
    columns.append((0, 0))
    select = jnp.where(
        lax.broadcasted_iota(jnp.int32, (POS_ROWS, 384), 0)
        == lax.broadcasted_iota(jnp.int32, (POS_ROWS, 384), 1) // 128,
        1.0,
        0.0,
    ).astype(BF16)
    stretch = math.sqrt(SHARPNESS)
    centers = [stretch * (CENTER_LOW + b * (CENTER_SPAN / (basis - 1))) for b in range(basis)]

    placed = []
    for dx, dy in columns:
        coords = near_pos(dx, dy).astype(F32)[0:8]
        occ = jnp.broadcast_to(coords[OCC_ROW : OCC_ROW + 1, :], coords.shape)
        shift = jnp.where(sub == 0, float(dx), jnp.where(sub == 1, float(dy), 0.0))
        placed.append(jnp.where(occ > 0.0, coords + shift, FAR))
    own_all = lax.dot_general(own_pos, select, TN, preferred_element_type=F32)
    for p in range(pairs):
        packed = []
        for h in range(3):
            merged = None
            for c in range(4 * h, min(4 * h + 4, 9)):
                amount = (window * (c % 4) - two * p) % 128
                moved = pltpu.roll(placed[c], amount, axis=1) if amount else placed[c]
                merged = moved if merged is None else jnp.where(lane_block == c % 4, moved, merged)
            merged = merged + z_off
            if h == 2:
                merged = jnp.where(lane_block == 0, merged, FAR)
            packed.append([jnp.broadcast_to(merged[d : d + 1, :], (8, 128)) for d in range(3)])
        parts = [[None, None] for _ in range(3)]
        for h in range(3):
            for q in range(2):
                r0 = (two * p + slots * (1 + q)) % rows
                d2 = None
                for d in range(3):
                    mine = own_all[r0 : r0 + slots, 128 * d : 128 * d + 128]
                    if d == 2 and q == 1:
                        mine = mine + 1.0
                    delta = packed[h][d] - mine
                    d2 = delta * delta if d2 is None else d2 + delta * delta
                env = jnp.maximum(1.0 - d2, 0.0)
                env = env * env
                if h == 2:
                    env = jnp.where(lane == sub + slots * (1 + q), 0.0, env)
                ar = (d2 * stretch) * lax.rsqrt(jnp.maximum(d2, 1e-30))
                values = []
                for b in range(basis):
                    u = ar - centers[b]
                    values.append(jnp.exp(u * (centers[b] - ar)) * env)
                parts[h][q] = values
        lhs = []
        for h in range(3):
            lhs.append(
                jnp.concatenate(
                    [
                        jnp.concatenate([parts[h][0][b], parts[h][1][b]], axis=0).astype(BF16)
                        for b in range(basis)
                    ],
                    axis=0,
                )
            )
        near = []
        nxt = two * ((p + 1) % pairs)
        for dx, dy in columns:
            near.append(near_feat(dx, dy, two * p, two))
            near.append(near_feat(dx, dy, nxt, two))
        near.append(jnp.zeros((384 - 9 * window, near[0].shape[1]), BF16))
        total = jnp.dot(
            jnp.concatenate(lhs, axis=1),
            jnp.concatenate(near, axis=0),
            preferred_element_type=F32,
        ).astype(BF16)
        for b in range(basis):
            write(two * p, two, b, total[two * b : two * b + two])


def turn(value, slots):
    return jnp.concatenate([value[128 - slots :], value[: 128 - slots]], axis=0)


def plane_kernel(slots, basis, plane, first, count, feat, pos, side_feat, side_pos, w, *rest):
    out, agg = rest[-2:]
    planes, _, rows, width = feat.shape

    def pick(ref, side, dx):
        x = plane + dx
        return (ref, x) if 0 <= x < planes else (side, 0)

    def body(i, carry):
        y = first + i

        def near_feat(dx, dy, start, size):
            ref, x = pick(feat, side_feat, dx)
            return ref[x, y + dy, start : start + size, :]

        def near_pos(dx, dy):
            ref, x = pick(pos, side_pos, dx)
            return ref[x, y + dy]

        def write(start, size, b, value):
            agg[i, start : start + size, width * b : width * (b + 1)] = value

        aggregate_row(slots, basis, near_feat, near_pos, pos[plane, y], write)
        return carry

    lax.fori_loop(0, count, body, 0)
    value = jnp.dot(
        agg[...].reshape(count * rows, basis * width), w[...], preferred_element_type=F32
    )
    value = jax.nn.silu(value).reshape(count, rows, width)
    for i in range(count):
        out[first + i, plane] = feat[plane, first + i].astype(F32) + turn(value[i], slots)


def edge_kernel(
    slots, basis, y, halo_dy, feat, pos, before, pos_before, after, pos_after, halo, w, *rest
):
    out, agg = rest[-2:]
    planes, _, rows, width = feat.shape
    for plane in range(planes):

        def near_feat(dx, dy, start, size):
            x = plane + dx
            if dy == halo_dy:
                return halo[x + 1, 0, start : start + size, :]
            if 0 <= x < planes:
                return feat[x, y + dy, start : start + size, :]
            return (before if x < 0 else after)[0, y + dy, start : start + size, :]

        def near_pos(dx, dy):
            x = plane + dx
            if dy == halo_dy:
                return halo[x + 1, 0, rows : rows + POS_ROWS, 0:128]
            if 0 <= x < planes:
                return pos[x, y + dy]
            return (pos_before if x < 0 else pos_after)[0, y + dy]

        def write(start, size, b, value):
            agg[plane, start : start + size, width * b : width * (b + 1)] = value

        aggregate_row(slots, basis, near_feat, near_pos, pos[plane, y], write)
    value = jnp.dot(
        agg[...].reshape(planes * rows, basis * width), w[...], preferred_element_type=F32
    )
    value = jax.nn.silu(value).reshape(planes, rows, width)
    for plane in range(planes):
        out[y, plane] = feat[plane, y].astype(F32) + turn(value[plane], slots)


def short_call(kernel, name, lines, basis, args, base):
    planes, cols, rows, width = args[0].shape
    whole = pl.BlockSpec(memory_space=VMEM)
    aliases = {}
    if base is not None:
        aliases = {len(args): 0}
        args = (*args, base)
    return pl.pallas_call(
        kernel,
        in_specs=[whole] * len(args),
        out_specs=whole,
        out_shape=VMEM((cols, planes, rows, width), F32),
        scratch_shapes=[VMEM((lines, rows, basis * width), BF16)],
        input_output_aliases=aliases,
        compiler_params=pltpu.CompilerParams(vmem_limit_bytes=16 << 20),
        cost_estimate=pl.CostEstimate(
            flops=lines * rows * width * 8 * (basis * 384 + basis * width),
            bytes_accessed=4 << 20,
            transcendentals=lines * rows * 384 * (basis + 1),
        ),
        name=name,
    )(*pinned(*args))


def phase_loads(ph_all, ph, sems, half, lines):
    size = ph.shape[2] // lines
    loads = []
    for i in range(lines):
        part = pl.ds(size * i, size)
        load = pltpu.make_async_copy(
            ph_all.at[pl.ds(half * ph.shape[0], ph.shape[0]), :, part, :],
            ph.at[:, :, part, :],
            sems.at[i],
        )
        load.start()
        loads.append(load)
    return loads


def half_field(ph, rhs, tiles, part):
    lhs = jnp.concatenate([ph[t // 2, t % 2, part, :] for t in range(tiles)], axis=1)
    return jnp.dot(lhs, rhs[...], preferred_element_type=F32)


def near_field_kernel(lines, ph_all, weighted, out, ph, rhs, in_sems):
    tiles = weighted.shape[0]
    loads = phase_loads(ph_all, ph, in_sems, lax.rem(lax.axis_index("gy"), 2), lines)
    for t in range(tiles):
        rhs[t * KTILE : (t + 1) * KTILE, :] = weighted[t].T
    size = ph.shape[2] // lines
    for i in range(lines):
        loads[i].wait()
        part = slice(size * i, size * (i + 1))
        out[part, :] = half_field(ph, rhs, tiles, part)


def far_field_kernel(
    lines, ph_all, weighted, partial, w_out, base, pos, out, ph, rhs, held, in_sems, out_sems
):
    tiles, width, _ = weighted.shape
    cols, planes, rows, _ = base.shape
    loads = phase_loads(ph_all, ph, in_sems, 1 - lax.rem(lax.axis_index("gy"), 2), lines)
    for t in range(tiles):
        rhs[t * KTILE : (t + 1) * KTILE, :] = weighted[t].T
    sub = lax.broadcasted_iota(jnp.int32, (POS_ROWS, width), 0)
    select = jnp.where(sub == OCC_ROW, 1.0, 0.0).astype(BF16)
    size = ph.shape[2] // lines
    each = size // rows
    stores = []
    for i in range(lines):
        loads[i].wait()
        part = slice(size * i, size * (i + 1))
        recip = partial[part, :] + half_field(ph, rhs, tiles, part)
        far = jnp.dot(recip.astype(BF16), w_out[...], preferred_element_type=F32)
        for j in range(each):
            x, y = divmod(each * i + j, cols)
            occ = lax.dot_general(pos[x, y], select, TN, preferred_element_type=F32)
            value = base[y, x] + far[rows * j : rows * (j + 1)]
            held[i, rows * j : rows * (j + 1), :] = jnp.where(occ > 0.0, value, 0.0).astype(BF16)
        store = pltpu.make_async_copy(held.at[i], out.at[pl.ds(size * i, size), :], out_sems.at[i])
        store.start()
        stores.append(store)
    for store in stores:
        store.wait()


def field_call(kernel, name, out_shape, extra, ph, weighted, *args, lines=4):
    steps, _, atoms, _ = ph.shape
    tiles, width, _ = weighted.shape
    whole = pl.BlockSpec(memory_space=VMEM)
    in_hbm = pl.BlockSpec(memory_space=pltpu.HBM)
    return pl.pallas_call(
        functools.partial(kernel, lines),
        in_specs=[in_hbm] + [whole] * (1 + len(args)),
        out_specs=in_hbm if extra else whole,
        out_shape=out_shape,
        scratch_shapes=[
            VMEM((steps // 2,) + ph.shape[1:], BF16),
            VMEM((tiles * KTILE, width), BF16),
            *([VMEM((lines, atoms // lines, width), BF16)] if extra else []),
            pltpu.SemaphoreType.DMA((lines,)),
            *([pltpu.SemaphoreType.DMA((lines,))] if extra else []),
        ],
        compiler_params=pltpu.CompilerParams(vmem_limit_bytes=16 << 20),
        cost_estimate=pl.CostEstimate(
            flops=4 * atoms * tiles * KTILE * width, bytes_accessed=4 << 20, transcendentals=0
        ),
        name=name,
    )(pltpu.with_memory_space_constraint(ph, pltpu.HBM), *pinned(weighted, *args))


def my_index():
    return lax.axis_index("gx") * lax.axis_size("gy") + lax.axis_index("gy")


def swap(value, mask):
    count = lax.axis_size("gx") * lax.axis_size("gy")
    return lax.ppermute(value, AXES, [(i, i ^ mask) for i in range(count)])


def tied(*values):
    return lax.optimization_barrier(values)


def no_work():
    return ()


class Exchange:
    def __init__(self):
        size_y = lax.axis_size("gy")
        count = lax.axis_size("gx") * size_y
        bits = [1 << i for i in range(count.bit_length() - 1)]
        low = [b for b in bits if b < size_y]
        self.halved = low[:2]
        self.direct = low[2:4]
        self.whole = low[4:] + [b for b in bits if b >= size_y]
        self.masks = [0]
        for b in self.direct:
            self.masks = self.masks + [m ^ b for m in self.masks]

    def place(self):
        return sum(((my_index() // b) % 2) << k for k, b in enumerate(self.direct))

    def halve(self, value, bit, work=no_work):
        half = value.shape[0] // 2
        mine = (my_index() // bit) % 2
        keep = lax.dynamic_slice_in_dim(value, mine * half, half, 0)
        give = lax.dynamic_slice_in_dim(value, (1 - mine) * half, half, 0).astype(BF16)
        (got,), done = run_under([give], [bit], work)
        return keep + got.astype(F32), done

    def spread_sum(self, value, work):
        count = len(self.masks)
        value = value.reshape((count, -1) + value.shape[1:])
        me = self.place()
        keep = lax.dynamic_index_in_dim(value, me, 0, False)
        gives = [
            lax.dynamic_index_in_dim(value, me ^ j, 0, False).astype(BF16) for j in range(1, count)
        ]
        gives, done = run_under(gives, self.masks[1:], work)
        for got in gives:
            keep = keep + got.astype(F32)
        return keep, done

    def whole_sum(self, value, bit, work=no_work):
        (got,), done = run_under([value.astype(BF16)], [bit], work)
        return value + got.astype(F32), done

    def spread(self, value, work):
        count = len(self.masks)
        got, done = run_under([value] * (count - 1), self.masks[1:], work)
        parts = jnp.stack([value] + got)
        me = self.place()
        for k in range(len(self.direct)):
            b = 1 << k
            cut = parts.reshape((count // (2 * b), 2, b) + value.shape)
            parts = jnp.where((me >> k) & 1 == 0, cut, cut[:, ::-1]).reshape(parts.shape)
        return parts.reshape((-1,) + value.shape[1:]), done

    def double(self, value, bit, work=no_work):
        mine = (my_index() // bit) % 2
        (other,), done = run_under([value], [bit], work)
        return (
            jnp.where(
                mine == 0, jnp.concatenate([value, other]), jnp.concatenate([other, value])
            ),
            done,
        )


def run_under(gives, masks, work):
    inputs = work.inputs if work is not no_work else ()
    gives, inputs = tied(list(gives), inputs)
    got = [swap(give, mask) for give, mask in zip(gives, masks)]
    done = work(*inputs) if work is not no_work else ()
    return tied(got, done)


class Work:
    def __init__(self, call, *inputs):
        self.call = call
        self.inputs = inputs

    def __call__(self, *inputs):
        return self.call(*inputs)


def from_before(cells, axis, dim):
    count = lax.axis_size(axis)
    size = cells.shape[dim]
    tail = lax.slice_in_dim(cells, size - 1, size, axis=dim)
    return lax.ppermute(tail, axis, [(i, (i + 1) % count) for i in range(count)])


def from_after(cells, axis, dim):
    count = lax.axis_size(axis)
    head = lax.slice_in_dim(cells, 0, 1, axis=dim)
    return lax.ppermute(head, axis, [((i + 1) % count, i) for i in range(count)])


def edge_rows(feat_planes, pos_planes, y):
    parts = []
    for f, q in zip(feat_planes, pos_planes):
        q = jnp.pad(q[:, y : y + 1], ((0, 0), (0, 0), (0, 0), (0, f.shape[3] - q.shape[3])))
        parts.append(jnp.concatenate([f[:, y : y + 1], q], axis=2))
    return jnp.concatenate(parts, axis=0)


def on_device(features, fractions, counts, k_index, w_short, w_charge, w_out):
    planes, cols, depth, slots, width = features.shape
    basis = w_short.shape[0]
    vectors = k_index.shape[0]
    rows = depth * slots
    atoms = planes * cols * rows
    size_x, size_y = lax.axis_size("gx"), lax.axis_size("gy")
    grid_all = (planes * size_x, cols * size_y, depth)
    assert rows == 128 and slots == 8 and planes == 2 and cols == 8 and width == KTILE
    assert vectors % KTILE == 0
    for extent in grid_all:
        assert extent & (extent - 1) == 0 and extent <= 256
    scale_all = math.sqrt(vectors / (grid_all[0] * grid_all[1] * grid_all[2] * slots))

    feat = features.reshape(planes, cols, rows, width)
    before = from_before(feat, "gx", 0)

    occupied = (jnp.arange(slots, dtype=jnp.int32) < counts[..., None]).astype(BF16)
    frac = jnp.transpose(fractions, (0, 1, 4, 2, 3)).reshape(planes, cols, 3, rows)
    pos = jnp.concatenate(
        [
            frac,
            occupied.reshape(planes, cols, 1, rows),
            jnp.zeros((planes, cols, POS_ROWS - 4, rows), BF16),
        ],
        axis=2,
    )
    ph, partial = factor_call(
        pos, k_index.T, feat.reshape(atoms, width), w_charge, grid_all, scale_all
    )
    partial, pos_late = tied(partial, pos)
    pos_before = from_before(pos_late, "gx", 0)
    pos_after = from_after(pos_late, "gx", 0)

    w_flat = w_short.reshape(basis * width, width)
    exchange = Exchange()

    def plane_work(plane, first, count, base, *sides):
        kernel = functools.partial(plane_kernel, slots, basis, plane, first, count)
        call = lambda *args: short_call(
            kernel, "plane", count, basis, args[:5], args[5] if len(args) > 5 else None
        )
        inputs = (feat, pos, *sides, w_flat) + (() if base is None else (base,))
        return Work(call, *inputs)

    def edges(*args):
        feat, pos, before, pos_before, after, pos_after, low, high, w, base = args
        common = (feat, pos, before, pos_before, after, pos_after)
        for name, y, dy, halo in (("low", 0, -1, low), ("high", cols - 1, 1, high)):
            kernel = functools.partial(edge_kernel, slots, basis, y, dy)
            base = short_call(kernel, name, planes, basis, (*common, halo, w), base)
        return base

    value, before = exchange.halve(
        partial, exchange.halved[0], Work(lambda plane: plane, before)
    )
    value, before, pos_before, head = tied(value, before, pos_before, feat[:1])
    after = from_after(head, "gx", 0)
    value, base = exchange.halve(
        value, exchange.halved[1], plane_work(0, 1, 3, None, before, pos_before)
    )
    value, base = exchange.spread_sum(value, plane_work(0, 4, 3, base, before, pos_before))
    value, base, after, pos_after = tied(value, base, after, pos_after)
    feat_planes = (before, feat, after)
    pos_planes = (pos_before, pos, pos_after)
    low = from_before(edge_rows(feat_planes, pos_planes, cols - 1), "gy", 1)
    high = from_after(edge_rows(feat_planes, pos_planes, 0), "gy", 1)
    for i, bit in enumerate(exchange.whole):
        if i == 0:
            value, base = exchange.whole_sum(
                value, bit, plane_work(1, 1, 3, base, after, pos_after)
            )
        else:
            value, _ = exchange.whole_sum(value, bit)
    value = value.astype(BF16)
    value, base = exchange.spread(value, plane_work(1, 4, 3, base, after, pos_after))
    value, base = exchange.double(
        value,
        exchange.halved[1],
        Work(edges, feat, pos, before, pos_before, after, pos_after, low, high, w_flat, base),
    )
    assert exchange.halved[0] == 1 and (vectors // KTILE) % 2 == 0
    half = (vectors // KTILE, width, KTILE)

    def near_field(ph, value):
        return field_call(
            near_field_kernel, "near", VMEM((atoms, width), F32), False, ph, value.reshape(half)
        )

    (other,), partial = run_under([value], [exchange.halved[0]], Work(near_field, ph, value))
    out = field_call(
        far_field_kernel,
        "far",
        jax.ShapeDtypeStruct((atoms, width), BF16),
        True,
        ph,
        other.reshape(half),
        partial,
        w_out,
        base,
        pos,
    )
    return out.reshape(features.shape)


def solution(mesh):
    return jax.shard_map(
        on_device,
        mesh=mesh,
        in_specs=(
            P("gx", "gy", None, None, None),
            P("gx", "gy", None, None, None),
            P("gx", "gy", None),
            P(),
            P(),
            P(),
            P(),
        ),
        out_specs=P("gx", "gy", None, None, None),
        check_vma=False,
    )
```
